256 devices in a mesh: dp: 2 (over z_hi), tensor: 4 (over y), pool: 32 (over x, z_lo, core).
Axes of the slice: x: 4, y: 4, z: 8 (z_hi: 2, z_lo: 4; z = z_hi * 4 + z_lo), core: 2. Of those that a mesh axis runs over, the one named last changes fastest.
Arguments:
- tokens: bfloat16 [64, 1024, 4096], P(('dp', 'pool')), may hold values from -192 to 192, as said below
- w_hidden: bfloat16 [4096, 4096], P('pool', 'tensor'), may hold values from -0.09375 to 0.09375
- w_out: bfloat16 [4096, 256], P('tensor'), may hold values from -0.09375 to 0.09375
- bank: bfloat16 [32768, 256], P('pool'), may hold values from -0.5 to 0.5
- item_ids: int32 [32768], P('pool'), may hold values from 0 to 1048575
- log_freq: bfloat16 [1048576], replicated, may hold values from -14 to -6
- positives: int32 [64, 1024], P(('dp', 'pool'), 'tensor'), may hold values from 0 to 32767
- new_items: bfloat16 [8192, 256], P('pool'), may hold values from -0.5 to 0.5
- new_owner: int32 [8192, 1], P('pool'), may hold values from 0 to 31; in each aligned block of 256 rows (0 to 255, 256 to 511, ...) at most 16 rows name the same one
- queue_head: int32 [32], P('pool'), may hold values from 0 to 1023
Outputs:
- query_loss: float32 [64, 1024], P(('dp', 'pool'), 'tensor')
- new_bank: bfloat16 [32768, 256], P('pool')
The draws below stay inside these ranges and needn't reach their ends.
Inputs may be any that keep to these rules, and one draw needn't show every extreme that they name: `tokens`: float values within the range. `new_owner`: among the 256 new rows of one pool index, no shard is named by more than 16 rows, a bound that some block reaches.
All inputs are finite; a program needn't handle non-finite values.
Results may differ from the reference program's by a relative error of at most 0.002.
Values may be sent and summed in bfloat16 or wider, within the bound.
A program may use at most 128 MiB of HBM per device.

```python
import math
import jax
import jax.numpy as jnp
import numpy as np
from jax import lax

D = 4096
HID = 4096
E = 256
ITEMS = 1048576
TOK_DEV = 1024
BANK_DEV = 1024
NEW_DEV = 256
GROUPS = 64
BANK = 32768
NEW = 8192
CAP = 16
N_POOL = 32


def draw_tokens(key, part):
    dims_shape = (GROUPS, TOK_DEV, D)
    values = jax.random.truncated_normal(key, -6.0, 6.0, dims_shape, jnp.float32)
    return values.astype(jnp.bfloat16)


def plant(array, rng, low, largest):
    shape = array.shape
    place = [jax.random.randint(jax.random.fold_in(rng, axis), (), 0, shape[axis]) for axis in range(len(shape))]
    array = array.at[tuple(place)].set(low)
    longest = shape.index(max(shape))
    place[longest] = (place[longest] + 1) % shape[longest]
    return array.at[tuple(place)].set(largest)


def block_scale(own_key, shape, split, smallest, top_value):
    gain = 1.0
    for position, blocks in split:
        steps = jax.random.uniform(jax.random.fold_in(jax.random.fold_in(own_key, 6), position), (blocks,), jnp.float32, smallest / len(split), top_value / len(split))
        gain = gain * jnp.repeat(jnp.exp(steps), shape[position] // blocks).reshape((-1,) + (1,) * (len(shape) - 1 - position))
    return gain


def ranked_wide(own_key, shape, amount, skew):
    portions = [min(1 << octave, amount + 1 - (1 << octave)) * (1 << 20) // math.isqrt((1 << octave) ** skew) + 1 for octave in range((amount + 1).bit_length()) if 1 << octave <= amount]
    spread = 1 + sum(portions) // (1 << 30)
    grid = np.cumsum(np.array([max(1, weight // spread) for weight in portions]))
    ticket = jax.random.randint(jax.random.fold_in(own_key, 1), shape, 0, int(grid[len(portions) - 1]))
    start = jnp.left_shift(1, jnp.searchsorted(jnp.asarray(grid, jnp.int32), ticket, side="right").astype(jnp.int32))
    rank = start - 1 + jax.random.randint(jax.random.fold_in(own_key, 4), shape, 0, 1 << 30) % jnp.minimum(start, amount + 1 - start)
    return jax.random.permutation(jax.random.fold_in(own_key, 2), amount)[rank].astype(jnp.int32)


def deal_out(key, own, number, rows, number_of, top, reach, slope):
    sequence = jax.random.permutation(key, number_of)
    heavy_load, ordinary = shares(number_of, rows * top, reach, slope, True), shares(number_of, rows * top, reach, slope, False)
    places = jnp.arange(number_of)

    def named(tallies, turn):
        used = int((tallies > 0).sum())
        fixed = max(1, used // 4)
        shifted = fixed + (places - fixed + turn * (used - fixed)) % max(1, number_of - fixed)
        return jnp.zeros((number_of,), jnp.int32).at[sequence[jnp.where(places < fixed, places, shifted)]].set(jnp.asarray(tallies, jnp.int32))

    tallies = jnp.where(number % 4 == 0, named(heavy_load, number // 4), named(ordinary, number - number // 4 - 1))
    mixed = jax.random.permutation(jax.random.fold_in(own, 3), number_of)
    source_of, receiver = mixed[0:number_of // 2 * 2:2], mixed[1:number_of // 2 * 2:2]
    slack = jnp.minimum(tallies[source_of] - 1, reach - tallies[receiver]) // 2
    slack = jnp.where((source_of == sequence[0]) | (receiver == sequence[0]) | (tallies[receiver] == 0), 0, jnp.maximum(slack, 0))
    shifted = jax.random.randint(jax.random.fold_in(own, 4), (number_of // 2,), 0, 1 << 20) % (slack + 1)
    tallies = tallies.at[source_of].add(-shifted).at[receiver].add(shifted)
    items = jnp.searchsorted(jnp.cumsum(tallies), jnp.arange(rows * top), side="right").astype(jnp.int32)
    grid = items.reshape(top, rows).T
    grid = grid[jax.random.permutation(jax.random.fold_in(own, 1), rows)]
    turn = jax.random.randint(jax.random.fold_in(own, 2), (rows, 1), 0, top)
    return jnp.take_along_axis(grid, (jnp.arange(top)[None, :] + turn) % top, axis=1)


def shares(number_of, total, bound, skew, full):
    loads = [(1 << 20) // math.isqrt(rank ** skew) + 1 for rank in range(1, number_of + 1)]
    largest = bound if full else min(bound, max(-(-total // number_of), total * loads[0] // sum(loads)))
    least = 1 if total - largest >= number_of - 1 else 0
    given, surplus = [largest] + [least] * (number_of - 1), total - largest - least * (number_of - 1)
    while surplus > 0:
        movable = [i for i in range(1, number_of) if given[i] < largest] or [i for i in range(1, number_of) if given[i] < bound]
        whole, budget = sum([loads[i] for i in movable]), surplus
        for i in movable:
            more = min(bound - given[i], max(1, budget * loads[i] // whole), surplus)
            given[i] = given[i] + more
            surplus = surplus - more
    return np.array(given)


def centred(rng, extent, width, most, split=(), kind=jnp.bfloat16):
    entries = jax.random.normal(rng, extent, jnp.float32) * width
    if len(split) > 0:
        entries = block_scale(rng, extent, split, -0.22, 0.18) * entries
    return jnp.clip(entries, min=-most, max=most).astype(kind)


def setup_inputs(seed: int = 0) -> dict:
    key_of = jax.random.split(jax.random.key(seed), 11)
    tokens = draw_tokens(jax.random.fold_in(key_of[10], 71), 0)
    w_hidden = centred(key_of[1], (D, HID), D ** -0.5, 0.09375, ((0, 32), (1, 4)))
    w_out = centred(key_of[2], (HID, E), HID ** -0.5, 0.09375, ((0, 4),))
    bank = centred(key_of[3], (BANK, E), 0.0625, 0.5, ((0, 32),))
    item_ids = plant(ranked_wide(key_of[4], (BANK,), ITEMS, 2), jax.random.fold_in(key_of[4], 3), 0, ITEMS - 1).astype(jnp.int32)
    log_freq = jnp.clip(jax.random.uniform(key_of[5], (ITEMS,), jnp.float32, -14.0, -6.0), -14.0, -6.0).astype(jnp.bfloat16)
    positives = plant(jax.random.randint(key_of[6], (GROUPS, TOK_DEV), 0, BANK), jax.random.fold_in(key_of[6], 1), 0, BANK - 1).astype(jnp.int32)
    new_items = centred(key_of[7], (NEW, E), 0.0625, 0.5, ((0, 32),))
    new_owner_keys = jax.random.split(jax.random.fold_in(key_of[8], 1), NEW // NEW_DEV)
    new_owner_turns = jax.random.permutation(jax.random.fold_in(key_of[8], 3), NEW // NEW_DEV)
    new_owner = jax.vmap(lambda own, number: deal_out(jax.random.fold_in(key_of[8], 2), own, number, NEW_DEV, N_POOL, 1, CAP, 1))(new_owner_keys, new_owner_turns).reshape((NEW, 1))
    queue_head = plant(jax.random.randint(key_of[9], (N_POOL,), 0, BANK_DEV), jax.random.fold_in(key_of[9], 1), 0, BANK_DEV - 1).astype(jnp.int32)
    return dict(tokens=tokens, w_hidden=w_hidden, w_out=w_out, bank=bank, item_ids=item_ids, log_freq=log_freq, positives=positives, new_items=new_items, new_owner=new_owner, queue_head=queue_head)


inv_temp = 5.0


def reference(tokens, w_hidden, w_out, bank, item_ids, log_freq, positives, new_items, new_owner, queue_head):
    token_rows = tokens.reshape(-1, tokens.shape[2])
    pre_act = jnp.dot(token_rows, w_hidden, preferred_element_type=jnp.float32)
    hidden = jnp.maximum(pre_act, 0.0).astype(jnp.bfloat16)
    queries = jnp.dot(hidden, w_out, preferred_element_type=jnp.float32).astype(jnp.bfloat16)
    offsets = jnp.take(log_freq, item_ids).astype(jnp.float32)
    targets = positives.reshape(-1).astype(jnp.int32)
    row_count = queries.shape[0]
    bank_rows = bank.shape[0]
    block_width = 512 if bank_rows % 512 == 0 else bank_rows
    block_count = bank_rows // block_width
    blocks = bank.reshape(block_count, block_width, bank.shape[1])
    shifts = offsets.reshape(block_count, block_width)

    def block_step(running, inputs):
        run_max, run_sum, run_pos = running
        bank_block, block_offsets, block_index = inputs
        logits = inv_temp * jnp.dot(queries, bank_block.T, preferred_element_type=jnp.float32) - block_offsets[None, :]
        next_max = jnp.maximum(run_max, jnp.max(logits, axis=1))
        run_sum = run_sum * jnp.exp(run_max - next_max) + jnp.sum(jnp.exp(logits - next_max[:, None]), axis=1)
        columns = block_index * block_width + jnp.arange(block_width, dtype=jnp.int32)
        run_pos = run_pos + jnp.sum(jnp.where(columns[None, :] == targets[:, None], logits, 0.0), axis=1)
        return (next_max, run_sum, run_pos), None

    initial = (jnp.full((row_count,), -jnp.inf, jnp.float32), jnp.zeros((row_count,), jnp.float32), jnp.zeros((row_count,), jnp.float32))
    (run_max, run_sum, run_pos), _ = lax.scan(block_step, initial, (blocks, shifts, jnp.arange(block_count, dtype=jnp.int32)))
    query_loss = (run_max + jnp.log(run_sum) - run_pos).reshape(tokens.shape[0], tokens.shape[1])

    owners = new_owner[:, 0].astype(jnp.int32)
    onehot = (owners[:, None] == jnp.arange(N_POOL, dtype=jnp.int32)[None, :]).astype(jnp.int32)
    earlier = jnp.cumsum(onehot, axis=0, dtype=jnp.int32) - onehot
    ranks = jnp.sum(earlier * onehot, axis=1, dtype=jnp.int32)
    head_slot = jnp.sum(onehot * queue_head[None, :].astype(jnp.int32), axis=1, dtype=jnp.int32)
    slots = owners * BANK_DEV + (head_slot + ranks) % BANK_DEV
    new_bank = bank.at[slots].set(new_items)
    return query_loss, new_bank
```

```python
import functools
import jax
import jax.numpy as jnp
from jax import lax
from jax.experimental import pallas as pl
from jax.experimental.pallas import tpu as pltpu

AXES = ("dp", "tensor", "pool_0", "pool_1", "pool_2")
from jax.sharding import Mesh
from jax.sharding import PartitionSpec as P

MESH = pl.DeviceIdType.MESH

POOL = ("pool_0", "pool_1", "pool_2")
DP_POOL = ("dp", "pool_0", "pool_1", "pool_2")


inv_temp = 5.0


def split_up(x, dim, count):
    before, after = (x.shape[:dim], x.shape[dim + 1 :])
    return jnp.moveaxis(x.reshape(*before, count, -1, *after), dim, 0)


def sum_at_owner(x, axis, dim):
    count = lax.axis_size(axis)
    blocks = lax.all_to_all(split_up(x, dim, count), axis, 0, 0, tiled=True)
    return jnp.sum(blocks, axis=0)


def all_in_one(x, axis):
    leaves = jax.tree.leaves(x)
    turns = sorted(range(len(leaves)), key=lambda k: -leaves[k].size)
    width = (1, *leaves[turns[0]].shape)[-1]
    lines = [
        jnp.pad(leaves[k].reshape(-1), (0, -leaves[k].size % width)).reshape(-1, width)
        for k in turns
    ]
    both, at, found = (lax.all_gather(jnp.concatenate(lines), axis), 0, {})
    for k, line in zip(turns, lines):
        section = both[:, at : at + len(line)].reshape(len(both), -1)
        found[k] = section[:, : leaves[k].size].reshape(-1, *leaves[k].shape)
        at += len(line)
    numbers = iter(range(len(leaves)))
    return jax.tree.map(lambda _: found[next(numbers)], x)


def joined_all(x, axes, combine):
    for axis in axes:
        pieces = all_in_one(x, axis)
        x = jax.tree.map(lambda part: part[0], pieces)
        for k in range(1, lax.axis_size(axis)):
            x = combine(x, jax.tree.map(lambda part: part[k], pieces))
    return x


def copy_for_each(x, axis):
    copies = jnp.broadcast_to(x, (lax.axis_size(axis), *x.shape))
    return lax.all_to_all(copies, axis, split_axis=0, concat_axis=0, tiled=True)


def folded_in_pairs(pieces, combine):
    while len(jax.tree.leaves(pieces)[0]) > 1:
        pieces = jax.vmap(combine)(*(pieces[side::2] for side in (0, 1)))
    return pieces[0]


def entering(x, axis, combine, identity):
    count, position = (lax.axis_size(axis), lax.axis_index(axis))
    passed = jnp.arange(count) < position

    def kept(part, zero, own):
        part = jnp.where(
            passed.reshape(-1, *(1 for _ in own.shape)), part, jnp.asarray(zero, own.dtype)
        )
        return part

    pieces = copy_for_each(x, axis)
    return folded_in_pairs(kept(pieces, identity, x), combine)


def local_stats(query_rows, target_rows, bank, offsets, base_column):
    row_count = query_rows.shape[0]
    bank_rows = bank.shape[0]
    block_width = 512
    block_count = bank_rows // block_width
    blocks = bank.reshape(block_count, block_width, bank.shape[1])
    shifts = offsets.reshape(block_count, block_width)

    def block_step(running, inputs):
        run_max, run_sum, run_pos = running
        bank_block, block_offsets, block_index = inputs
        logits = (
            inv_temp * jnp.dot(query_rows, bank_block.T, preferred_element_type=jnp.float32)
            - block_offsets[None, :]
        )
        next_max = jnp.maximum(run_max, jnp.max(logits, axis=1))
        run_sum = run_sum * jnp.exp(run_max - next_max) + jnp.sum(
            jnp.exp(logits - next_max[:, None]), axis=1
        )
        columns = base_column + block_index * block_width + jnp.arange(block_width, dtype=jnp.int32)
        run_pos = run_pos + jnp.sum(
            jnp.where(columns[None, :] == target_rows[:, None], logits, 0.0), axis=1
        )
        return ((next_max, run_sum, run_pos), None)

    initial = (
        jnp.full((row_count,), -jnp.inf, jnp.float32),
        jnp.zeros((row_count,), jnp.float32),
        jnp.zeros((row_count,), jnp.float32),
    )
    final, _ = lax.scan(
        block_step, initial, (blocks, shifts, jnp.arange(block_count, dtype=jnp.int32))
    )
    return final


def combine(earlier_part, later_part):
    both_max = jnp.maximum(earlier_part[0], later_part[0])
    both_sum = earlier_part[1] * jnp.exp(earlier_part[0] - both_max) + later_part[1] * jnp.exp(
        later_part[0] - both_max
    )
    return (both_max, both_sum, earlier_part[2] + later_part[2])


def add_counts(earlier_part, later_part):
    return earlier_part + later_part


def tower_kernel(tok_hbm, w_hbm, wo_ref, out_ref, tok, wbuf, acc, tok_sem, own_sem, send_sem, recv_sem, psend, precv):
    dp, y, x, zl, c = (lax.axis_index(a) for a in AXES)
    pz = dp * 4 + zl
    R = w_hbm.shape[0]
    C = w_hbm.shape[1] // 2
    Q = C // 2
    M = tok.shape[1]
    offs = (0, -1, 1, 2)

    def chip(dx, dz):
        xx = lax.rem(x + dx + 4, 4)
        zz = lax.rem(pz + dz + 8, 8)
        return (zz // 4, y, xx, lax.rem(zz, 4), c)

    def along(h, first, step):
        return chip(step, 0) if (h == 0) == first else chip(0, step)

    partner = (dp, y, x, zl, 1 - c)

    def block_of(h, f, s):
        dx = f * (1 - h) + s * h
        dz = s * (1 - h) + f * h
        return lax.rem(x + dx + 4, 4) * 4 + lax.rem(zl + dz + 4, 4)

    def view(h, f, s, piece, core):
        row = pl.multiple_of(block_of(h, f, s) * (2 * R) + core * R, R)
        cols = slice(None) if piece is None else pl.ds(piece * Q, Q)
        return wbuf.at[h, pl.ds(row, R), cols]

    def key(h, f, s, piece):
        return ((h * 4 + offs.index(f)) * 4 + offs.index(s)) * 2 + (piece or 0)

    sends = []

    def send(h, f, s, piece, first, step, kind):
        nf, ns = kind
        ref = view(h, f, s, piece, c)
        cp = pltpu.make_async_remote_copy(
            src_ref=ref, dst_ref=ref, send_sem=send_sem.at[len(sends)],
            recv_sem=recv_sem.at[key(h, nf, ns, piece)],
            device_id=along(h, first, step), device_id_type=MESH)
        cp.start()
        sends.append(cp)

    psends = []

    def to_partner(h, f, s, piece):
        ref = view(h, f, s, piece, c)
        cp = pltpu.make_async_remote_copy(
            src_ref=ref, dst_ref=ref, send_sem=psend.at[key(h, f, s, piece)],
            recv_sem=precv.at[key(h, f, s, piece)], device_id=partner, device_id_type=MESH)
        cp.start()
        psends.append(cp)

    def wait_link(h, f, s, piece):
        ref = view(h, f, s, piece, c)
        pltpu.make_async_remote_copy(
            src_ref=ref, dst_ref=ref, send_sem=send_sem.at[0],
            recv_sem=recv_sem.at[key(h, f, s, piece)], device_id=partner, device_id_type=MESH).wait_recv()

    def wait_partner(h, f, s, piece):
        ref = view(h, f, s, piece, 1 - c)
        pltpu.make_async_remote_copy(
            src_ref=ref, dst_ref=ref, send_sem=send_sem.at[0],
            recv_sem=precv.at[key(h, f, s, piece)], device_id=partner, device_id_type=MESH).wait_recv()

    def pieces(f, s):
        return (0, 1) if (f == 2 and s == 0) or s == 2 else (None,)

    own = [pltpu.make_async_copy(w_hbm.at[:, pl.ds(h * C, C)], view(h, 0, 0, None, c), own_sem.at[h]) for h in (0, 1)]
    for cp in own:
        cp.start()

    barrier = pltpu.get_barrier_semaphore()
    peers = [chip(1, 0), chip(-1, 0), chip(0, 1), chip(0, -1), partner]
    for p in peers:
        pl.semaphore_signal(barrier, inc=1, device_id=p, device_id_type=MESH)

    groups = [[(0, 0)], [(-1, 0), (1, 0)], [(0, -1), (0, 1)], [(2, 0)],
              [(-1, -1), (-1, 1), (1, -1), (1, 1)], [(0, 2)], [(2, -1), (2, 1)], [(-1, 2), (1, 2)], [(2, 2)]]

    tok_wait = {}
    n = 0
    for g in groups:
        for f, s in g:
            for h in (0, 1):
                dx, dz = (f, s) if h == 0 else (s, f)
                if (dx, dz) in tok_wait:
                    continue
                b = block_of(0, dx, dz)
                cp = pltpu.make_async_copy(
                    tok_hbm.at[0, :, pl.ds(pl.multiple_of(b * 2 * R, 2 * R), 2 * R)], tok.at[b], tok_sem.at[n])
                cp.start()
                tok_wait[(dx, dz)] = cp
                n += 1

    for cp in own:
        cp.wait()
    pl.semaphore_wait(barrier, len(peers))

    for h in (0, 1):
        for step in (1, -1):
            send(h, 0, 0, None, True, step, (-step, 0))
    for h in (0, 1):
        to_partner(h, 0, 0, None)
    for h in (0, 1):
        for step in (1, -1):
            send(h, 0, 0, None, False, step, (0, -step))

    def relay(g):
        for f, s in groups[g]:
            for h in (0, 1):
                for p in pieces(f, s):
                    wait_link(h, f, s, p)
                if s == 0 and f != 2:
                    send(h, f, 0, 0 if f == -1 else 1, True, -f, (2, 0))
                if s == 0:
                    for step in (1, -1):
                        send(h, f, 0, None, False, step, (f, -step))
                elif s != 2:
                    send(h, f, s, 0 if s == -1 else 1, False, -s, (f, 2))
                for p in pieces(f, s):
                    to_partner(h, f, s, p)

    def mm(g):
        items = groups[g]
        for f, s in items:
            for h in (0, 1):
                dx, dz = (f, s) if h == 0 else (s, f)
                if (dx, dz) in tok_wait:
                    tok_wait.pop((dx, dz)).wait()
                for p in pieces(f, s):
                    wait_partner(h, f, s, p)

        def step(i, carry):
            h = lax.rem(i, 2)
            j = i // 2
            f = sum(jnp.where(j == k, fs[0], 0) for k, fs in enumerate(items))
            s = sum(jnp.where(j == k, fs[1], 0) for k, fs in enumerate(items))
            b = block_of(h, f, s)
            row = pl.multiple_of(b * (2 * R), 2 * R)
            d = jnp.dot(tok[b], wbuf[h, pl.ds(row, 2 * R), :], preferred_element_type=jnp.float32)
            if g == 0:
                acc[h] = d
            else:
                acc[h] = acc[h] + d
            return carry

        lax.fori_loop(0, 2 * len(items), step, 0)

    relay(1)
    mm(0)
    relay(2)
    mm(1)
    relay(3)
    mm(2)
    mm(3)
    relay(4)
    mm(4)
    relay(5)
    mm(5)
    relay(6)
    mm(6)
    relay(7)
    mm(7)
    relay(8)
    mm(8)

    T = min(256, M)

    def out_step(r, carry):
        rs = pl.ds(pl.multiple_of(r * T, T), T)
        total = None
        for h in (0, 1):
            hid = jnp.maximum(acc[h, rs, :], 0.0).astype(jnp.bfloat16)
            d = jnp.dot(hid, wo_ref[pl.ds(h * C, C), :], preferred_element_type=jnp.float32)
            total = d if total is None else total + d
        out_ref[rs, :] = total
        return carry

    lax.fori_loop(0, M // T, out_step, 0)

    for cp in sends + psends:
        cp.wait_send()


def tower(tokens, w_hidden, w_out):
    M, K = tokens.shape[1:]
    R, N = w_hidden.shape
    E = w_out.shape[1]
    return pl.pallas_call(
        tower_kernel,
        out_shape=jax.ShapeDtypeStruct((M, E), jnp.float32),
        in_specs=[pl.BlockSpec(memory_space=pl.ANY), pl.BlockSpec(memory_space=pl.ANY), pl.BlockSpec(memory_space=pltpu.VMEM)],
        out_specs=pl.BlockSpec(memory_space=pltpu.VMEM),
        scratch_shapes=[
            pltpu.VMEM((16, M, 2 * R), jnp.bfloat16),
            pltpu.VMEM((2, K, N // 2), jnp.bfloat16),
            pltpu.VMEM((2, M, N // 2), jnp.float32),
            pltpu.SemaphoreType.DMA((16,)),
            pltpu.SemaphoreType.DMA((2,)),
            pltpu.SemaphoreType.DMA((46,)),
            pltpu.SemaphoreType.DMA((64,)),
            pltpu.SemaphoreType.DMA((64,)),
            pltpu.SemaphoreType.DMA((64,)),
        ],
        compiler_params=pltpu.CompilerParams(collective_id=0, has_side_effects=True, vmem_limit_bytes=50 * 1024 * 1024),
        name="tower",
    )(tokens, w_hidden, w_out)


def body(
    tokens, w_hidden, w_out, bank, item_ids, log_freq, positives, new_items, new_owner, queue_head
):
    partial_value = tower(tokens, w_hidden, w_out)
    queries = sum_at_owner(partial_value, "tensor", 0).astype(jnp.bfloat16)
    offsets = jnp.take(log_freq, item_ids).astype(jnp.float32)
    own_index = lax.axis_index(POOL)
    base_column = own_index * bank.shape[0]
    query_piece = lax.all_gather(queries[None], POOL, axis=0, tiled=True)
    target_piece = lax.all_gather(positives, POOL, axis=0, tiled=True)
    groups_in = query_piece.shape[0]
    run_max, run_sum, run_pos = local_stats(
        query_piece.reshape(-1, query_piece.shape[2]),
        target_piece.reshape(-1),
        bank,
        offsets,
        base_column,
    )
    maxima = run_max.reshape(groups_in, -1)
    totals = run_sum.reshape(groups_in, -1)
    scores = run_pos.reshape(groups_in, -1)
    maxima, totals, scores = (maxima, totals, scores)
    maxima, totals, scores = joined_all((maxima, totals, scores), POOL, combine)
    own_max = lax.dynamic_slice_in_dim(maxima, own_index, 1, 0)
    own_sum = lax.dynamic_slice_in_dim(totals, own_index, 1, 0)
    own_pos = lax.dynamic_slice_in_dim(scores, own_index, 1, 0)
    query_loss = own_max + jnp.log(own_sum) - own_pos
    owners = new_owner[:, 0]
    head_slot = queue_head[0]
    shard_rows = bank.shape[0]
    peer_count = lax.axis_size(POOL)
    local_rows = new_items.shape[0]
    capacity = 2 * local_rows // peer_count
    onehot = (owners[:, None] == jnp.arange(peer_count, dtype=jnp.int32)[None, :]).astype(jnp.int32)
    counts = jnp.sum(onehot, axis=0, dtype=jnp.int32)
    before = jnp.sum(
        (jnp.cumsum(onehot, axis=0, dtype=jnp.int32) - onehot) * onehot, axis=1, dtype=jnp.int32
    )
    earlier = entering(counts, POOL, add_counts, jnp.zeros_like(counts))
    ranks = before + jnp.sum(onehot * earlier[None, :], axis=1, dtype=jnp.int32)
    send_pos = owners * capacity + before
    rows_out = (
        jnp.zeros((peer_count * capacity, new_items.shape[1]), jnp.bfloat16)
        .at[send_pos]
        .set(new_items)
    )
    ranks_out = jnp.full((peer_count * capacity,), -1, jnp.int32).at[send_pos].set(ranks)
    rows_in, ranks_in = (
        lax.all_to_all(
            rows_out.reshape(peer_count, capacity, -1),
            POOL,
            split_axis=0,
            concat_axis=0,
            tiled=True,
        ),
        lax.all_to_all(
            ranks_out.reshape(peer_count, capacity), POOL, split_axis=0, concat_axis=0, tiled=True
        ),
    )
    local_slots = jnp.where(ranks_in >= 0, (head_slot + ranks_in) % shard_rows, shard_rows).reshape(
        -1
    )
    new_bank = bank.at[local_slots].set(rows_in.reshape(-1, new_items.shape[1]), mode="drop")
    return (query_loss, new_bank)


def solution(mesh):
    finer = Mesh(
        mesh.devices.reshape(mesh.shape["dp"], mesh.shape["tensor"], 4, 4, 2),
        ("dp", "tensor", "pool_0", "pool_1", "pool_2"),
    )
    in_specs = (
        P(DP_POOL, None, None),
        P(POOL, "tensor"),
        P("tensor", None),
        P(POOL, None),
        P(POOL),
        P(),
        P(DP_POOL, "tensor"),
        P(POOL, None),
        P(POOL, None),
        P(POOL),
    )
    out_specs = (P(DP_POOL, "tensor"), P(POOL, None))
    return jax.shard_map(body, mesh=finer, in_specs=in_specs, out_specs=out_specs, check_vma=False)
```

```python
import functools
import jax
import jax.numpy as jnp
from jax import lax
from jax.experimental import pallas as pl
from jax.experimental.pallas import tpu as pltpu

AXES = ("dp", "tensor", "pool_0", "pool_1", "pool_2")
from jax.sharding import Mesh
from jax.sharding import PartitionSpec as P

MESH = pl.DeviceIdType.MESH
POOL = ("pool_0", "pool_1", "pool_2")
DP_POOL = ("dp", "pool_0", "pool_1", "pool_2")


LOG2E = 1.4426950408889634
LN2 = 0.6931471805599453


def tower_kernel(tok_hbm, w_hbm, wo_ref, bank_hbm, off_hbm, pos_ref, out_ref, tok, wbuf, acc, part, ysend, yrecv,
                 bankbuf, offb, qbuf, qt, tbuf, sbuf, stats, tok_sem, own_sem, send_sem, recv_sem, psend, precv,
                 xsend, xrecv, ysem, yrsem, qsend, qrecv, tsend, trecv, ssend, srecv):
    dp, y, x, zl, c = (lax.axis_index(a) for a in AXES)
    ny = lax.axis_size("tensor")
    pz = dp * 4 + zl
    R = w_hbm.shape[0]
    C = w_hbm.shape[1] // 2
    Q = C // 2
    M = tok.shape[1]
    offs = (0, -1, 1, 2)

    def chip(dx, dz):
        xx = lax.rem(x + dx + 4, 4)
        zz = lax.rem(pz + dz + 8, 8)
        return (zz // 4, y, xx, lax.rem(zz, 4), c)

    def along(h, first, step):
        return chip(step, 0) if (h == 0) == first else chip(0, step)

    partner = (dp, y, x, zl, 1 - c)

    def column(step):
        return (dp, lax.rem(y + step + ny, ny), x, zl, c)

    def block_of(h, f, s):
        dx = f * (1 - h) + s * h
        dz = s * (1 - h) + f * h
        return lax.rem(x + dx + 4, 4) * 4 + lax.rem(zl + dz + 4, 4)

    def view(h, f, s, piece, core):
        row = pl.multiple_of(block_of(h, f, s) * (2 * R) + core * R, R)
        cols = slice(None) if piece is None else pl.ds(piece * Q, Q)
        return wbuf.at[h, pl.ds(row, R), cols]

    def key(h, f, s, piece):
        return ((h * 4 + offs.index(f)) * 4 + offs.index(s)) * 2 + (piece or 0)

    sends = []

    def send(h, f, s, piece, first, step, kind):
        nf, ns = kind
        ref = view(h, f, s, piece, c)
        cp = pltpu.make_async_remote_copy(
            src_ref=ref, dst_ref=ref, send_sem=send_sem.at[len(sends)],
            recv_sem=recv_sem.at[key(h, nf, ns, piece)],
            device_id=along(h, first, step), device_id_type=MESH)
        cp.start()
        sends.append(cp)

    psends = []

    def to_partner(h, f, s, piece):
        ref = view(h, f, s, piece, c)
        cp = pltpu.make_async_remote_copy(
            src_ref=ref, dst_ref=ref, send_sem=psend.at[key(h, f, s, piece)],
            recv_sem=precv.at[key(h, f, s, piece)], device_id=partner, device_id_type=MESH)
        cp.start()
        psends.append(cp)

    def wait_link(h, f, s, piece):
        ref = view(h, f, s, piece, c)
        pltpu.make_async_remote_copy(
            src_ref=ref, dst_ref=ref, send_sem=send_sem.at[0],
            recv_sem=recv_sem.at[key(h, f, s, piece)], device_id=partner, device_id_type=MESH).wait_recv()

    def wait_partner(h, f, s, piece):
        ref = view(h, f, s, piece, 1 - c)
        pltpu.make_async_remote_copy(
            src_ref=ref, dst_ref=ref, send_sem=send_sem.at[0],
            recv_sem=precv.at[key(h, f, s, piece)], device_id=partner, device_id_type=MESH).wait_recv()

    def pieces(f, s):
        return (0, 1) if (f == 2 and s == 0) or s == 2 else (None,)

    B = bank_hbm.shape[0]
    mine = pl.ds(pl.multiple_of(c * B, B), B)
    own = [pltpu.make_async_copy(w_hbm.at[:, pl.ds(h * C, C)], view(h, 0, 0, None, c), own_sem.at[h]) for h in (0, 1)]
    own.append(pltpu.make_async_copy(bank_hbm, bankbuf.at[mine, :], own_sem.at[2]))
    own.append(pltpu.make_async_copy(off_hbm, offb.at[mine, :], own_sem.at[3]))
    for cp in own:
        cp.start()

    barrier = pltpu.get_barrier_semaphore()
    peers = [chip(1, 0), chip(-1, 0), chip(0, 1), chip(0, -1), partner]
    if ny > 1:
        peers += [column(1), column(-1)]
    for p in peers:
        pl.semaphore_signal(barrier, inc=1, device_id=p, device_id_type=MESH)

    groups = [[(0, 0)], [(-1, 0), (1, 0)], [(0, -1), (0, 1)], [(2, 0)],
              [(-1, -1), (-1, 1), (1, -1), (1, 1)], [(0, 2)], [(2, -1), (2, 1)], [(-1, 2), (1, 2)], [(2, 2)]]

    tok_wait = {}
    n = 0
    for g in groups:
        for f, s in g:
            for h in (0, 1):
                dx, dz = (f, s) if h == 0 else (s, f)
                if (dx, dz) in tok_wait:
                    continue
                b = block_of(0, dx, dz)
                cp = pltpu.make_async_copy(
                    tok_hbm.at[0, :, pl.ds(pl.multiple_of(b * 2 * R, 2 * R), 2 * R)], tok.at[b], tok_sem.at[n])
                cp.start()
                tok_wait[(dx, dz)] = cp
                n += 1

    for cp in own:
        cp.wait()
    pl.semaphore_wait(barrier, len(peers))

    for h in (0, 1):
        for step in (1, -1):
            send(h, 0, 0, None, True, step, (-step, 0))
    for h in (0, 1):
        to_partner(h, 0, 0, None)
    for h in (0, 1):
        for step in (1, -1):
            send(h, 0, 0, None, False, step, (0, -step))

    swaps = []
    for i, ref in enumerate((bankbuf, offb)):
        cp = pltpu.make_async_remote_copy(
            src_ref=ref.at[mine, :], dst_ref=ref.at[mine, :], send_sem=xsend.at[i], recv_sem=xrecv.at[i],
            device_id=partner, device_id_type=MESH)
        cp.start()
        swaps.append(cp)

    def relay(g):
        for f, s in groups[g]:
            for h in (0, 1):
                for p in pieces(f, s):
                    wait_link(h, f, s, p)
                if s == 0 and f != 2:
                    send(h, f, 0, 0 if f == -1 else 1, True, -f, (2, 0))
                if s == 0:
                    for step in (1, -1):
                        send(h, f, 0, None, False, step, (f, -step))
                elif s != 2:
                    send(h, f, s, 0 if s == -1 else 1, False, -s, (f, 2))
                for p in pieces(f, s):
                    to_partner(h, f, s, p)

    def mm(g):
        items = groups[g]
        for f, s in items:
            for h in (0, 1):
                dx, dz = (f, s) if h == 0 else (s, f)
                if (dx, dz) in tok_wait:
                    tok_wait.pop((dx, dz)).wait()
                for p in pieces(f, s):
                    wait_partner(h, f, s, p)

        def step(i, carry):
            h = lax.rem(i, 2)
            j = i // 2
            f = sum(jnp.where(j == k, fs[0], 0) for k, fs in enumerate(items))
            s = sum(jnp.where(j == k, fs[1], 0) for k, fs in enumerate(items))
            b = block_of(h, f, s)
            row = pl.multiple_of(b * (2 * R), 2 * R)
            d = jnp.dot(tok[b], wbuf[h, pl.ds(row, 2 * R), :], preferred_element_type=jnp.float32)
            if g == 0:
                acc[h] = d
            else:
                acc[h] = acc[h] + d
            return carry

        lax.fori_loop(0, 2 * len(items), step, 0)

    relay(1)
    mm(0)
    relay(2)
    mm(1)
    relay(3)
    mm(2)
    mm(3)
    relay(4)
    mm(4)
    relay(5)
    mm(5)
    relay(6)
    mm(6)
    relay(7)
    mm(7)
    relay(8)
    mm(8)

    far = [(i, k) for i in offs for k in (0, -1, 1, 2, -2) if (i, k) != (0, 0)]

    def spot(i, k):
        return offs.index(i) * 5 + (0, -1, 1, 2, -2).index(k)

    def mirror(i, k):
        return spot(i if i == 2 else -i, -k)

    tcopies = []
    for n, (i, k) in enumerate(far):
        cp = pltpu.make_async_remote_copy(
            src_ref=pos_ref, dst_ref=tbuf.at[mirror(i, k)], send_sem=tsend.at[n], recv_sem=trecv.at[mirror(i, k)],
            device_id=chip(i, k), device_id_type=MESH)
        cp.start()
        tcopies.append(cp)

    T = M // 4
    H = part.shape[1] // 2
    left, right = pl.ds(0, H), pl.ds(H, H)

    def quarter(step):
        return pl.ds(pl.multiple_of(lax.rem(y + step + 4, 4) * T, T), T)

    def partial(step):
        rs = quarter(step)
        total = None
        for h in (0, 1):
            hid = jnp.maximum(acc[h, rs, :], 0.0).astype(jnp.bfloat16)
            d = jnp.dot(hid, wo_ref[pl.ds(h * C, C), :], preferred_element_type=jnp.float32)
            total = d if total is None else total + d
        part[rs, :] = total

    ycopies = []

    def ysend_to(slot, step):
        cp = pltpu.make_async_remote_copy(
            src_ref=ysend.at[slot], dst_ref=yrecv.at[slot], send_sem=ysem.at[slot], recv_sem=yrsem.at[slot],
            device_id=column(step), device_id_type=MESH)
        cp.start()
        ycopies.append(cp)

    def ywait(slot):
        pltpu.make_async_remote_copy(
            src_ref=ysend.at[slot], dst_ref=yrecv.at[slot], send_sem=ysem.at[slot], recv_sem=yrsem.at[slot],
            device_id=partner, device_id_type=MESH).wait_recv()

    bf = jnp.bfloat16
    f32 = jnp.float32
    if ny > 1:
        partial(2)
        ysend[0] = part[quarter(2), left].astype(bf)
        ysend_to(0, -1)
        ysend[1] = part[quarter(2), right].astype(bf)
        ysend_to(1, 1)
        partial(-1)
        ysend[2] = part[quarter(-1), right].astype(bf)
        ysend_to(2, -1)
        partial(1)
        ysend[3] = part[quarter(1), left].astype(bf)
        ysend_to(3, 1)
        ywait(0)
        ysend[4] = (yrecv[0].astype(f32) + part[quarter(-1), left]).astype(bf)
        ysend_to(4, -1)
        ywait(1)
        ysend[5] = (yrecv[1].astype(f32) + part[quarter(1), right]).astype(bf)
        ysend_to(5, 1)
        partial(0)
        ywait(2)
        ywait(3)
        ywait(4)
        ywait(5)
        own_q = quarter(0)
        qbuf[0, :, left] = (part[own_q, left] + yrecv[3].astype(f32) + yrecv[4].astype(f32)).astype(bf)
        qbuf[0, :, right] = (part[own_q, right] + yrecv[2].astype(f32) + yrecv[5].astype(f32)).astype(bf)
    else:
        partial(0)
        qbuf[0] = part[pl.ds(0, T), :].astype(bf)

    P2 = T // 2
    P4 = T // 4

    def qview(h, f, s, piece):
        dx, dz = (f, s) if h == 0 else (s, f)
        rows = pl.ds(h * P2, P2) if piece is None else pl.ds(h * P2 + piece * P4, P4)
        return qbuf.at[offs.index(dx) * 4 + offs.index(dz), rows, :]

    qsends = []

    def qgo(h, f, s, piece, first, step, kind):
        cp = pltpu.make_async_remote_copy(
            src_ref=qview(h, f, s, piece), dst_ref=qview(h, kind[0], kind[1], piece), send_sem=qsend.at[len(qsends)],
            recv_sem=qrecv.at[key(h, kind[0], kind[1], piece)],
            device_id=along(h, first, step), device_id_type=MESH)
        cp.start()
        qsends.append(cp)

    def qwait(h, f, s, piece):
        ref = qview(h, f, s, piece)
        pltpu.make_async_remote_copy(
            src_ref=ref, dst_ref=ref, send_sem=qsend.at[0],
            recv_sem=qrecv.at[key(h, f, s, piece)], device_id=partner, device_id_type=MESH).wait_recv()

    for first in (True, False):
        for h in (0, 1):
            for step in (1, -1):
                qgo(h, 0, 0, None, first, step, (-step, 0) if first else (0, -step))

    def qrelay(g):
        for f, s in groups[g]:
            for h in (0, 1):
                for p in pieces(f, s):
                    qwait(h, f, s, p)
                if s == 0 and f != 2:
                    qgo(h, f, 0, 0 if f == -1 else 1, True, -f, (2, 0))
                if s == 0:
                    for step in (1, -1):
                        qgo(h, f, 0, None, False, step, (f, -step))
                elif s != 2:
                    qgo(h, f, s, 0 if s == -1 else 1, False, -s, (f, 2))

    for cp in swaps:
        cp.wait_recv()
    tbuf[0] = pos_ref[...]
    for i, k in far:
        pltpu.make_async_remote_copy(
            src_ref=pos_ref, dst_ref=tbuf.at[spot(i, k)], send_sem=tsend.at[0], recv_sem=trecv.at[spot(i, k)],
            device_id=partner, device_id_type=MESH).wait_recv()

    base = (x * 4 + zl) * (2 * B)
    CH = min(512, 2 * B)
    lane = lax.broadcasted_iota(jnp.int32, (1, T), 1)
    lower = lax.rem(lane, P2) < P4
    sub = lax.broadcasted_iota(jnp.int32, (8, T), 0)
    W = sbuf.shape[2]
    scopies = []

    def block(dx, dz):
        slot = offs.index(dx) * 4 + offs.index(dz)
        qt[...] = jnp.transpose(qbuf[slot])
        if dz == 2:
            target = jnp.where(lower, tbuf[spot(dx, -2)], tbuf[spot(dx, 2)])
        else:
            target = tbuf[spot(dx, dz)]
        t = jnp.broadcast_to(target - base, (8, T))
        group = lax.shift_right_arithmetic(t, 3)

        def chunk(k, carry):
            m, total, hit = carry
            rows = pl.ds(pl.multiple_of(k * CH, CH), CH)
            prod = jnp.dot(bankbuf[rows, :], qt[...], preferred_element_type=f32)
            off = offb[rows, :]
            if T > off.shape[1]:
                off = jnp.concatenate([off] * (T // off.shape[1]), axis=1)
            logit = (prod * (5.0 * LOG2E) - off).reshape(CH // 8, 8, T)
            top = jnp.maximum(m, jnp.max(logit, axis=0))
            here = group - k * (CH // 8)
            for r in range(CH // 8):
                hit = jnp.where(here == r, logit[r], hit)
            total = total * jnp.exp2(m - top) + jnp.sum(jnp.exp2(logit - top[None]), axis=0)
            return top, total, hit

        zero = jnp.zeros((8, T), f32)
        m, total, hit = lax.fori_loop(0, 2 * B // CH, chunk, (jnp.full((8, T), -jnp.inf, f32), zero, zero))
        top = jnp.max(m, axis=0, keepdims=True)
        total = jnp.sum(total * jnp.exp2(m - top), axis=0, keepdims=True)
        score = jnp.sum(jnp.where(jnp.bitwise_and(t, 7) == sub, hit, 0.0), axis=0, keepdims=True)
        for n, v in enumerate((top, total, score)):
            for k in range(2):
                sbuf[slot, pl.ds(n * 2 + k, 1), :] = v[:, k * W:(k + 1) * W]
        for k in ((dz,) if dz != 2 else (2, -2)):
            if (dx, k) == (0, 0):
                continue
            cp = pltpu.make_async_remote_copy(
                src_ref=sbuf.at[slot], dst_ref=stats.at[mirror(dx, k)], send_sem=ssend.at[len(scopies)],
                recv_sem=srecv.at[mirror(dx, k)], device_id=chip(dx, k), device_id_type=MESH)
            cp.start()
            scopies.append(cp)

    block(0, 0)
    qrelay(1)
    qrelay(2)
    for dx, dz in ((-1, 0), (1, 0), (0, -1), (0, 1)):
        block(dx, dz)
    qrelay(3)
    qrelay(4)
    for dx, dz in ((-1, -1), (-1, 1), (1, -1), (1, 1)):
        block(dx, dz)
    qrelay(5)
    block(2, 0)
    block(0, 2)
    qrelay(6)
    qrelay(7)
    for dx, dz in ((2, -1), (2, 1), (-1, 2), (1, 2)):
        block(dx, dz)
    qrelay(8)
    block(2, 2)

    stats[0] = sbuf[0]
    for i, k in far:
        pltpu.make_async_remote_copy(
            src_ref=sbuf.at[0], dst_ref=stats.at[spot(i, k)], send_sem=ssend.at[0], recv_sem=srecv.at[spot(i, k)],
            device_id=partner, device_id_type=MESH).wait_recv()
    low = lax.broadcasted_iota(jnp.int32, (8, W), 1) < P4
    parts = []
    for i in offs:
        for k in (0, -1, 1):
            st = stats[spot(i, k)]
            parts.append((st[0:2], st[2:4], st[4:6]))
        st = jnp.where(low, stats[spot(i, 2)], stats[spot(i, -2)])
        parts.append((st[0:2], st[2:4], st[4:6]))
    top = functools.reduce(jnp.maximum, [p[0] for p in parts])
    total = sum(p[1] * jnp.exp2(p[0] - top) for p in parts)
    score = sum(p[2] for p in parts)
    loss = LN2 * (top - score) + jnp.log(total)
    for k in range(2):
        out_ref[:, k * W:(k + 1) * W] = loss[k:k + 1, :]

    for cp in sends + psends + swaps + tcopies + ycopies + qsends + scopies:
        cp.wait_send()


def tower(tokens, w_hidden, w_out, bank, offsets, positives):
    M, K = tokens.shape[1:]
    R, N = w_hidden.shape
    E = w_out.shape[1]
    B = bank.shape[0]
    T = M // 4
    anywhere = pl.BlockSpec(memory_space=pl.ANY)
    vmem = pl.BlockSpec(memory_space=pltpu.VMEM)
    dma = pltpu.SemaphoreType.DMA
    return pl.pallas_call(
        tower_kernel,
        out_shape=jax.ShapeDtypeStruct((1, T), jnp.float32),
        in_specs=[anywhere, anywhere, vmem, anywhere, anywhere, vmem],
        out_specs=vmem,
        scratch_shapes=[
            pltpu.VMEM((16, M, 2 * R), jnp.bfloat16),
            pltpu.VMEM((2, K, N // 2), jnp.bfloat16),
            pltpu.VMEM((2, M, N // 2), jnp.float32),
            pltpu.VMEM((M, E), jnp.float32),
            pltpu.VMEM((6, T, E // 2), jnp.bfloat16),
            pltpu.VMEM((6, T, E // 2), jnp.bfloat16),
            pltpu.VMEM((2 * B, E), jnp.bfloat16),
            pltpu.VMEM((2 * B, offsets.shape[1]), jnp.float32),
            pltpu.VMEM((16, T, E), jnp.bfloat16),
            pltpu.VMEM((E, T), jnp.bfloat16),
            pltpu.VMEM((20, 1, T), jnp.int32),
            pltpu.VMEM((16, 8, T // 2), jnp.float32),
            pltpu.VMEM((20, 8, T // 2), jnp.float32),
            dma((16,)), dma((4,)), dma((40,)), dma((64,)), dma((64,)), dma((64,)),
            dma((2,)), dma((2,)), dma((6,)), dma((6,)), dma((40,)), dma((64,)),
            dma((19,)), dma((20,)), dma((19,)), dma((20,)),
        ],
        compiler_params=pltpu.CompilerParams(collective_id=0, has_side_effects=True, vmem_limit_bytes=56 * 1024 * 1024),
        name="tower",
    )(tokens, w_hidden, w_out, bank, offsets, positives)


def copy_for_each(x, axis):
    copies = jnp.broadcast_to(x, (lax.axis_size(axis), *x.shape))
    return lax.all_to_all(copies, axis, split_axis=0, concat_axis=0, tiled=True)


def folded_in_pairs(pieces, combine):
    while len(jax.tree.leaves(pieces)[0]) > 1:
        pieces = jax.vmap(combine)(*(pieces[side::2] for side in (0, 1)))
    return pieces[0]


def entering(x, axis, combine, identity):
    count, position = (lax.axis_size(axis), lax.axis_index(axis))
    passed = jnp.arange(count) < position

    def kept(part, zero, own):
        part = jnp.where(
            passed.reshape(-1, *(1 for _ in own.shape)), part, jnp.asarray(zero, own.dtype)
        )
        return part

    pieces = copy_for_each(x, axis)
    return folded_in_pairs(kept(pieces, identity, x), combine)


def add_counts(earlier_part, later_part):
    return earlier_part + later_part


def body(
    tokens, w_hidden, w_out, bank, item_ids, log_freq, positives, new_items, new_owner, queue_head
):
    offsets = jnp.take(log_freq, item_ids).astype(jnp.float32) * LOG2E
    offsets = jnp.broadcast_to(offsets[:, None], (bank.shape[0], 128))
    query_loss = tower(tokens, w_hidden, w_out, bank, offsets, positives)
    owners = new_owner[:, 0]
    head_slot = queue_head[0]
    shard_rows = bank.shape[0]
    peer_count = lax.axis_size(POOL)
    local_rows = new_items.shape[0]
    capacity = 2 * local_rows // peer_count
    onehot = (owners[:, None] == jnp.arange(peer_count, dtype=jnp.int32)[None, :]).astype(jnp.int32)
    counts = jnp.sum(onehot, axis=0, dtype=jnp.int32)
    before = jnp.sum(
        (jnp.cumsum(onehot, axis=0, dtype=jnp.int32) - onehot) * onehot, axis=1, dtype=jnp.int32
    )
    earlier = entering(counts, POOL, add_counts, jnp.zeros_like(counts))
    ranks = before + jnp.sum(onehot * earlier[None, :], axis=1, dtype=jnp.int32)
    send_pos = owners * capacity + before
    rows_out = (
        jnp.zeros((peer_count * capacity, new_items.shape[1]), jnp.bfloat16)
        .at[send_pos]
        .set(new_items)
    )
    ranks_out = jnp.full((peer_count * capacity,), -1, jnp.int32).at[send_pos].set(ranks)
    rows_in, ranks_in = (
        lax.all_to_all(
            rows_out.reshape(peer_count, capacity, -1),
            POOL,
            split_axis=0,
            concat_axis=0,
            tiled=True,
        ),
        lax.all_to_all(
            ranks_out.reshape(peer_count, capacity), POOL, split_axis=0, concat_axis=0, tiled=True
        ),
    )
    local_slots = jnp.where(ranks_in >= 0, (head_slot + ranks_in) % shard_rows, shard_rows).reshape(
        -1
    )
    new_bank = bank.at[local_slots].set(rows_in.reshape(-1, new_items.shape[1]), mode="drop")
    return (query_loss, new_bank)


def solution(mesh):
    finer = Mesh(
        mesh.devices.reshape(mesh.shape["dp"], mesh.shape["tensor"], 4, 4, 2),
        ("dp", "tensor", "pool_0", "pool_1", "pool_2"),
    )
    in_specs = (
        P(DP_POOL, None, None),
        P(POOL, "tensor"),
        P("tensor", None),
        P(POOL, None),
        P(POOL),
        P(),
        P(DP_POOL, "tensor"),
        P(POOL, None),
        P(POOL, None),
        P(POOL),
    )
    out_specs = (P(DP_POOL, "tensor"), P(POOL, None))
    return jax.shard_map(body, mesh=finer, in_specs=in_specs, out_specs=out_specs, check_vma=False)
```

```python
import functools
import jax
import jax.numpy as jnp
from jax import lax
from jax.experimental import pallas as pl
from jax.experimental.pallas import tpu as pltpu

AXES = ("dp", "tensor", "pool_0", "pool_1", "pool_2")
from jax.sharding import Mesh
from jax.sharding import PartitionSpec as P

MESH = pl.DeviceIdType.MESH
POOL = ("pool_0", "pool_1", "pool_2")
DP_POOL = ("dp", "pool_0", "pool_1", "pool_2")


LOG2E = 1.4426950408889634
LN2 = 0.6931471805599453


def tower_kernel(tok_hbm, w_hbm, wo_ref, bank_hbm, freq_hbm, ids_ref, pos_ref, items_ref,
                 owner_ref, head_ref, out_ref, newbank_ref, tok, wbuf, acc, part, ysend, yrecv,
                 bankbuf, offb, qbuf, qt, tbuf, sbuf, stats, table, pick, where_at, found, packed, counts, rows_in, counts_in, tok_sem, own_sem, send_sem, recv_sem, psend, precv,
                 xsend, xrecv, ysem, yrsem, qsend, qrecv, tsend, trecv, ssend, srecv,
                 nsend, nrecv, csend, crecv):
    dp, y, x, zl, c = (lax.axis_index(a) for a in AXES)
    ny = lax.axis_size("tensor")
    pz = dp * 4 + zl
    R = w_hbm.shape[0]
    C = w_hbm.shape[1] // 2
    Q = C // 2
    M = tok.shape[1]
    offs = (0, -1, 1, 2)

    def chip(dx, dz):
        xx = lax.rem(x + dx + 4, 4)
        zz = lax.rem(pz + dz + 8, 8)
        return (zz // 4, y, xx, lax.rem(zz, 4), c)

    def along(h, first, step):
        return chip(step, 0) if (h == 0) == first else chip(0, step)

    partner = (dp, y, x, zl, 1 - c)

    def column(step):
        return (dp, lax.rem(y + step + ny, ny), x, zl, c)

    def block_of(h, f, s):
        dx = f * (1 - h) + s * h
        dz = s * (1 - h) + f * h
        return lax.rem(x + dx + 4, 4) * 4 + lax.rem(zl + dz + 4, 4)

    def view(h, f, s, piece, core):
        row = pl.multiple_of(block_of(h, f, s) * (2 * R) + core * R, R)
        cols = slice(None) if piece is None else pl.ds(piece * Q, Q)
        return wbuf.at[h, pl.ds(row, R), cols]

    def key(h, f, s, piece):
        return ((h * 4 + offs.index(f)) * 4 + offs.index(s)) * 2 + (piece or 0)

    sends = []

    def send(h, f, s, piece, first, step, kind):
        nf, ns = kind
        ref = view(h, f, s, piece, c)
        cp = pltpu.make_async_remote_copy(
            src_ref=ref, dst_ref=ref, send_sem=send_sem.at[len(sends)],
            recv_sem=recv_sem.at[key(h, nf, ns, piece)],
            device_id=along(h, first, step), device_id_type=MESH)
        cp.start()
        sends.append(cp)

    psends = []

    def to_partner(h, f, s, piece):
        ref = view(h, f, s, piece, c)
        cp = pltpu.make_async_remote_copy(
            src_ref=ref, dst_ref=ref, send_sem=psend.at[key(h, f, s, piece)],
            recv_sem=precv.at[key(h, f, s, piece)], device_id=partner, device_id_type=MESH)
        cp.start()
        psends.append(cp)

    def wait_link(h, f, s, piece):
        ref = view(h, f, s, piece, c)
        pltpu.make_async_remote_copy(
            src_ref=ref, dst_ref=ref, send_sem=send_sem.at[0],
            recv_sem=recv_sem.at[key(h, f, s, piece)], device_id=partner, device_id_type=MESH).wait_recv()

    def wait_partner(h, f, s, piece):
        ref = view(h, f, s, piece, 1 - c)
        pltpu.make_async_remote_copy(
            src_ref=ref, dst_ref=ref, send_sem=send_sem.at[0],
            recv_sem=precv.at[key(h, f, s, piece)], device_id=partner, device_id_type=MESH).wait_recv()

    def pieces(f, s):
        return (0, 1) if (f == 2 and s == 0) or s == 2 else (None,)

    B = bank_hbm.shape[0]
    mine = pl.ds(pl.multiple_of(c * B, B), B)
    own = [pltpu.make_async_copy(w_hbm.at[:, pl.ds(h * C, C)], view(h, 0, 0, None, c), own_sem.at[h]) for h in (0, 1)]
    own.append(pltpu.make_async_copy(bank_hbm, bankbuf.at[mine, :], own_sem.at[2]))
    freq_copy = pltpu.make_async_copy(freq_hbm, table, own_sem.at[3])
    for cp in own:
        cp.start()

    barrier = pltpu.get_barrier_semaphore()
    peers = [chip(1, 0), chip(-1, 0), chip(0, 1), chip(0, -1), partner]
    if ny > 1:
        peers += [column(1), column(-1)]
    for p in peers:
        pl.semaphore_signal(barrier, inc=1, device_id=p, device_id_type=MESH)

    groups = [[(0, 0)], [(-1, 0), (1, 0)], [(0, -1), (0, 1)], [(2, 0)],
              [(-1, -1), (-1, 1), (1, -1), (1, 1)], [(0, 2)], [(2, -1), (2, 1)], [(-1, 2), (1, 2)], [(2, 2)]]

    tok_wait = {}
    n = 0
    for g in groups:
        for f, s in g:
            for h in (0, 1):
                dx, dz = (f, s) if h == 0 else (s, f)
                if (dx, dz) in tok_wait:
                    continue
                b = block_of(0, dx, dz)
                cp = pltpu.make_async_copy(
                    tok_hbm.at[0, :, pl.ds(pl.multiple_of(b * 2 * R, 2 * R), 2 * R)], tok.at[b], tok_sem.at[n])
                cp.start()
                tok_wait[(dx, dz)] = cp
                n += 1

    for cp in own:
        cp.wait()
    pl.semaphore_wait(barrier, len(peers))

    for h in (0, 1):
        for step in (1, -1):
            send(h, 0, 0, None, True, step, (-step, 0))
    for h in (0, 1):
        to_partner(h, 0, 0, None)
    for h in (0, 1):
        for step in (1, -1):
            send(h, 0, 0, None, False, step, (0, -step))

    swaps = []

    def swap(ref):
        cp = pltpu.make_async_remote_copy(
            src_ref=ref.at[mine, :], dst_ref=ref.at[mine, :], send_sem=xsend.at[len(swaps)],
            recv_sem=xrecv.at[len(swaps)], device_id=partner, device_id_type=MESH)
        cp.start()
        swaps.append(cp)

    swap(bankbuf)
    freq_copy.start()

    bf = jnp.bfloat16
    f32 = jnp.float32
    i32 = jnp.int32

    def onehot(a, b):
        return jnp.where(a == b, 1.0, 0.0).astype(bf)

    peers_in_pool = packed.shape[0]
    cap = packed.shape[1]

    def pack():
        n = items_ref.shape[0]
        width = counts.shape[1]
        owner = owner_ref[...]
        mark = jnp.where(lax.broadcasted_iota(i32, (width, n), 0) == owner, 1.0, 0.0)
        lowrow = lax.broadcasted_iota(i32, (n, n), 0)
        lowcol = lax.broadcasted_iota(i32, (n, n), 1)
        upper = jnp.where(lowrow < lowcol, 1.0, 0.0).astype(bf)
        ahead = jnp.dot(mark.astype(bf), upper, preferred_element_type=f32)
        before = jnp.sum(mark * ahead, axis=0, keepdims=True)
        place = owner * cap + before.astype(i32)
        spread = onehot(lax.broadcasted_iota(i32, (peers_in_pool * cap, n), 0), place)
        rows = jnp.dot(spread, items_ref[...], preferred_element_type=f32)
        packed[...] = rows.astype(bf).reshape(packed.shape)
        tally = lax.dot_general(jnp.ones((8, n), bf), mark.astype(bf), (((1,), (1,)), ((), ())), preferred_element_type=f32)
        counts[...] = tally[0:1, :]

    L = ids_ref.shape[1]
    A = table.shape[0] // 8

    def off_start():
        for g in range(ids_ref.shape[0]):
            row = ids_ref[g:g + 1, :].astype(f32)
            idx = jnp.transpose(jnp.broadcast_to(row, (L, L))).astype(i32)
            where_at[pl.ds(g * L, L), :] = idx
            line = lax.rem(idx // L, A)
            wide = jnp.concatenate([line] * (A // L), axis=1) if A > L else line[:, :A]
            pick[pl.ds(g * L, L), :] = onehot(wide, lax.broadcasted_iota(i32, (L, A), 1))

    def off_step(j):
        if j == 0:
            freq_copy.wait()
        tile = min(256, B)

        def rows_step(r, carry):
            rs = pl.ds(pl.multiple_of(r * tile, tile), tile)
            pair = jnp.concatenate([table[pl.ds(2 * j * A, A), :], table[pl.ds((2 * j + 1) * A, A), :]], axis=1)
            d = jnp.dot(pick[rs, :], pair, preferred_element_type=f32)
            part_of = where_at[rs, :] // (L * A)
            got = jnp.where(part_of == 2 * j, d[:, :L], jnp.where(part_of == 2 * j + 1, d[:, L:], 0.0))
            if j == 0:
                found[rs, :] = got
            else:
                found[rs, :] = found[rs, :] + got
            return carry

        lax.fori_loop(0, B // tile, rows_step, 0)

    def off_end():
        lane_at = lax.broadcasted_iota(i32, (B, L), 1)
        val = jnp.sum(jnp.where(lax.rem(where_at[...], L) == lane_at, found[...], 0.0), axis=1, keepdims=True)
        offb[mine, :] = jnp.broadcast_to(val * LOG2E, (B, offb.shape[1]))
        swap(offb)

    def relay(g):
        for f, s in groups[g]:
            for h in (0, 1):
                for p in pieces(f, s):
                    wait_link(h, f, s, p)
                if s == 0 and f != 2:
                    send(h, f, 0, 0 if f == -1 else 1, True, -f, (2, 0))
                if s == 0:
                    for step in (1, -1):
                        send(h, f, 0, None, False, step, (f, -step))
                elif s != 2:
                    send(h, f, s, 0 if s == -1 else 1, False, -s, (f, 2))
                for p in pieces(f, s):
                    to_partner(h, f, s, p)

    def mm(g):
        items = groups[g]
        for f, s in items:
            for h in (0, 1):
                dx, dz = (f, s) if h == 0 else (s, f)
                if (dx, dz) in tok_wait:
                    tok_wait.pop((dx, dz)).wait()
                for p in pieces(f, s):
                    wait_partner(h, f, s, p)

        def step(i, carry):
            h = lax.rem(i, 2)
            j = i // 2
            f = sum(jnp.where(j == k, fs[0], 0) for k, fs in enumerate(items))
            s = sum(jnp.where(j == k, fs[1], 0) for k, fs in enumerate(items))
            b = block_of(h, f, s)
            row = pl.multiple_of(b * (2 * R), 2 * R)
            d = jnp.dot(tok[b], wbuf[h, pl.ds(row, 2 * R), :], preferred_element_type=jnp.float32)
            if g == 0:
                acc[h] = d
            else:
                acc[h] = acc[h] + d
            return carry

        lax.fori_loop(0, 2 * len(items), step, 0)

    pack()
    mm(0)
    relay(1)
    off_start()
    relay(2)
    mm(1)
    off_step(0)
    relay(3)
    mm(2)
    off_step(1)
    mm(3)
    relay(4)
    off_step(2)
    mm(4)
    off_step(3)
    off_end()
    relay(5)
    mm(5)
    relay(6)
    mm(6)
    relay(7)
    mm(7)
    relay(8)
    mm(8)

    far = [(i, k) for i in offs for k in (0, -1, 1, 2, -2) if (i, k) != (0, 0)]

    def spot(i, k):
        return offs.index(i) * 5 + (0, -1, 1, 2, -2).index(k)

    def mirror(i, k):
        return spot(i if i == 2 else -i, -k)

    tcopies = []
    for n, (i, k) in enumerate(far):
        cp = pltpu.make_async_remote_copy(
            src_ref=pos_ref, dst_ref=tbuf.at[mirror(i, k)], send_sem=tsend.at[n], recv_sem=trecv.at[mirror(i, k)],
            device_id=chip(i, k), device_id_type=MESH)
        cp.start()
        tcopies.append(cp)

    zs = (0, -1, 1, 2)
    near = [(i, k, o) for i in offs for k in zs for o in (0, 1) if (i, k, o) != (0, 0, 0)]

    def post(i, k, o):
        return (offs.index(i) * 4 + zs.index(k)) * 2 + o

    me = (x * 4 + zl) * 2 + c
    ncopies = []
    for n, (i, k, o) in enumerate(near):
        to = chip(i, k)
        core = 1 - c if o else c
        to = to[:4] + (core,)
        owner_at = (to[2] * 4 + to[3]) * 2 + core
        slot = post(i if i == 2 else -i, k if k == 2 else -k, o)
        for src, dst, ss, rr in ((packed.at[owner_at], rows_in.at[me], nsend, nrecv), (counts, counts_in.at[me], csend, crecv)):
            cp = pltpu.make_async_remote_copy(
                src_ref=src, dst_ref=dst, send_sem=ss.at[n], recv_sem=rr.at[slot], device_id=to, device_id_type=MESH)
            cp.start()
            ncopies.append(cp)
    rows_in[me] = packed[me]
    counts_in[me] = counts[...]

    T = M // 4
    H = part.shape[1] // 2
    left, right = pl.ds(0, H), pl.ds(H, H)

    def quarter(step):
        return pl.ds(pl.multiple_of(lax.rem(y + step + 4, 4) * T, T), T)

    def partial(step):
        rs = quarter(step)
        total = None
        for h in (0, 1):
            hid = jnp.maximum(acc[h, rs, :], 0.0).astype(jnp.bfloat16)
            d = jnp.dot(hid, wo_ref[pl.ds(h * C, C), :], preferred_element_type=jnp.float32)
            total = d if total is None else total + d
        part[rs, :] = total

    ycopies = []

    def ysend_to(slot, step):
        cp = pltpu.make_async_remote_copy(
            src_ref=ysend.at[slot], dst_ref=yrecv.at[slot], send_sem=ysem.at[slot], recv_sem=yrsem.at[slot],
            device_id=column(step), device_id_type=MESH)
        cp.start()
        ycopies.append(cp)

    def ywait(slot):
        pltpu.make_async_remote_copy(
            src_ref=ysend.at[slot], dst_ref=yrecv.at[slot], send_sem=ysem.at[slot], recv_sem=yrsem.at[slot],
            device_id=partner, device_id_type=MESH).wait_recv()

    if ny > 1:
        partial(2)
        ysend[0] = part[quarter(2), left].astype(bf)
        ysend_to(0, -1)
        ysend[1] = part[quarter(2), right].astype(bf)
        ysend_to(1, 1)
        partial(-1)
        ysend[2] = part[quarter(-1), right].astype(bf)
        ysend_to(2, -1)
        partial(1)
        ysend[3] = part[quarter(1), left].astype(bf)
        ysend_to(3, 1)
        ywait(0)
        ysend[4] = (yrecv[0].astype(f32) + part[quarter(-1), left]).astype(bf)
        ysend_to(4, -1)
        ywait(1)
        ysend[5] = (yrecv[1].astype(f32) + part[quarter(1), right]).astype(bf)
        ysend_to(5, 1)
        partial(0)
        ywait(2)
        ywait(3)
        ywait(4)
        ywait(5)
        own_q = quarter(0)
        qbuf[0, :, left] = (part[own_q, left] + yrecv[3].astype(f32) + yrecv[4].astype(f32)).astype(bf)
        qbuf[0, :, right] = (part[own_q, right] + yrecv[2].astype(f32) + yrecv[5].astype(f32)).astype(bf)
    else:
        partial(0)
        qbuf[0] = part[pl.ds(0, T), :].astype(bf)

    P2 = T // 2
    P4 = T // 4

    def qview(h, f, s, piece):
        dx, dz = (f, s) if h == 0 else (s, f)
        rows = pl.ds(h * P2, P2) if piece is None else pl.ds(h * P2 + piece * P4, P4)
        return qbuf.at[offs.index(dx) * 4 + offs.index(dz), rows, :]

    qsends = []

    def qgo(h, f, s, piece, first, step, kind):
        cp = pltpu.make_async_remote_copy(
            src_ref=qview(h, f, s, piece), dst_ref=qview(h, kind[0], kind[1], piece), send_sem=qsend.at[len(qsends)],
            recv_sem=qrecv.at[key(h, kind[0], kind[1], piece)],
            device_id=along(h, first, step), device_id_type=MESH)
        cp.start()
        qsends.append(cp)

    def qwait(h, f, s, piece):
        ref = qview(h, f, s, piece)
        pltpu.make_async_remote_copy(
            src_ref=ref, dst_ref=ref, send_sem=qsend.at[0],
            recv_sem=qrecv.at[key(h, f, s, piece)], device_id=partner, device_id_type=MESH).wait_recv()

    for first in (True, False):
        for h in (0, 1):
            for step in (1, -1):
                qgo(h, 0, 0, None, first, step, (-step, 0) if first else (0, -step))

    def qrelay(g):
        for f, s in groups[g]:
            for h in (0, 1):
                for p in pieces(f, s):
                    qwait(h, f, s, p)
                if s == 0 and f != 2:
                    qgo(h, f, 0, 0 if f == -1 else 1, True, -f, (2, 0))
                if s == 0:
                    for step in (1, -1):
                        qgo(h, f, 0, None, False, step, (f, -step))
                elif s != 2:
                    qgo(h, f, s, 0 if s == -1 else 1, False, -s, (f, 2))

    for cp in swaps:
        cp.wait_recv()
    tbuf[0] = pos_ref[...]
    for i, k in far:
        pltpu.make_async_remote_copy(
            src_ref=pos_ref, dst_ref=tbuf.at[spot(i, k)], send_sem=tsend.at[0], recv_sem=trecv.at[spot(i, k)],
            device_id=partner, device_id_type=MESH).wait_recv()

    base = (x * 4 + zl) * (2 * B)
    CH = min(512, 2 * B)
    lane = lax.broadcasted_iota(jnp.int32, (1, T), 1)
    lower = lax.rem(lane, P2) < P4
    sub = lax.broadcasted_iota(jnp.int32, (8, T), 0)
    W = sbuf.shape[2]
    scopies = []

    def block(dx, dz):
        slot = offs.index(dx) * 4 + offs.index(dz)
        qt[...] = jnp.transpose(qbuf[slot])
        if dz == 2:
            target = jnp.where(lower, tbuf[spot(dx, -2)], tbuf[spot(dx, 2)])
        else:
            target = tbuf[spot(dx, dz)]
        t = jnp.broadcast_to(target - base, (8, T))
        group = lax.shift_right_arithmetic(t, 3)

        def chunk(k, carry):
            m, total, hit = carry
            rows = pl.ds(pl.multiple_of(k * CH, CH), CH)
            prod = jnp.dot(bankbuf[rows, :], qt[...], preferred_element_type=f32)
            off = offb[rows, :]
            if T > off.shape[1]:
                off = jnp.concatenate([off] * (T // off.shape[1]), axis=1)
            logit = (prod * (5.0 * LOG2E) - off).reshape(CH // 8, 8, T)
            top = jnp.maximum(m, jnp.max(logit, axis=0))
            here = group - k * (CH // 8)
            for r in range(CH // 8):
                hit = jnp.where(here == r, logit[r], hit)
            total = total * jnp.exp2(m - top) + jnp.sum(jnp.exp2(logit - top[None]), axis=0)
            return top, total, hit

        zero = jnp.zeros((8, T), f32)
        m, total, hit = lax.fori_loop(0, 2 * B // CH, chunk, (jnp.full((8, T), -jnp.inf, f32), zero, zero))
        top = jnp.max(m, axis=0, keepdims=True)
        total = jnp.sum(total * jnp.exp2(m - top), axis=0, keepdims=True)
        score = jnp.sum(jnp.where(jnp.bitwise_and(t, 7) == sub, hit, 0.0), axis=0, keepdims=True)
        for n, v in enumerate((top, total, score)):
            for k in range(2):
                sbuf[slot, pl.ds(n * 2 + k, 1), :] = v[:, k * W:(k + 1) * W]
        for k in ((dz,) if dz != 2 else (2, -2)):
            if (dx, k) == (0, 0):
                continue
            cp = pltpu.make_async_remote_copy(
                src_ref=sbuf.at[slot], dst_ref=stats.at[mirror(dx, k)], send_sem=ssend.at[len(scopies)],
                recv_sem=srecv.at[mirror(dx, k)], device_id=chip(dx, k), device_id_type=MESH)
            cp.start()
            scopies.append(cp)

    block(0, 0)
    qrelay(1)
    qrelay(2)
    for dx, dz in ((-1, 0), (1, 0), (0, -1), (0, 1)):
        block(dx, dz)
    qrelay(3)
    qrelay(4)
    for dx, dz in ((-1, -1), (-1, 1), (1, -1), (1, 1)):
        block(dx, dz)
    qrelay(5)
    block(2, 0)
    block(0, 2)
    qrelay(6)
    qrelay(7)
    for dx, dz in ((2, -1), (2, 1), (-1, 2), (1, 2)):
        block(dx, dz)
    qrelay(8)
    block(2, 2)

    for i, k, o in near:
        n = post(i, k, o)
        for src, ref, ss, rr in ((packed, rows_in, nsend, nrecv), (None, counts_in, csend, crecv)):
            pltpu.make_async_remote_copy(
                src_ref=ref.at[0], dst_ref=ref.at[0], send_sem=ss.at[0], recv_sem=rr.at[n],
                device_id=partner, device_id_type=MESH).wait_recv()
    J = peers_in_pool * cap
    width = counts.shape[1]
    every = counts_in[...].reshape(peers_in_pool, width)
    mine_only = jnp.where(lax.broadcasted_iota(i32, every.shape, 1) == me, every, 0.0)
    count = jnp.sum(mine_only, axis=1, keepdims=True)
    source = lax.broadcasted_iota(i32, (peers_in_pool, J), 0)
    column_of = lax.broadcasted_iota(i32, (peers_in_pool, J), 1) // cap
    valid = jnp.sum(jnp.where(source == column_of, count, 0.0), axis=0, keepdims=True)
    ahead = jnp.sum(jnp.where(source < column_of, count, 0.0), axis=0, keepdims=True)
    nth = lax.rem(lax.broadcasted_iota(i32, (1, J), 1), cap)
    slot_of = lax.rem(head_ref[0] + ahead.astype(i32) + nth, B)
    slot_of = jnp.where(nth < valid.astype(i32), slot_of, -1)
    tile = min(256, B)

    def write(r, carry):
        first = pl.multiple_of(r * tile, tile)
        spread = onehot(lax.broadcasted_iota(i32, (tile, J), 0) + first, slot_of)
        fresh = jnp.dot(spread, rows_in[...].reshape(J, rows_in.shape[2]), preferred_element_type=f32)
        hits = jnp.dot(spread, jnp.ones((J, rows_in.shape[2]), bf), preferred_element_type=f32)
        old = bankbuf[pl.ds(pl.multiple_of(c * B + first, tile), tile), :]
        newbank_ref[pl.ds(first, tile), :] = jnp.where(hits > 0.5, fresh, old.astype(f32)).astype(bf)
        return carry

    lax.fori_loop(0, B // tile, write, 0)

    stats[0] = sbuf[0]
    for i, k in far:
        pltpu.make_async_remote_copy(
            src_ref=sbuf.at[0], dst_ref=stats.at[spot(i, k)], send_sem=ssend.at[0], recv_sem=srecv.at[spot(i, k)],
            device_id=partner, device_id_type=MESH).wait_recv()
    low = lax.broadcasted_iota(jnp.int32, (8, W), 1) < P4
    parts = []
    for i in offs:
        for k in (0, -1, 1):
            st = stats[spot(i, k)]
            parts.append((st[0:2], st[2:4], st[4:6]))
        st = jnp.where(low, stats[spot(i, 2)], stats[spot(i, -2)])
        parts.append((st[0:2], st[2:4], st[4:6]))
    top = functools.reduce(jnp.maximum, [p[0] for p in parts])
    total = sum(p[1] * jnp.exp2(p[0] - top) for p in parts)
    score = sum(p[2] for p in parts)
    loss = LN2 * (top - score) + jnp.log(total)
    for k in range(2):
        out_ref[:, k * W:(k + 1) * W] = loss[k:k + 1, :]

    for cp in sends + psends + swaps + tcopies + ncopies + ycopies + qsends + scopies:
        cp.wait_send()


def tower(tokens, w_hidden, w_out, bank, log_freq, item_ids, positives, new_items, new_owner, queue_head):
    M, K = tokens.shape[1:]
    R, N = w_hidden.shape
    E = w_out.shape[1]
    B = bank.shape[0]
    T = M // 4
    L = item_ids.shape[1]
    pool = K // R
    cap = 2 * new_items.shape[0] // pool
    anywhere = pl.BlockSpec(memory_space=pl.ANY)
    vmem = pl.BlockSpec(memory_space=pltpu.VMEM)
    dma = pltpu.SemaphoreType.DMA
    return pl.pallas_call(
        tower_kernel,
        out_shape=(jax.ShapeDtypeStruct((1, T), jnp.float32), jax.ShapeDtypeStruct((B, E), jnp.bfloat16)),
        in_specs=[anywhere, anywhere, vmem, anywhere, anywhere, vmem, vmem, vmem, vmem,
                  pl.BlockSpec(memory_space=pltpu.SMEM)],
        out_specs=(vmem, vmem),
        scratch_shapes=[
            pltpu.VMEM((16, M, 2 * R), jnp.bfloat16),
            pltpu.VMEM((2, K, N // 2), jnp.bfloat16),
            pltpu.VMEM((2, M, N // 2), jnp.float32),
            pltpu.VMEM((M, E), jnp.float32),
            pltpu.VMEM((6, T, E // 2), jnp.bfloat16),
            pltpu.VMEM((6, T, E // 2), jnp.bfloat16),
            pltpu.VMEM((2 * B, E), jnp.bfloat16),
            pltpu.VMEM((2 * B, T // 2), jnp.float32),
            pltpu.VMEM((16, T, E), jnp.bfloat16),
            pltpu.VMEM((E, T), jnp.bfloat16),
            pltpu.VMEM((20, 1, T), jnp.int32),
            pltpu.VMEM((16, 8, T // 2), jnp.float32),
            pltpu.VMEM((20, 8, T // 2), jnp.float32),
            pltpu.VMEM(log_freq.shape, jnp.bfloat16),
            pltpu.VMEM((B, log_freq.shape[0] // 8), jnp.bfloat16),
            pltpu.VMEM((B, L), jnp.int32),
            pltpu.VMEM((B, L), jnp.float32),
            pltpu.VMEM((pool, cap, E), jnp.bfloat16),
            pltpu.VMEM((1, 128), jnp.float32),
            pltpu.VMEM((pool, cap, E), jnp.bfloat16),
            pltpu.VMEM((pool, 1, 128), jnp.float32),
            dma((16,)), dma((4,)), dma((40,)), dma((64,)), dma((64,)), dma((64,)),
            dma((2,)), dma((2,)), dma((6,)), dma((6,)), dma((40,)), dma((64,)),
            dma((19,)), dma((20,)), dma((19,)), dma((20,)), dma((31,)), dma((32,)), dma((31,)), dma((32,)),
        ],
        compiler_params=pltpu.CompilerParams(collective_id=0, has_side_effects=True, vmem_limit_bytes=56 * 1024 * 1024),
        name="tower",
    )(tokens, w_hidden, w_out, bank, log_freq, item_ids, positives, new_items, new_owner, queue_head)


def body(
    tokens, w_hidden, w_out, bank, item_ids, log_freq, positives, new_items, new_owner, queue_head
):
    return tower(
        tokens, w_hidden, w_out, bank, log_freq.reshape(-1, 128), item_ids.reshape(-1, 128),
        positives, new_items, new_owner.reshape(1, -1), queue_head,
    )


def solution(mesh):
    finer = Mesh(
        mesh.devices.reshape(mesh.shape["dp"], mesh.shape["tensor"], 4, 4, 2),
        ("dp", "tensor", "pool_0", "pool_1", "pool_2"),
    )
    in_specs = (
        P(DP_POOL, None, None),
        P(POOL, "tensor"),
        P("tensor", None),
        P(POOL, None),
        P(POOL),
        P(),
        P(DP_POOL, "tensor"),
        P(POOL, None),
        P(POOL, None),
        P(POOL),
    )
    out_specs = (P(DP_POOL, "tensor"), P(POOL, None))
    return jax.shard_map(body, mesh=finer, in_specs=in_specs, out_specs=out_specs, check_vma=False)
```

```python
import functools
import jax
import jax.numpy as jnp
from jax import lax
from jax.experimental import pallas as pl
from jax.experimental.pallas import tpu as pltpu

AXES = ("dp", "tensor", "pool_0", "pool_1", "pool_2")
from jax.sharding import Mesh
from jax.sharding import PartitionSpec as P

MESH = pl.DeviceIdType.MESH
POOL = ("pool_0", "pool_1", "pool_2")
DP_POOL = ("dp", "pool_0", "pool_1", "pool_2")


LOG2E = 1.4426950408889634
LN2 = 0.6931471805599453
SCALE = 5.0 * LOG2E


def tower_kernel(tok_hbm, w_hbm, wo_ref, bank_hbm, freq_hbm, ids_ref, pos_ref, items_ref,
                 owner_ref, head_ref, out_ref, newbank_ref, tok, wbuf, acc, part, ysend, yrecv,
                 bankbuf, offb, qbuf, qt, tbuf, sbuf, stats, table, pick, where_at, found, packed, counts, rows_in, counts_in, tok_sem, own_sem, send_sem, recv_sem, psend, precv,
                 xsend, xrecv, ysem, yrsem, qsend, qrecv, tsend, trecv, ssend, srecv,
                 nsend, nrecv, csend, crecv, osend, orecv):
    dp, y, x, zl, c = (lax.axis_index(a) for a in AXES)
    ny = lax.axis_size("tensor")
    pz = dp * 4 + zl
    R = w_hbm.shape[0]
    C = w_hbm.shape[1] // 2
    Q = C // 2
    M = tok.shape[1]
    offs = (0, -1, 1, 2)

    def chip(dx, dz):
        xx = lax.rem(x + dx + 4, 4)
        zz = lax.rem(pz + dz + 8, 8)
        return (zz // 4, y, xx, lax.rem(zz, 4), c)

    def along(h, first, step):
        return chip(step, 0) if (h == 0) == first else chip(0, step)

    partner = (dp, y, x, zl, 1 - c)

    def arrived(ref, sem):
        pltpu.make_async_remote_copy(
            src_ref=ref, dst_ref=ref, send_sem=send_sem.at[0], recv_sem=sem,
            device_id=partner, device_id_type=MESH).wait_recv()

    def sent(ref, sem):
        pltpu.make_async_remote_copy(
            src_ref=ref, dst_ref=ref, send_sem=sem, recv_sem=recv_sem.at[0],
            device_id=partner, device_id_type=MESH).wait_send()

    def column(step):
        return (dp, lax.rem(y + step + ny, ny), x, zl, c)

    def block_of(h, f, s):
        dx = f * (1 - h) + s * h
        dz = s * (1 - h) + f * h
        return lax.rem(x + dx + 4, 4) * 4 + lax.rem(zl + dz + 4, 4)

    def view(h, f, s, piece, core):
        row = pl.multiple_of(block_of(h, f, s) * (2 * R) + core * R, R)
        cols = slice(None) if piece is None else pl.ds(piece * Q, Q)
        return wbuf.at[h, pl.ds(row, R), cols]

    def key(h, f, s, piece):
        return ((h * 4 + offs.index(f)) * 4 + offs.index(s)) * 2 + (piece or 0)

    sends = []

    def send(h, f, s, piece, first, step, kind):
        nf, ns = kind
        ref = view(h, f, s, piece, c)
        cp = pltpu.make_async_remote_copy(
            src_ref=ref, dst_ref=ref, send_sem=send_sem.at[0],
            recv_sem=recv_sem.at[key(h, nf, ns, piece)],
            device_id=along(h, first, step), device_id_type=MESH)
        cp.start()
        sends.append(cp)

    psends = []

    def to_partner(h, f, s, piece):
        ref = view(h, f, s, piece, c)
        cp = pltpu.make_async_remote_copy(
            src_ref=ref, dst_ref=ref, send_sem=psend.at[0],
            recv_sem=precv.at[key(h, f, s, piece)], device_id=partner, device_id_type=MESH)
        cp.start()
        psends.append(cp)

    def wait_link(h, f, s, piece):
        ref = view(h, f, s, piece, c)
        pltpu.make_async_remote_copy(
            src_ref=ref, dst_ref=ref, send_sem=send_sem.at[0],
            recv_sem=recv_sem.at[key(h, f, s, piece)], device_id=partner, device_id_type=MESH).wait_recv()

    def wait_partner(h, f, s, piece):
        ref = view(h, f, s, piece, 1 - c)
        pltpu.make_async_remote_copy(
            src_ref=ref, dst_ref=ref, send_sem=send_sem.at[0],
            recv_sem=precv.at[key(h, f, s, piece)], device_id=partner, device_id_type=MESH).wait_recv()

    def pieces(f, s):
        return (0, 1) if (f == 2 and s == 0) or s == 2 else (None,)

    B = bank_hbm.shape[0]
    mine = pl.ds(pl.multiple_of(c * B, B), B)
    own = [pltpu.make_async_copy(w_hbm.at[:, pl.ds(h * C, C)], view(h, 0, 0, None, c), own_sem.at[h]) for h in (0, 1)]
    own.append(pltpu.make_async_copy(bank_hbm, bankbuf.at[mine, :], own_sem.at[2]))
    freq_copy = pltpu.make_async_copy(freq_hbm, table, own_sem.at[3])
    for cp in own:
        cp.start()

    barrier = pltpu.get_barrier_semaphore()
    peers = [chip(1, 0), chip(-1, 0), chip(0, 1), chip(0, -1), partner]
    if ny > 1:
        peers += [column(step) for step in range(1, ny)]
    for p in peers:
        pl.semaphore_signal(barrier, inc=1, device_id=p, device_id_type=MESH)

    groups = [[(0, 0)], [(-1, 0), (1, 0)], [(0, -1), (0, 1)], [(2, 0)],
              [(-1, -1), (-1, 1)], [(1, -1), (1, 1)], [(0, 2)], [(2, -1), (2, 1)], [(-1, 2), (1, 2)], [(2, 2)]]

    tok_wait = {}
    n = 0
    for g in groups:
        for f, s in g:
            for h in (0, 1):
                dx, dz = (f, s) if h == 0 else (s, f)
                if (dx, dz) in tok_wait:
                    continue
                b = block_of(0, dx, dz)
                cp = pltpu.make_async_copy(
                    tok_hbm.at[0, :, pl.ds(pl.multiple_of(b * 2 * R, 2 * R), 2 * R)], tok.at[b], tok_sem.at[n])
                cp.start()
                tok_wait[(dx, dz)] = cp
                n += 1

    for cp in own:
        cp.wait()
    pl.semaphore_wait(barrier, len(peers))

    for h in (0, 1):
        to_partner(h, 0, 0, None)
    for h in (0, 1):
        for step in (1, -1):
            send(h, 0, 0, None, True, step, (-step, 0))
    for h in (0, 1):
        for step in (1, -1):
            send(h, 0, 0, None, False, step, (0, -step))

    swaps = []

    def swap(ref):
        cp = pltpu.make_async_remote_copy(
            src_ref=ref.at[mine, :], dst_ref=ref.at[mine, :], send_sem=xsend.at[len(swaps)],
            recv_sem=xrecv.at[len(swaps)], device_id=partner, device_id_type=MESH)
        cp.start()
        swaps.append(cp)

    swap(bankbuf)
    freq_copy.start()

    bf = jnp.bfloat16
    f32 = jnp.float32
    i32 = jnp.int32

    def onehot(a, b):
        return jnp.where(a == b, 1.0, 0.0).astype(bf)

    peers_in_pool = packed.shape[0]
    cap = packed.shape[1]

    def pack():
        n = items_ref.shape[0]
        width = counts.shape[1]
        owner = owner_ref[...]
        mark = jnp.where(lax.broadcasted_iota(i32, (width, n), 0) == owner, 1.0, 0.0)
        lowrow = lax.broadcasted_iota(i32, (n, n), 0)
        lowcol = lax.broadcasted_iota(i32, (n, n), 1)
        upper = jnp.where(lowrow < lowcol, 1.0, 0.0).astype(bf)
        ahead = jnp.dot(mark.astype(bf), upper, preferred_element_type=f32)
        before = jnp.sum(mark * ahead, axis=0, keepdims=True)
        place = owner * cap + before.astype(i32)
        spread = onehot(lax.broadcasted_iota(i32, (peers_in_pool * cap, n), 0), place)
        rows = jnp.dot(spread, items_ref[...], preferred_element_type=f32)
        packed[...] = rows.astype(bf).reshape(packed.shape)
        tally = lax.dot_general(jnp.ones((8, n), bf), mark.astype(bf), (((1,), (1,)), ((), ())), preferred_element_type=f32)
        counts[...] = tally[0:1, :]

    L = ids_ref.shape[1]
    A = table.shape[0] // 8

    G = ids_ref.shape[0] // ny
    OR = B // ny
    here_rows = pl.ds(pl.multiple_of(c * B + y * OR, OR), OR)

    def off_start():
        for g in range(G):
            row = ids_ref[pl.ds(y * G + g, 1), :].astype(f32)
            idx = jnp.transpose(jnp.broadcast_to(row, (L, L))).astype(i32)
            where_at[pl.ds(g * L, L), :] = idx
            line = lax.rem(idx // L, A)
            wide = jnp.concatenate([line] * (A // L), axis=1) if A > L else line[:, :A]
            pick[pl.ds(g * L, L), :] = onehot(wide, lax.broadcasted_iota(i32, (L, A), 1))

    def off_step(j):
        if j == 0:
            freq_copy.wait()
        tile = min(256, OR)

        def rows_step(r, carry):
            rs = pl.ds(pl.multiple_of(r * tile, tile), tile)
            pair = jnp.concatenate([table[pl.ds(2 * j * A, A), :], table[pl.ds((2 * j + 1) * A, A), :]], axis=1)
            d = jnp.dot(pick[rs, :], pair, preferred_element_type=f32)
            part_of = where_at[rs, :] // (L * A)
            got = jnp.where(part_of == 2 * j, d[:, :L], jnp.where(part_of == 2 * j + 1, d[:, L:], 0.0))
            if j == 0:
                found[rs, :] = got
            else:
                found[rs, :] = found[rs, :] + got
            return carry

        lax.fori_loop(0, OR // tile, rows_step, 0)

    def off_end():
        lane_at = lax.broadcasted_iota(i32, (OR, L), 1)
        val = jnp.sum(jnp.where(lax.rem(where_at[...], L) == lane_at, found[...], 0.0), axis=1, keepdims=True)
        offb[here_rows, :] = jnp.broadcast_to(val * LOG2E, (OR, offb.shape[1]))
        for step in range(1, ny):
            pltpu.make_async_remote_copy(
                src_ref=offb.at[here_rows, :], dst_ref=offb.at[here_rows, :], send_sem=osend.at[0],
                recv_sem=orecv.at[0], device_id=column(step), device_id_type=MESH).start()

    def off_collect():
        if ny > 1:
            arrived(offb.at[pl.ds(0, (ny - 1) * OR), :], orecv.at[0])
        swap(offb)

    def relay(g):
        for f, s in groups[g]:
            for h in (0, 1):
                for p in pieces(f, s):
                    wait_link(h, f, s, p)
                for p in pieces(f, s):
                    to_partner(h, f, s, p)
                if s == 0 and f != 2:
                    send(h, f, 0, 0 if f == -1 else 1, True, -f, (2, 0))
                if s == 0:
                    for step in (1, -1):
                        send(h, f, 0, None, False, step, (f, -step))
                elif s != 2:
                    send(h, f, s, 0 if s == -1 else 1, False, -s, (f, 2))

    def mm(g):
        items = groups[g]
        for f, s in items:
            for h in (0, 1):
                dx, dz = (f, s) if h == 0 else (s, f)
                if (dx, dz) in tok_wait:
                    tok_wait.pop((dx, dz)).wait()
                for p in pieces(f, s):
                    wait_partner(h, f, s, p)

        def step(i, carry):
            h = lax.rem(i, 2)
            j = i // 2
            f = sum(jnp.where(j == k, fs[0], 0) for k, fs in enumerate(items))
            s = sum(jnp.where(j == k, fs[1], 0) for k, fs in enumerate(items))
            b = block_of(h, f, s)
            row = pl.multiple_of(b * (2 * R), 2 * R)
            d = jnp.dot(tok[b], wbuf[h, pl.ds(row, 2 * R), :], preferred_element_type=jnp.float32)
            if g == 0:
                acc[h] = d
            else:
                acc[h] = acc[h] + d
            return carry

        lax.fori_loop(0, 2 * len(items), step, 0)

    pack()
    mm(0)
    off_start()
    relay(1)
    off_step(0)
    off_step(1)
    relay(2)
    mm(1)
    off_step(2)
    off_step(3)
    off_end()
    relay(3)
    mm(2)
    relay(4)
    mm(3)
    relay(5)
    mm(4)
    relay(6)
    mm(5)
    relay(7)
    mm(6)
    off_collect()
    relay(8)
    mm(7)
    relay(9)
    mm(8)
    mm(9)

    far = [(i, k) for i in offs for k in (0, -1, 1, 2, -2) if (i, k) != (0, 0)]

    def spot(i, k):
        return offs.index(i) * 5 + (0, -1, 1, 2, -2).index(k)

    def mirror(i, k):
        return spot(i if i == 2 else -i, -k)

    tcopies = []
    for n, (i, k) in enumerate(far):
        cp = pltpu.make_async_remote_copy(
            src_ref=pos_ref, dst_ref=tbuf.at[mirror(i, k)], send_sem=tsend.at[0], recv_sem=trecv.at[0],
            device_id=chip(i, k), device_id_type=MESH)
        cp.start()
        tcopies.append(cp)

    zs = (0, -1, 1, 2)
    near = [(i, k, o) for i in offs for k in zs for o in (0, 1) if (i, k, o) != (0, 0, 0)]

    me = (x * 4 + zl) * 2 + c
    ncopies = []
    for n, (i, k, o) in enumerate(near):
        to = chip(i, k)
        core = 1 - c if o else c
        to = to[:4] + (core,)
        owner_at = (to[2] * 4 + to[3]) * 2 + core
        for src, dst, ss, rr in ((packed.at[owner_at], rows_in.at[me], nsend, nrecv), (counts, counts_in.at[me], csend, crecv)):
            cp = pltpu.make_async_remote_copy(
                src_ref=src, dst_ref=dst, send_sem=ss.at[0], recv_sem=rr.at[0], device_id=to, device_id_type=MESH)
            cp.start()
            ncopies.append(cp)
    rows_in[me] = packed[me]
    counts_in[me] = counts[...]

    T = M // 4
    H = part.shape[1] // 2
    left, right = pl.ds(0, H), pl.ds(H, H)

    def quarter(step):
        return pl.ds(pl.multiple_of(lax.rem(y + step + 4, 4) * T, T), T)

    def partial(step):
        rs = quarter(step)
        total = None
        for h in (0, 1):
            hid = jnp.maximum(acc[h, rs, :], 0.0).astype(jnp.bfloat16)
            d = jnp.dot(hid, wo_ref[pl.ds(h * C, C), :], preferred_element_type=jnp.float32)
            total = d if total is None else total + d
        part[rs, :] = total

    ycopies = []

    def ysend_to(slot, step):
        cp = pltpu.make_async_remote_copy(
            src_ref=ysend.at[slot], dst_ref=yrecv.at[slot], send_sem=ysem.at[0], recv_sem=yrsem.at[slot],
            device_id=column(step), device_id_type=MESH)
        cp.start()
        ycopies.append(cp)

    def ywait(slot):
        pltpu.make_async_remote_copy(
            src_ref=ysend.at[slot], dst_ref=yrecv.at[slot], send_sem=ysem.at[0], recv_sem=yrsem.at[slot],
            device_id=partner, device_id_type=MESH).wait_recv()

    if ny > 1:
        partial(2)
        ysend[0] = part[quarter(2), left].astype(bf)
        ysend_to(0, -1)
        ysend[1] = part[quarter(2), right].astype(bf)
        ysend_to(1, 1)
        partial(-1)
        ysend[2] = part[quarter(-1), right].astype(bf)
        ysend_to(2, -1)
        partial(1)
        ysend[3] = part[quarter(1), left].astype(bf)
        ysend_to(3, 1)
        ywait(0)
        ysend[4] = (yrecv[0].astype(f32) + part[quarter(-1), left]).astype(bf)
        ysend_to(4, -1)
        ywait(1)
        ysend[5] = (yrecv[1].astype(f32) + part[quarter(1), right]).astype(bf)
        ysend_to(5, 1)
        partial(0)
        ywait(2)
        ywait(3)
        ywait(4)
        ywait(5)
        own_q = quarter(0)
        qbuf[0, :, left] = ((part[own_q, left] + yrecv[3].astype(f32) + yrecv[4].astype(f32)) * SCALE).astype(bf)
        qbuf[0, :, right] = ((part[own_q, right] + yrecv[2].astype(f32) + yrecv[5].astype(f32)) * SCALE).astype(bf)
    else:
        partial(0)
        qbuf[0] = (part[pl.ds(0, T), :] * SCALE).astype(bf)

    P2 = T // 2
    P4 = T // 4

    def qview(h, f, s, piece):
        dx, dz = (f, s) if h == 0 else (s, f)
        rows = pl.ds(h * P2, P2) if piece is None else pl.ds(h * P2 + piece * P4, P4)
        return qbuf.at[offs.index(dx) * 4 + offs.index(dz), rows, :]

    qsends = []

    def qgo(h, f, s, piece, first, step, kind):
        cp = pltpu.make_async_remote_copy(
            src_ref=qview(h, f, s, piece), dst_ref=qview(h, kind[0], kind[1], piece), send_sem=qsend.at[0],
            recv_sem=qrecv.at[key(h, kind[0], kind[1], piece)],
            device_id=along(h, first, step), device_id_type=MESH)
        cp.start()
        qsends.append(cp)

    def qwait(h, f, s, piece):
        ref = qview(h, f, s, piece)
        pltpu.make_async_remote_copy(
            src_ref=ref, dst_ref=ref, send_sem=qsend.at[0],
            recv_sem=qrecv.at[key(h, f, s, piece)], device_id=partner, device_id_type=MESH).wait_recv()

    for first in (True, False):
        for h in (0, 1):
            for step in (1, -1):
                qgo(h, 0, 0, None, first, step, (-step, 0) if first else (0, -step))

    def qrelay(g):
        for f, s in groups[g]:
            for h in (0, 1):
                for p in pieces(f, s):
                    qwait(h, f, s, p)
                if s == 0 and f != 2:
                    qgo(h, f, 0, 0 if f == -1 else 1, True, -f, (2, 0))
                if s == 0:
                    for step in (1, -1):
                        qgo(h, f, 0, None, False, step, (f, -step))
                elif s != 2:
                    qgo(h, f, s, 0 if s == -1 else 1, False, -s, (f, 2))

    for cp in swaps:
        cp.wait_recv()
    tbuf[0] = pos_ref[...]
    arrived(tbuf.at[pl.ds(1, len(far))], trecv.at[0])

    base = (x * 4 + zl) * (2 * B)
    CH = min(512, 2 * B)
    lane = lax.broadcasted_iota(jnp.int32, (1, T), 1)
    lower = lax.rem(lane, P2) < P4
    sub = lax.broadcasted_iota(jnp.int32, (8, T), 0)
    W = sbuf.shape[2]

    SUB = min(64, CH)
    G8 = SUB // 8
    levels = G8.bit_length() - 1

    def pick_of(values, i):
        return sum(jnp.where(i == k, v, 0) for k, v in enumerate(values))

    def blocks(items):
        def one(i, carry):
            dx = pick_of([a for a, _ in items], i)
            dz = pick_of([b for _, b in items], i)
            ix = jnp.where(dx == -1, 1, jnp.where(dx == 1, 2, jnp.where(dx == 2, 3, 0)))
            iz = jnp.where(dz == -1, 1, jnp.where(dz == 1, 2, jnp.where(dz == 2, 3, 0)))
            slot = ix * 4 + iz
            qt[...] = jnp.transpose(qbuf[slot])
            target = tbuf[ix * 5 + iz]
            target = jnp.where(jnp.logical_and(lower, jnp.broadcast_to(iz, lower.shape) == 3), tbuf[ix * 5 + 4], target)
            t = jnp.broadcast_to(target - base, (8, T))
            group = lax.shift_right_arithmetic(t, 3)
            bits = [jnp.bitwise_and(lax.shift_right_arithmetic(group, b), 1) == 1 for b in range(levels)]
            which = lax.shift_right_arithmetic(group, levels)
            m = total = None
            hit = jnp.zeros((8, T), f32)
            for k in range(2 * B // CH):
                rows = pl.ds(k * CH, CH)
                prod = jnp.dot(bankbuf[rows, :], qt[...], preferred_element_type=f32)
                off = offb[rows, :]
                if T > off.shape[1]:
                    off = jnp.concatenate([off] * (T // off.shape[1]), axis=1)
                every_logit = (prod - off).reshape(CH // SUB, G8, 8, T)
                for u in range(CH // SUB):
                    logit = every_logit[u]
                    high = jnp.max(logit, axis=0)
                    top = high if m is None else jnp.maximum(m, high)
                    chosen = [logit[r] for r in range(G8)]
                    for b in range(levels):
                        chosen = [jnp.where(bits[b], chosen[2 * r + 1], chosen[2 * r]) for r in range(len(chosen) // 2)]
                    hit = jnp.where(which == k * (CH // SUB) + u, chosen[0], hit)
                    gain = jnp.sum(jnp.exp2(logit - top[None]), axis=0)
                    total = gain if m is None else total * jnp.exp2(m - top) + gain
                    m = top
            top = jnp.max(m, axis=0, keepdims=True)
            total = jnp.sum(total * jnp.exp2(m - top), axis=0, keepdims=True)
            score = jnp.sum(jnp.where(jnp.bitwise_and(t, 7) == sub, hit, 0.0), axis=0, keepdims=True)
            for n, v in enumerate((top, total, score)):
                for k in range(2):
                    sbuf[slot, pl.ds(n * 2 + k, 1), :] = v[:, k * W:(k + 1) * W]
            return carry

        if len(items) == 1:
            one(0, 0)
        else:
            lax.fori_loop(0, len(items), one, 0)
        for dx, dz in items:
            for k in ((dz,) if dz != 2 else (2, -2)):
                if (dx, k) == (0, 0):
                    continue
                cp = pltpu.make_async_remote_copy(
                    src_ref=sbuf.at[offs.index(dx) * 4 + offs.index(dz)], dst_ref=stats.at[mirror(dx, k)],
                    send_sem=ssend.at[0], recv_sem=srecv.at[0], device_id=chip(dx, k), device_id_type=MESH)
                cp.start()

    blocks([(0, 0)])
    qrelay(1)
    qrelay(2)
    blocks([(-1, 0), (1, 0), (0, -1), (0, 1)])
    qrelay(3)
    qrelay(4)
    qrelay(5)
    blocks([(-1, -1), (-1, 1), (1, -1), (1, 1)])
    qrelay(6)
    blocks([(2, 0), (0, 2)])
    qrelay(7)
    qrelay(8)
    blocks([(2, -1), (2, 1), (-1, 2), (1, 2)])
    qrelay(9)
    blocks([(2, 2)])

    arrived(rows_in.at[pl.ds(0, len(near))], nrecv.at[0])
    arrived(counts_in.at[pl.ds(0, len(near))], crecv.at[0])
    J = peers_in_pool * cap
    width = counts.shape[1]
    every = counts_in[...].reshape(peers_in_pool, width)
    mine_only = jnp.where(lax.broadcasted_iota(i32, every.shape, 1) == me, every, 0.0)
    count = jnp.sum(mine_only, axis=1, keepdims=True)
    source = lax.broadcasted_iota(i32, (peers_in_pool, J), 0)
    column_of = lax.broadcasted_iota(i32, (peers_in_pool, J), 1) // cap
    valid = jnp.sum(jnp.where(source == column_of, count, 0.0), axis=0, keepdims=True)
    ahead = jnp.sum(jnp.where(source < column_of, count, 0.0), axis=0, keepdims=True)
    nth = lax.rem(lax.broadcasted_iota(i32, (1, J), 1), cap)
    slot_of = lax.rem(head_ref[0] + ahead.astype(i32) + nth, B)
    slot_of = jnp.where(nth < valid.astype(i32), slot_of, -1)
    tile = min(256, B)

    def write(r, carry):
        first = pl.multiple_of(r * tile, tile)
        spread = onehot(lax.broadcasted_iota(i32, (tile, J), 0) + first, slot_of)
        fresh = jnp.dot(spread, rows_in[...].reshape(J, rows_in.shape[2]), preferred_element_type=f32)
        hits = jnp.dot(spread, jnp.ones((J, rows_in.shape[2]), bf), preferred_element_type=f32)
        old = bankbuf[pl.ds(pl.multiple_of(c * B + first, tile), tile), :]
        newbank_ref[pl.ds(first, tile), :] = jnp.where(hits > 0.5, fresh, old.astype(f32)).astype(bf)
        return carry

    lax.fori_loop(0, B // tile, write, 0)

    stats[0] = sbuf[0]
    arrived(stats.at[pl.ds(1, len(far))], srecv.at[0])
    low = lax.broadcasted_iota(jnp.int32, (8, W), 1) < P4
    parts = []
    for i in offs:
        for k in (0, -1, 1):
            st = stats[spot(i, k)]
            parts.append((st[0:2], st[2:4], st[4:6]))
        st = jnp.where(low, stats[spot(i, 2)], stats[spot(i, -2)])
        parts.append((st[0:2], st[2:4], st[4:6]))
    top = functools.reduce(jnp.maximum, [p[0] for p in parts])
    total = sum(p[1] * jnp.exp2(p[0] - top) for p in parts)
    score = sum(p[2] for p in parts)
    loss = LN2 * (top - score) + jnp.log(total)
    for k in range(2):
        out_ref[:, k * W:(k + 1) * W] = loss[k:k + 1, :]

    sent(wbuf.at[0, pl.ds(0, 30 * R), :], send_sem.at[0])
    sent(wbuf.at[0], psend.at[0])
    sent(tbuf.at[pl.ds(1, len(far))], tsend.at[0])
    sent(rows_in.at[pl.ds(0, len(near))], nsend.at[0])
    sent(counts_in.at[pl.ds(0, len(near))], csend.at[0])
    sent(qbuf.at[pl.ds(0, 15)], qsend.at[0])
    sent(stats.at[pl.ds(1, len(far))], ssend.at[0])
    for cp in swaps:
        cp.wait_send()
    if ny > 1:
        sent(ysend, ysem.at[0])
        sent(offb.at[pl.ds(0, (ny - 1) * OR), :], osend.at[0])


def tower(tokens, w_hidden, w_out, bank, log_freq, item_ids, positives, new_items, new_owner, queue_head):
    M, K = tokens.shape[1:]
    R, N = w_hidden.shape
    E = w_out.shape[1]
    B = bank.shape[0]
    T = M // 4
    L = item_ids.shape[1]
    pool = K // R
    OR = B // lax.axis_size("tensor")
    cap = 2 * new_items.shape[0] // pool
    anywhere = pl.BlockSpec(memory_space=pl.ANY)
    vmem = pl.BlockSpec(memory_space=pltpu.VMEM)
    dma = pltpu.SemaphoreType.DMA
    return pl.pallas_call(
        tower_kernel,
        out_shape=(jax.ShapeDtypeStruct((1, T), jnp.float32), jax.ShapeDtypeStruct((B, E), jnp.bfloat16)),
        in_specs=[anywhere, anywhere, vmem, anywhere, anywhere, vmem, vmem, vmem, vmem,
                  pl.BlockSpec(memory_space=pltpu.SMEM)],
        out_specs=(vmem, vmem),
        scratch_shapes=[
            pltpu.VMEM((16, M, 2 * R), jnp.bfloat16),
            pltpu.VMEM((2, K, N // 2), jnp.bfloat16),
            pltpu.VMEM((2, M, N // 2), jnp.float32),
            pltpu.VMEM((M, E), jnp.float32),
            pltpu.VMEM((6, T, E // 2), jnp.bfloat16),
            pltpu.VMEM((6, T, E // 2), jnp.bfloat16),
            pltpu.VMEM((2 * B, E), jnp.bfloat16),
            pltpu.VMEM((2 * B, T // 2), jnp.float32),
            pltpu.VMEM((16, T, E), jnp.bfloat16),
            pltpu.VMEM((E, T), jnp.bfloat16),
            pltpu.VMEM((20, 1, T), jnp.int32),
            pltpu.VMEM((16, 8, T // 2), jnp.float32),
            pltpu.VMEM((20, 8, T // 2), jnp.float32),
            pltpu.VMEM(log_freq.shape, jnp.bfloat16),
            pltpu.VMEM((OR, log_freq.shape[0] // 8), jnp.bfloat16),
            pltpu.VMEM((OR, L), jnp.int32),
            pltpu.VMEM((OR, L), jnp.float32),
            pltpu.VMEM((pool, cap, E), jnp.bfloat16),
            pltpu.VMEM((1, 128), jnp.float32),
            pltpu.VMEM((pool, cap, E), jnp.bfloat16),
            pltpu.VMEM((pool, 1, 128), jnp.float32),
            dma((16,)), dma((4,)), dma((1,)), dma((64,)), dma((1,)), dma((64,)),
            dma((2,)), dma((2,)), dma((1,)), dma((6,)), dma((1,)), dma((64,)),
            dma((1,)), dma((1,)), dma((1,)), dma((1,)), dma((1,)), dma((1,)), dma((1,)), dma((1,)),
            dma((1,)), dma((1,)),
        ],
        compiler_params=pltpu.CompilerParams(collective_id=0, has_side_effects=True, vmem_limit_bytes=56 * 1024 * 1024),
        name="tower",
    )(tokens, w_hidden, w_out, bank, log_freq, item_ids, positives, new_items, new_owner, queue_head)


def body(
    tokens, w_hidden, w_out, bank, item_ids, log_freq, positives, new_items, new_owner, queue_head
):
    return tower(
        tokens, w_hidden, w_out, bank, log_freq.reshape(-1, 128), item_ids.reshape(-1, 128),
        positives, new_items, new_owner.reshape(1, -1), queue_head,
    )


def solution(mesh):
    finer = Mesh(
        mesh.devices.reshape(mesh.shape["dp"], mesh.shape["tensor"], 4, 4, 2),
        ("dp", "tensor", "pool_0", "pool_1", "pool_2"),
    )
    in_specs = (
        P(DP_POOL, None, None),
        P(POOL, "tensor"),
        P("tensor", None),
        P(POOL, None),
        P(POOL),
        P(),
        P(DP_POOL, "tensor"),
        P(POOL, None),
        P(POOL, None),
        P(POOL),
    )
    out_specs = (P(DP_POOL, "tensor"), P(POOL, None))
    return jax.shard_map(body, mesh=finer, in_specs=in_specs, out_specs=out_specs, check_vma=False)
```

```python
import functools
import jax
import jax.numpy as jnp
from jax import lax
from jax.experimental import pallas as pl
from jax.experimental.pallas import tpu as pltpu

AXES = ("dp", "tensor", "pool_0", "pool_1", "pool_2")
from jax.sharding import Mesh
from jax.sharding import PartitionSpec as P

MESH = pl.DeviceIdType.MESH
POOL = ("pool_0", "pool_1", "pool_2")
DP_POOL = ("dp", "pool_0", "pool_1", "pool_2")


LOG2E = 1.4426950408889634
LN2 = 0.6931471805599453
SCALE = 5.0 * LOG2E


def tower_kernel(tok_hbm, w_hbm, wo_ref, bank_hbm, freq_hbm, ids_ref, pos_ref, items_ref,
                 owner_ref, head_ref, out_ref, newbank_ref, tok, wbuf, acc, part, ysend, yrecv,
                 bankbuf, offb, qbuf, qt0, qt1, logits0, logits1, tbuf, sbuf, stats, table, pick, where_at, found, packed, counts, rows_in, counts_in, tok_sem, own_sem, send_sem, recv_sem, psend, precv,
                 xsend, xrecv, ysem, yrsem, qsend, qrecv, tsend, trecv, ssend, srecv,
                 nsend, nrecv, csend, crecv, osend, orecv):
    dp, y, x, zl, c = (lax.axis_index(a) for a in AXES)
    ny = lax.axis_size("tensor")
    pz = dp * 4 + zl
    R = w_hbm.shape[0]
    C = w_hbm.shape[1] // 2
    Q = C // 2
    M = tok.shape[1]
    offs = (0, -1, 1, 2)

    def chip(dx, dz):
        xx = lax.rem(x + dx + 4, 4)
        zz = lax.rem(pz + dz + 8, 8)
        return (zz // 4, y, xx, lax.rem(zz, 4), c)

    def along(h, first, step):
        return chip(step, 0) if (h == 0) == first else chip(0, step)

    partner = (dp, y, x, zl, 1 - c)

    def arrived(ref, sem):
        pltpu.make_async_remote_copy(
            src_ref=ref, dst_ref=ref, send_sem=send_sem.at[0], recv_sem=sem,
            device_id=partner, device_id_type=MESH).wait_recv()

    def sent(ref, sem):
        pltpu.make_async_remote_copy(
            src_ref=ref, dst_ref=ref, send_sem=sem, recv_sem=recv_sem.at[0],
            device_id=partner, device_id_type=MESH).wait_send()

    def column(step):
        return (dp, lax.rem(y + step + ny, ny), x, zl, c)

    def block_of(h, f, s):
        dx = f * (1 - h) + s * h
        dz = s * (1 - h) + f * h
        return lax.rem(x + dx + 4, 4) * 4 + lax.rem(zl + dz + 4, 4)

    def view(h, f, s, piece, core):
        row = pl.multiple_of(block_of(h, f, s) * (2 * R) + core * R, R)
        cols = slice(None) if piece is None else pl.ds(piece * Q, Q)
        return wbuf.at[h, pl.ds(row, R), cols]

    def key(h, f, s, piece):
        return ((h * 4 + offs.index(f)) * 4 + offs.index(s)) * 2 + (piece or 0)

    sends = []

    def send(h, f, s, piece, first, step, kind):
        nf, ns = kind
        ref = view(h, f, s, piece, c)
        cp = pltpu.make_async_remote_copy(
            src_ref=ref, dst_ref=ref, send_sem=send_sem.at[0],
            recv_sem=recv_sem.at[key(h, nf, ns, piece)],
            device_id=along(h, first, step), device_id_type=MESH)
        cp.start()
        sends.append(cp)

    psends = []

    def to_partner(h, f, s, piece):
        ref = view(h, f, s, piece, c)
        cp = pltpu.make_async_remote_copy(
            src_ref=ref, dst_ref=ref, send_sem=psend.at[0],
            recv_sem=precv.at[key(h, f, s, piece)], device_id=partner, device_id_type=MESH)
        cp.start()
        psends.append(cp)

    def wait_link(h, f, s, piece):
        ref = view(h, f, s, piece, c)
        pltpu.make_async_remote_copy(
            src_ref=ref, dst_ref=ref, send_sem=send_sem.at[0],
            recv_sem=recv_sem.at[key(h, f, s, piece)], device_id=partner, device_id_type=MESH).wait_recv()

    def wait_partner(h, f, s, piece):
        ref = view(h, f, s, piece, 1 - c)
        pltpu.make_async_remote_copy(
            src_ref=ref, dst_ref=ref, send_sem=send_sem.at[0],
            recv_sem=precv.at[key(h, f, s, piece)], device_id=partner, device_id_type=MESH).wait_recv()

    def pieces(f, s):
        return (0, 1) if (f == 2 and s == 0) or s == 2 else (None,)

    B = bank_hbm.shape[0]
    mine = pl.ds(pl.multiple_of(c * B, B), B)
    own = [pltpu.make_async_copy(w_hbm.at[:, pl.ds(h * C, C)], view(h, 0, 0, None, c), own_sem.at[h]) for h in (0, 1)]
    own.append(pltpu.make_async_copy(bank_hbm, bankbuf.at[mine, :], own_sem.at[2]))
    freq_copy = pltpu.make_async_copy(freq_hbm, table, own_sem.at[3])
    for cp in own:
        cp.start()

    barrier = pltpu.get_barrier_semaphore()
    peers = [chip(1, 0), chip(-1, 0), chip(0, 1), chip(0, -1), partner]
    if ny > 1:
        peers += [column(step) for step in range(1, ny)]
    for p in peers:
        pl.semaphore_signal(barrier, inc=1, device_id=p, device_id_type=MESH)

    groups = [[(0, 0)], [(-1, 0), (1, 0)], [(0, -1), (0, 1)], [(2, 0)],
              [(-1, -1), (-1, 1)], [(1, -1), (1, 1)], [(0, 2)], [(2, -1), (2, 1)], [(-1, 2), (1, 2)], [(2, 2)]]

    tok_wait = {}
    n = 0
    for g in groups:
        for f, s in g:
            for h in (0, 1):
                dx, dz = (f, s) if h == 0 else (s, f)
                if (dx, dz) in tok_wait:
                    continue
                b = block_of(0, dx, dz)
                cp = pltpu.make_async_copy(
                    tok_hbm.at[0, :, pl.ds(pl.multiple_of(b * 2 * R, 2 * R), 2 * R)], tok.at[b], tok_sem.at[n])
                cp.start()
                tok_wait[(dx, dz)] = cp
                n += 1

    for cp in own:
        cp.wait()
    pl.semaphore_wait(barrier, len(peers))

    for h in (0, 1):
        to_partner(h, 0, 0, None)
    for h in (0, 1):
        for step in (1, -1):
            send(h, 0, 0, None, True, step, (-step, 0))
    for h in (0, 1):
        for step in (1, -1):
            send(h, 0, 0, None, False, step, (0, -step))

    swaps = []

    def swap(ref):
        cp = pltpu.make_async_remote_copy(
            src_ref=ref.at[mine, :], dst_ref=ref.at[mine, :], send_sem=xsend.at[len(swaps)],
            recv_sem=xrecv.at[len(swaps)], device_id=partner, device_id_type=MESH)
        cp.start()
        swaps.append(cp)

    swap(bankbuf)
    freq_copy.start()

    bf = jnp.bfloat16
    f32 = jnp.float32
    i32 = jnp.int32

    def onehot(a, b):
        return jnp.where(a == b, 1.0, 0.0).astype(bf)

    peers_in_pool = packed.shape[0]
    cap = packed.shape[1]

    def pack():
        n = items_ref.shape[0]
        width = counts.shape[1]
        owner = owner_ref[...]
        mark = jnp.where(lax.broadcasted_iota(i32, (width, n), 0) == owner, 1.0, 0.0)
        lowrow = lax.broadcasted_iota(i32, (n, n), 0)
        lowcol = lax.broadcasted_iota(i32, (n, n), 1)
        upper = jnp.where(lowrow < lowcol, 1.0, 0.0).astype(bf)
        ahead = jnp.dot(mark.astype(bf), upper, preferred_element_type=f32)
        before = jnp.sum(mark * ahead, axis=0, keepdims=True)
        place = owner * cap + before.astype(i32)
        spread = onehot(lax.broadcasted_iota(i32, (peers_in_pool * cap, n), 0), place)
        rows = jnp.dot(spread, items_ref[...], preferred_element_type=f32)
        packed[...] = rows.astype(bf).reshape(packed.shape)
        tally = lax.dot_general(jnp.ones((8, n), bf), mark.astype(bf), (((1,), (1,)), ((), ())), preferred_element_type=f32)
        counts[...] = tally[0:1, :]

    L = ids_ref.shape[1]
    A = table.shape[0] // 8

    G = ids_ref.shape[0] // ny
    OR = B // ny
    here_rows = pl.ds(pl.multiple_of(c * B + y * OR, OR), OR)

    def off_start():
        for g in range(G):
            row = ids_ref[pl.ds(y * G + g, 1), :].astype(f32)
            idx = jnp.transpose(jnp.broadcast_to(row, (L, L))).astype(i32)
            where_at[pl.ds(g * L, L), :] = idx
            line = lax.rem(idx // L, A)
            wide = jnp.concatenate([line] * (A // L), axis=1) if A > L else line[:, :A]
            pick[pl.ds(g * L, L), :] = onehot(wide, lax.broadcasted_iota(i32, (L, A), 1))

    def off_step(j):
        if j == 0:
            freq_copy.wait()
        tile = min(256, OR)

        def rows_step(r, carry):
            rs = pl.ds(pl.multiple_of(r * tile, tile), tile)
            pair = jnp.concatenate([table[pl.ds(2 * j * A, A), :], table[pl.ds((2 * j + 1) * A, A), :]], axis=1)
            d = jnp.dot(pick[rs, :], pair, preferred_element_type=f32)
            part_of = where_at[rs, :] // (L * A)
            got = jnp.where(part_of == 2 * j, d[:, :L], jnp.where(part_of == 2 * j + 1, d[:, L:], 0.0))
            if j == 0:
                found[rs, :] = got
            else:
                found[rs, :] = found[rs, :] + got
            return carry

        lax.fori_loop(0, OR // tile, rows_step, 0)

    def off_end():
        lane_at = lax.broadcasted_iota(i32, (OR, L), 1)
        val = jnp.sum(jnp.where(lax.rem(where_at[...], L) == lane_at, found[...], 0.0), axis=1, keepdims=True)
        offb[here_rows, :] = jnp.broadcast_to(val * LOG2E, (OR, offb.shape[1]))
        for step in range(1, ny):
            pltpu.make_async_remote_copy(
                src_ref=offb.at[here_rows, :], dst_ref=offb.at[here_rows, :], send_sem=osend.at[0],
                recv_sem=orecv.at[0], device_id=column(step), device_id_type=MESH).start()

    def off_collect():
        if ny > 1:
            arrived(offb.at[pl.ds(0, (ny - 1) * OR), :], orecv.at[0])
        swap(offb)

    def relay(g):
        for f, s in groups[g]:
            for h in (0, 1):
                for p in pieces(f, s):
                    wait_link(h, f, s, p)
                for p in pieces(f, s):
                    to_partner(h, f, s, p)
                if s == 0 and f != 2:
                    send(h, f, 0, 0 if f == -1 else 1, True, -f, (2, 0))
                if s == 0:
                    for step in (1, -1):
                        send(h, f, 0, None, False, step, (f, -step))
                elif s != 2:
                    send(h, f, s, 0 if s == -1 else 1, False, -s, (f, 2))

    def mm(g):
        items = groups[g]
        for f, s in items:
            for h in (0, 1):
                dx, dz = (f, s) if h == 0 else (s, f)
                if (dx, dz) in tok_wait:
                    tok_wait.pop((dx, dz)).wait()
                for p in pieces(f, s):
                    wait_partner(h, f, s, p)

        def step(i, carry):
            h = lax.rem(i, 2)
            j = i // 2
            f = sum(jnp.where(j == k, fs[0], 0) for k, fs in enumerate(items))
            s = sum(jnp.where(j == k, fs[1], 0) for k, fs in enumerate(items))
            b = block_of(h, f, s)
            row = pl.multiple_of(b * (2 * R), 2 * R)
            d = jnp.dot(tok[b], wbuf[h, pl.ds(row, 2 * R), :], preferred_element_type=jnp.float32)
            if g == 0:
                acc[h] = d
            else:
                acc[h] = acc[h] + d
            return carry

        lax.fori_loop(0, 2 * len(items), step, 0)

    pack()
    mm(0)
    off_start()
    relay(1)
    off_step(0)
    off_step(1)
    relay(2)
    mm(1)
    off_step(2)
    off_step(3)
    off_end()
    relay(3)
    mm(2)
    relay(4)
    mm(3)
    relay(5)
    mm(4)
    relay(6)
    mm(5)
    relay(7)
    mm(6)
    off_collect()
    relay(8)
    mm(7)
    relay(9)
    mm(8)
    mm(9)

    far = [(i, k) for i in offs for k in (0, -1, 1, 2, -2) if (i, k) != (0, 0)]

    def spot(i, k):
        return offs.index(i) * 5 + (0, -1, 1, 2, -2).index(k)

    def mirror(i, k):
        return spot(i if i == 2 else -i, -k)

    zs = (0, -1, 1, 2)
    near = [(i, k, o) for i in offs for k in zs for o in (0, 1) if (i, k, o) != (0, 0, 0)]

    me = (x * 4 + zl) * 2 + c
    rows_in[me] = packed[me]
    counts_in[me] = counts[...]

    def post():
        tcopies = []
        for n, (i, k) in enumerate(far):
            cp = pltpu.make_async_remote_copy(
                src_ref=pos_ref, dst_ref=tbuf.at[mirror(i, k)], send_sem=tsend.at[0], recv_sem=trecv.at[0],
                device_id=chip(i, k), device_id_type=MESH)
            cp.start()
            tcopies.append(cp)
        ncopies = []
        for n, (i, k, o) in enumerate(near):
            to = chip(i, k)
            core = 1 - c if o else c
            to = to[:4] + (core,)
            owner_at = (to[2] * 4 + to[3]) * 2 + core
            for src, dst, ss, rr in ((packed.at[owner_at], rows_in.at[me], nsend, nrecv), (counts, counts_in.at[me], csend, crecv)):
                cp = pltpu.make_async_remote_copy(
                    src_ref=src, dst_ref=dst, send_sem=ss.at[0], recv_sem=rr.at[0], device_id=to, device_id_type=MESH)
                cp.start()
                ncopies.append(cp)

    T = M // 4
    H = part.shape[1] // 2
    left, right = pl.ds(0, H), pl.ds(H, H)

    def quarter(step):
        return pl.ds(pl.multiple_of(lax.rem(y + step + 4, 4) * T, T), T)

    def partial(step):
        rs = quarter(step)
        total = None
        for h in (0, 1):
            hid = jnp.maximum(acc[h, rs, :], 0.0).astype(jnp.bfloat16)
            d = jnp.dot(hid, wo_ref[pl.ds(h * C, C), :], preferred_element_type=jnp.float32)
            total = d if total is None else total + d
        part[rs, :] = total

    ycopies = []

    def ysend_to(slot, step):
        cp = pltpu.make_async_remote_copy(
            src_ref=ysend.at[slot], dst_ref=yrecv.at[slot], send_sem=ysem.at[0], recv_sem=yrsem.at[slot],
            device_id=column(step), device_id_type=MESH)
        cp.start()
        ycopies.append(cp)

    def ywait(slot):
        pltpu.make_async_remote_copy(
            src_ref=ysend.at[slot], dst_ref=yrecv.at[slot], send_sem=ysem.at[0], recv_sem=yrsem.at[slot],
            device_id=partner, device_id_type=MESH).wait_recv()

    if ny > 1:
        partial(2)
        ysend[0] = part[quarter(2), left].astype(bf)
        ysend_to(0, -1)
        ysend[1] = part[quarter(2), right].astype(bf)
        ysend_to(1, 1)
        partial(-1)
        ysend[2] = part[quarter(-1), right].astype(bf)
        ysend_to(2, -1)
        partial(1)
        ysend[3] = part[quarter(1), left].astype(bf)
        ysend_to(3, 1)
        post()
        ywait(0)
        ysend[4] = (yrecv[0].astype(f32) + part[quarter(-1), left]).astype(bf)
        ysend_to(4, -1)
        ywait(1)
        ysend[5] = (yrecv[1].astype(f32) + part[quarter(1), right]).astype(bf)
        ysend_to(5, 1)
        partial(0)
        ywait(2)
        ywait(3)
        ywait(4)
        ywait(5)
        own_q = quarter(0)
        qbuf[0, :, left] = ((part[own_q, left] + yrecv[3].astype(f32) + yrecv[4].astype(f32)) * SCALE).astype(bf)
        qbuf[0, :, right] = ((part[own_q, right] + yrecv[2].astype(f32) + yrecv[5].astype(f32)) * SCALE).astype(bf)
    else:
        post()
        partial(0)
        qbuf[0] = (part[pl.ds(0, T), :] * SCALE).astype(bf)

    P2 = T // 2
    P4 = T // 4

    def qview(h, f, s, piece):
        dx, dz = (f, s) if h == 0 else (s, f)
        rows = pl.ds(h * P2, P2) if piece is None else pl.ds(h * P2 + piece * P4, P4)
        return qbuf.at[offs.index(dx) * 4 + offs.index(dz), rows, :]

    qsends = []

    def qgo(h, f, s, piece, first, step, kind):
        cp = pltpu.make_async_remote_copy(
            src_ref=qview(h, f, s, piece), dst_ref=qview(h, kind[0], kind[1], piece), send_sem=qsend.at[0],
            recv_sem=qrecv.at[key(h, kind[0], kind[1], piece)],
            device_id=along(h, first, step), device_id_type=MESH)
        cp.start()
        qsends.append(cp)

    def qwait(h, f, s, piece):
        ref = qview(h, f, s, piece)
        pltpu.make_async_remote_copy(
            src_ref=ref, dst_ref=ref, send_sem=qsend.at[0],
            recv_sem=qrecv.at[key(h, f, s, piece)], device_id=partner, device_id_type=MESH).wait_recv()

    for first in (True, False):
        for h in (0, 1):
            for step in (1, -1):
                qgo(h, 0, 0, None, first, step, (-step, 0) if first else (0, -step))

    def qrelay(g):
        for f, s in groups[g]:
            for h in (0, 1):
                for p in pieces(f, s):
                    qwait(h, f, s, p)
                if s == 0 and f != 2:
                    qgo(h, f, 0, 0 if f == -1 else 1, True, -f, (2, 0))
                if s == 0:
                    for step in (1, -1):
                        qgo(h, f, 0, None, False, step, (f, -step))
                elif s != 2:
                    qgo(h, f, s, 0 if s == -1 else 1, False, -s, (f, 2))

    for cp in swaps:
        cp.wait_recv()
    tbuf[0] = pos_ref[...]
    arrived(tbuf.at[pl.ds(1, len(far))], trecv.at[0])

    base = (x * 4 + zl) * (2 * B)
    CH = min(1024, 2 * B)
    lane = lax.broadcasted_iota(jnp.int32, (1, T), 1)
    lower = lax.rem(lane, P2) < P4
    sub = lax.broadcasted_iota(jnp.int32, (8, T), 0)
    W = sbuf.shape[2]

    SUB = min(64, CH)
    G8 = SUB // 8
    levels = G8.bit_length() - 1

    def pick_of(values, i):
        return sum(jnp.where(i == k, v, 0) for k, v in enumerate(values))

    def place(items, i):
        if isinstance(i, int):
            return tuple(offs.index(v) for v in items[i])
        return tuple(pick_of([offs.index(item[d]) for item in items], i) for d in (0, 1))

    def turn(at, qt):
        qt[...] = jnp.transpose(qbuf[at[0] * 4 + at[1]])

    def multiply(rows, logits, qt):
        prod = jnp.dot(bankbuf[rows, :], qt[...], preferred_element_type=f32)
        off = offb[rows, :]
        if T > off.shape[1]:
            off = jnp.concatenate([off] * (T // off.shape[1]), axis=1)
        logits[rows, :] = prod - off

    def block(ahead, logits_ahead, qt, at, logits):
        if ahead is not None:
            turn(ahead, qt)
        if at is not None:
            ix, iz = at
            slot = ix * 4 + iz
            target = tbuf[ix * 5 + iz]
            behind = jnp.logical_and(lower, jnp.broadcast_to(iz, lower.shape) == 3)
            target = jnp.where(behind, tbuf[ix * 5 + 4], target)
            t = jnp.broadcast_to(target - base, (8, T))
            group = lax.shift_right_arithmetic(t, 3)
            which = lax.shift_right_arithmetic(group, levels)

        def chunk(k, carry):
            first = pl.multiple_of(k * CH, CH)
            if ahead is not None:
                multiply(pl.ds(first, CH), logits_ahead, qt)
            if at is None:
                return carry
            m, total, hit = carry
            bits = [jnp.bitwise_and(lax.shift_right_arithmetic(group, b), 1) == 1 for b in range(levels)]
            for u in range(CH // SUB):
                logit = logits[pl.ds(first + u * SUB, SUB), :].reshape(G8, 8, T)
                top = jnp.maximum(m, jnp.max(logit, axis=0))
                chosen = [logit[r] for r in range(G8)]
                for b in range(levels):
                    chosen = [jnp.where(bits[b], chosen[2 * r + 1], chosen[2 * r]) for r in range(len(chosen) // 2)]
                hit = jnp.where(which == k * (CH // SUB) + u, chosen[0], hit)
                total = total * jnp.exp2(m - top) + jnp.sum(jnp.exp2(logit - top[None]), axis=0)
                m = top
            return m, total, hit

        zero = jnp.zeros((8, T), f32)
        m, total, hit = lax.fori_loop(0, 2 * B // CH, chunk, (jnp.full((8, T), -jnp.inf, f32), zero, zero))
        if at is None:
            return
        top = jnp.max(m, axis=0, keepdims=True)
        total = jnp.sum(total * jnp.exp2(m - top), axis=0, keepdims=True)
        score = jnp.sum(jnp.where(jnp.bitwise_and(t, 7) == sub, hit, 0.0), axis=0, keepdims=True)
        for n, v in enumerate((top, total, score)):
            for k in range(2):
                sbuf[slot, pl.ds(n * 2 + k, 1), :] = v[:, k * W:(k + 1) * W]

    def give_back(items):
        for dx, dz in items:
            for k in ((dz,) if dz != 2 else (2, -2)):
                if (dx, k) == (0, 0):
                    continue
                cp = pltpu.make_async_remote_copy(
                    src_ref=sbuf.at[offs.index(dx) * 4 + offs.index(dz)], dst_ref=stats.at[mirror(dx, k)],
                    send_sem=ssend.at[0], recv_sem=srecv.at[0], device_id=chip(dx, k), device_id_type=MESH)
                cp.start()

    def blocks(items, last):
        todo = [last] + items[:-1]

        def pair(i, carry):
            block(place(items, 2 * i), logits1, qt1, place(todo, 2 * i), logits0)
            block(place(items, 2 * i + 1), logits0, qt0, place(todo, 2 * i + 1), logits1)
            return carry

        if len(items) == 2:
            pair(0, 0)
        else:
            lax.fori_loop(0, len(items) // 2, pair, 0)
        give_back(todo)

    block((0, 0), logits0, qt0, None, None)
    qrelay(1)
    qrelay(2)
    blocks([(-1, 0), (1, 0), (0, -1), (0, 1)], (0, 0))
    qrelay(3)
    qrelay(4)
    qrelay(5)
    blocks([(-1, -1), (-1, 1), (1, -1), (1, 1)], (0, 1))
    qrelay(6)
    qrelay(7)
    blocks([(2, 0), (0, 2)], (1, 1))
    qrelay(8)
    blocks([(2, -1), (2, 1), (-1, 2), (1, 2)], (0, 2))
    qrelay(9)
    block((3, 3), logits1, qt1, (2, 3), logits0)
    give_back([(1, 2)])
    block(None, None, None, (3, 3), logits1)
    give_back([(2, 2)])

    arrived(rows_in.at[pl.ds(0, len(near))], nrecv.at[0])
    arrived(counts_in.at[pl.ds(0, len(near))], crecv.at[0])
    J = peers_in_pool * cap
    width = counts.shape[1]
    every = counts_in[...].reshape(peers_in_pool, width)
    mine_only = jnp.where(lax.broadcasted_iota(i32, every.shape, 1) == me, every, 0.0)
    count = jnp.sum(mine_only, axis=1, keepdims=True)
    source = lax.broadcasted_iota(i32, (peers_in_pool, J), 0)
    column_of = lax.broadcasted_iota(i32, (peers_in_pool, J), 1) // cap
    valid = jnp.sum(jnp.where(source == column_of, count, 0.0), axis=0, keepdims=True)
    ahead = jnp.sum(jnp.where(source < column_of, count, 0.0), axis=0, keepdims=True)
    nth = lax.rem(lax.broadcasted_iota(i32, (1, J), 1), cap)
    slot_of = lax.rem(head_ref[0] + ahead.astype(i32) + nth, B)
    slot_of = jnp.where(nth < valid.astype(i32), slot_of, -1)
    tile = min(256, B)

    def write(r, carry):
        first = pl.multiple_of(r * tile, tile)
        spread = onehot(lax.broadcasted_iota(i32, (tile, J), 0) + first, slot_of)
        fresh = jnp.dot(spread, rows_in[...].reshape(J, rows_in.shape[2]), preferred_element_type=f32)
        hits = jnp.dot(spread, jnp.ones((J, rows_in.shape[2]), bf), preferred_element_type=f32)
        old = bankbuf[pl.ds(pl.multiple_of(c * B + first, tile), tile), :]
        newbank_ref[pl.ds(first, tile), :] = jnp.where(hits > 0.5, fresh, old.astype(f32)).astype(bf)
        return carry

    lax.fori_loop(0, B // tile, write, 0)

    stats[0] = sbuf[0]
    arrived(stats.at[pl.ds(1, len(far))], srecv.at[0])
    low = lax.broadcasted_iota(jnp.int32, (8, W), 1) < P4
    parts = []
    for i in offs:
        for k in (0, -1, 1):
            st = stats[spot(i, k)]
            parts.append((st[0:2], st[2:4], st[4:6]))
        st = jnp.where(low, stats[spot(i, 2)], stats[spot(i, -2)])
        parts.append((st[0:2], st[2:4], st[4:6]))
    top = functools.reduce(jnp.maximum, [p[0] for p in parts])
    total = sum(p[1] * jnp.exp2(p[0] - top) for p in parts)
    score = sum(p[2] for p in parts)
    loss = LN2 * (top - score) + jnp.log(total)
    for k in range(2):
        out_ref[:, k * W:(k + 1) * W] = loss[k:k + 1, :]

    sent(wbuf.at[0, pl.ds(0, 30 * R), :], send_sem.at[0])
    sent(wbuf.at[0], psend.at[0])
    sent(tbuf.at[pl.ds(1, len(far))], tsend.at[0])
    sent(rows_in.at[pl.ds(0, len(near))], nsend.at[0])
    sent(counts_in.at[pl.ds(0, len(near))], csend.at[0])
    sent(qbuf.at[pl.ds(0, 15)], qsend.at[0])
    sent(stats.at[pl.ds(1, len(far))], ssend.at[0])
    for cp in swaps:
        cp.wait_send()
    if ny > 1:
        sent(ysend, ysem.at[0])
        sent(offb.at[pl.ds(0, (ny - 1) * OR), :], osend.at[0])


def tower(tokens, w_hidden, w_out, bank, log_freq, item_ids, positives, new_items, new_owner, queue_head):
    M, K = tokens.shape[1:]
    R, N = w_hidden.shape
    E = w_out.shape[1]
    B = bank.shape[0]
    T = M // 4
    L = item_ids.shape[1]
    pool = K // R
    OR = B // lax.axis_size("tensor")
    cap = 2 * new_items.shape[0] // pool
    anywhere = pl.BlockSpec(memory_space=pl.ANY)
    vmem = pl.BlockSpec(memory_space=pltpu.VMEM)
    dma = pltpu.SemaphoreType.DMA
    return pl.pallas_call(
        tower_kernel,
        out_shape=(jax.ShapeDtypeStruct((1, T), jnp.float32), jax.ShapeDtypeStruct((B, E), jnp.bfloat16)),
        in_specs=[anywhere, anywhere, vmem, anywhere, anywhere, vmem, vmem, vmem, vmem,
                  pl.BlockSpec(memory_space=pltpu.SMEM)],
        out_specs=(vmem, vmem),
        scratch_shapes=[
            pltpu.VMEM((16, M, 2 * R), jnp.bfloat16),
            pltpu.VMEM((2, K, N // 2), jnp.bfloat16),
            pltpu.VMEM((2, M, N // 2), jnp.float32),
            pltpu.VMEM((M, E), jnp.float32),
            pltpu.VMEM((6, T, E // 2), jnp.bfloat16),
            pltpu.VMEM((6, T, E // 2), jnp.bfloat16),
            pltpu.VMEM((2 * B, E), jnp.bfloat16),
            pltpu.VMEM((2 * B, T // 2), jnp.float32),
            pltpu.VMEM((16, T, E), jnp.bfloat16),
            pltpu.VMEM((E, T), jnp.bfloat16),
            pltpu.VMEM((E, T), jnp.bfloat16),
            pltpu.VMEM((2 * B, T), jnp.float32),
            pltpu.VMEM((2 * B, T), jnp.float32),
            pltpu.VMEM((20, 1, T), jnp.int32),
            pltpu.VMEM((16, 8, T // 2), jnp.float32),
            pltpu.VMEM((20, 8, T // 2), jnp.float32),
            pltpu.VMEM(log_freq.shape, jnp.bfloat16),
            pltpu.VMEM((OR, log_freq.shape[0] // 8), jnp.bfloat16),
            pltpu.VMEM((OR, L), jnp.int32),
            pltpu.VMEM((OR, L), jnp.float32),
            pltpu.VMEM((pool, cap, E), jnp.bfloat16),
            pltpu.VMEM((1, 128), jnp.float32),
            pltpu.VMEM((pool, cap, E), jnp.bfloat16),
            pltpu.VMEM((pool, 1, 128), jnp.float32),
            dma((16,)), dma((4,)), dma((1,)), dma((64,)), dma((1,)), dma((64,)),
            dma((2,)), dma((2,)), dma((1,)), dma((6,)), dma((1,)), dma((64,)),
            dma((1,)), dma((1,)), dma((1,)), dma((1,)), dma((1,)), dma((1,)), dma((1,)), dma((1,)),
            dma((1,)), dma((1,)),
        ],
        compiler_params=pltpu.CompilerParams(collective_id=0, has_side_effects=True, vmem_limit_bytes=56 * 1024 * 1024),
        name="tower",
    )(tokens, w_hidden, w_out, bank, log_freq, item_ids, positives, new_items, new_owner, queue_head)


def body(
    tokens, w_hidden, w_out, bank, item_ids, log_freq, positives, new_items, new_owner, queue_head
):
    results = tower(
        tokens, w_hidden, w_out, bank, log_freq.reshape(-1, 128), item_ids.reshape(-1, 128),
        positives, new_items, new_owner.reshape(1, -1), queue_head,
    )
    return settle(results)


def settle_kernel(loss_in, bank_in, loss_out, bank_out):
    loss_out[...] = loss_in[...]
    bank_out[...] = bank_in[...]


def settle(results):
    vmem = pl.BlockSpec(memory_space=pltpu.VMEM)
    return pl.pallas_call(
        settle_kernel,
        out_shape=tuple(jax.ShapeDtypeStruct(r.shape, r.dtype) for r in results),
        in_specs=[vmem, vmem],
        out_specs=(vmem, vmem),
        name="settle",
    )(*results)


def solution(mesh):
    finer = Mesh(
        mesh.devices.reshape(mesh.shape["dp"], mesh.shape["tensor"], 4, 4, 2),
        ("dp", "tensor", "pool_0", "pool_1", "pool_2"),
    )
    in_specs = (
        P(DP_POOL, None, None),
        P(POOL, "tensor"),
        P("tensor", None),
        P(POOL, None),
        P(POOL),
        P(),
        P(DP_POOL, "tensor"),
        P(POOL, None),
        P(POOL, None),
        P(POOL),
    )
    out_specs = (P(DP_POOL, "tensor"), P(POOL, None))
    return jax.shard_map(body, mesh=finer, in_specs=in_specs, out_specs=out_specs, check_vma=False)
```

```python
import functools
import jax
import jax.numpy as jnp
from jax import lax
from jax.experimental import pallas as pl
from jax.experimental.pallas import tpu as pltpu

AXES = ("dp", "tensor", "pool_0", "pool_1", "pool_2")
from jax.sharding import Mesh
from jax.sharding import PartitionSpec as P

MESH = pl.DeviceIdType.MESH
POOL = ("pool_0", "pool_1", "pool_2")
DP_POOL = ("dp", "pool_0", "pool_1", "pool_2")


LOG2E = 1.4426950408889634
LN2 = 0.6931471805599453
SCALE = 5.0 * LOG2E


def tower_kernel(tok_hbm, w_hbm, wo_ref, bank_hbm, freq_hbm, ids_ref, pos_ref, items_ref,
                 owner_ref, head_ref, out_ref, newbank_ref, tok, wbuf, acc, part, ysend, yrecv,
                 bankbuf, offb, qbuf, qt0, qt1, logits0, logits1, tbuf, sbuf, stats, table, pick, where_at, found, packed, counts, rows_in, counts_in, tok_sem, own_sem, send_sem, recv_sem, psend, precv,
                 xsend, xrecv, ysem, yrsem, qsend, qrecv, tsend, trecv, ssend, srecv,
                 nsend, nrecv, csend, crecv, osend, orecv):
    dp, y, x, zl, c = (lax.axis_index(a) for a in AXES)
    ny = lax.axis_size("tensor")
    pz = dp * 4 + zl
    R = w_hbm.shape[0]
    C = w_hbm.shape[1] // 2
    Q = C // 2
    M = tok.shape[1]
    offs = (0, -1, 1, 2)

    def chip(dx, dz):
        xx = lax.rem(x + dx + 4, 4)
        zz = lax.rem(pz + dz + 8, 8)
        return (zz // 4, y, xx, lax.rem(zz, 4), c)

    def along(h, first, step):
        return chip(step, 0) if (h == 0) == first else chip(0, step)

    partner = (dp, y, x, zl, 1 - c)

    def arrived(ref, sem):
        pltpu.make_async_remote_copy(
            src_ref=ref, dst_ref=ref, send_sem=send_sem.at[0], recv_sem=sem,
            device_id=partner, device_id_type=MESH).wait_recv()

    def sent(ref, sem):
        pltpu.make_async_remote_copy(
            src_ref=ref, dst_ref=ref, send_sem=sem, recv_sem=recv_sem.at[0],
            device_id=partner, device_id_type=MESH).wait_send()

    def column(step):
        return (dp, lax.rem(y + step + ny, ny), x, zl, c)

    def block_of(h, f, s):
        dx = f * (1 - h) + s * h
        dz = s * (1 - h) + f * h
        return lax.rem(x + dx + 4, 4) * 4 + lax.rem(zl + dz + 4, 4)

    def view(h, f, s, piece, core):
        row = pl.multiple_of(block_of(h, f, s) * (2 * R) + core * R, R)
        cols = slice(None) if piece is None else pl.ds(piece * Q, Q)
        return wbuf.at[h, pl.ds(row, R), cols]

    def key(h, f, s, piece):
        return ((h * 4 + offs.index(f)) * 4 + offs.index(s)) * 2 + (piece or 0)

    sends = []

    def send(h, f, s, piece, first, step, kind):
        nf, ns = kind
        ref = view(h, f, s, piece, c)
        cp = pltpu.make_async_remote_copy(
            src_ref=ref, dst_ref=ref, send_sem=send_sem.at[0],
            recv_sem=recv_sem.at[key(h, nf, ns, piece)],
            device_id=along(h, first, step), device_id_type=MESH)
        cp.start()
        sends.append(cp)

    psends = []

    def to_partner(h, f, s, piece):
        ref = view(h, f, s, piece, c)
        cp = pltpu.make_async_remote_copy(
            src_ref=ref, dst_ref=ref, send_sem=psend.at[0],
            recv_sem=precv.at[key(h, f, s, piece)], device_id=partner, device_id_type=MESH)
        cp.start()
        psends.append(cp)

    def wait_link(h, f, s, piece):
        ref = view(h, f, s, piece, c)
        pltpu.make_async_remote_copy(
            src_ref=ref, dst_ref=ref, send_sem=send_sem.at[0],
            recv_sem=recv_sem.at[key(h, f, s, piece)], device_id=partner, device_id_type=MESH).wait_recv()

    def wait_partner(h, f, s, piece):
        ref = view(h, f, s, piece, 1 - c)
        pltpu.make_async_remote_copy(
            src_ref=ref, dst_ref=ref, send_sem=send_sem.at[0],
            recv_sem=precv.at[key(h, f, s, piece)], device_id=partner, device_id_type=MESH).wait_recv()

    def pieces(f, s):
        return (0, 1) if (f == 2 and s == 0) or s == 2 else (None,)

    B = bank_hbm.shape[0]
    mine = pl.ds(pl.multiple_of(c * B, B), B)
    own = [pltpu.make_async_copy(w_hbm.at[:, pl.ds(h * C, C)], view(h, 0, 0, None, c), own_sem.at[h]) for h in (0, 1)]
    own.append(pltpu.make_async_copy(bank_hbm, bankbuf.at[mine, :], own_sem.at[2]))
    freq_copy = pltpu.make_async_copy(freq_hbm, table, own_sem.at[3])
    for cp in own:
        cp.start()

    barrier = pltpu.get_barrier_semaphore()
    peers = [chip(1, 0), chip(-1, 0), chip(0, 1), chip(0, -1), partner]
    if ny > 1:
        peers += [column(step) for step in range(1, ny)]
    for p in peers:
        pl.semaphore_signal(barrier, inc=1, device_id=p, device_id_type=MESH)

    groups = [[(0, 0)], [(-1, 0), (1, 0)], [(0, -1), (0, 1)], [(2, 0)],
              [(-1, -1), (-1, 1)], [(1, -1), (1, 1)], [(0, 2)], [(2, -1), (2, 1)], [(-1, 2), (1, 2)], [(2, 2)]]

    tok_wait = {}
    n = 0
    for g in groups:
        for f, s in g:
            for h in (0, 1):
                dx, dz = (f, s) if h == 0 else (s, f)
                if (dx, dz) in tok_wait:
                    continue
                b = block_of(0, dx, dz)
                cp = pltpu.make_async_copy(
                    tok_hbm.at[0, :, pl.ds(pl.multiple_of(b * 2 * R, 2 * R), 2 * R)], tok.at[b], tok_sem.at[n])
                cp.start()
                tok_wait[(dx, dz)] = cp
                n += 1

    for cp in own:
        cp.wait()
    pl.semaphore_wait(barrier, len(peers))

    for h in (0, 1):
        to_partner(h, 0, 0, None)
    for h in (0, 1):
        for step in (1, -1):
            send(h, 0, 0, None, True, step, (-step, 0))

    swaps = []

    def swap(ref):
        cp = pltpu.make_async_remote_copy(
            src_ref=ref.at[mine, :], dst_ref=ref.at[mine, :], send_sem=xsend.at[len(swaps)],
            recv_sem=xrecv.at[len(swaps)], device_id=partner, device_id_type=MESH)
        cp.start()
        swaps.append(cp)

    swap(bankbuf)
    freq_copy.start()

    bf = jnp.bfloat16
    f32 = jnp.float32
    i32 = jnp.int32

    def onehot(a, b):
        return jnp.where(a == b, 1.0, 0.0).astype(bf)

    peers_in_pool = packed.shape[0]
    cap = packed.shape[1]

    def pack():
        n = items_ref.shape[0]
        width = counts.shape[1]
        owner = owner_ref[...]
        mark = jnp.where(lax.broadcasted_iota(i32, (width, n), 0) == owner, 1.0, 0.0)
        lowrow = lax.broadcasted_iota(i32, (n, n), 0)
        lowcol = lax.broadcasted_iota(i32, (n, n), 1)
        upper = jnp.where(lowrow < lowcol, 1.0, 0.0).astype(bf)
        ahead = jnp.dot(mark.astype(bf), upper, preferred_element_type=f32)
        before = jnp.sum(mark * ahead, axis=0, keepdims=True)
        place = owner * cap + before.astype(i32)
        spread = onehot(lax.broadcasted_iota(i32, (peers_in_pool * cap, n), 0), place)
        rows = jnp.dot(spread, items_ref[...], preferred_element_type=f32)
        packed[...] = rows.astype(bf).reshape(packed.shape)
        tally = lax.dot_general(jnp.ones((8, n), bf), mark.astype(bf), (((1,), (1,)), ((), ())), preferred_element_type=f32)
        counts[...] = tally[0:1, :]

    L = ids_ref.shape[1]
    A = table.shape[0] // 8

    G = ids_ref.shape[0] // ny
    OR = B // ny
    here_rows = pl.ds(pl.multiple_of(c * B + y * OR, OR), OR)

    def off_start():
        for g in range(G):
            row = ids_ref[pl.ds(y * G + g, 1), :].astype(f32)
            idx = jnp.transpose(jnp.broadcast_to(row, (L, L))).astype(i32)
            where_at[pl.ds(g * L, L), :] = idx
            line = lax.rem(idx // L, A)
            wide = jnp.concatenate([line] * (A // L), axis=1) if A > L else line[:, :A]
            pick[pl.ds(g * L, L), :] = onehot(wide, lax.broadcasted_iota(i32, (L, A), 1))

    def off_step(j):
        if j == 0:
            freq_copy.wait()
        tile = min(256, OR)

        def rows_step(r, carry):
            rs = pl.ds(pl.multiple_of(r * tile, tile), tile)
            pair = jnp.concatenate([table[pl.ds(2 * j * A, A), :], table[pl.ds((2 * j + 1) * A, A), :]], axis=1)
            d = jnp.dot(pick[rs, :], pair, preferred_element_type=f32)
            part_of = where_at[rs, :] // (L * A)
            got = jnp.where(part_of == 2 * j, d[:, :L], jnp.where(part_of == 2 * j + 1, d[:, L:], 0.0))
            if j == 0:
                found[rs, :] = got
            else:
                found[rs, :] = found[rs, :] + got
            return carry

        lax.fori_loop(0, OR // tile, rows_step, 0)

    def off_end():
        lane_at = lax.broadcasted_iota(i32, (OR, L), 1)
        val = jnp.sum(jnp.where(lax.rem(where_at[...], L) == lane_at, found[...], 0.0), axis=1, keepdims=True)
        offb[here_rows, :] = jnp.broadcast_to(val * LOG2E, (OR, offb.shape[1]))
        for step in range(1, ny):
            pltpu.make_async_remote_copy(
                src_ref=offb.at[here_rows, :], dst_ref=offb.at[here_rows, :], send_sem=osend.at[0],
                recv_sem=orecv.at[0], device_id=column(step), device_id_type=MESH).start()

    def off_collect():
        if ny > 1:
            arrived(offb.at[pl.ds(0, (ny - 1) * OR), :], orecv.at[0])
        swap(offb)

    def take(g):
        for f, s in groups[g]:
            for h in (0, 1):
                for p in pieces(f, s):
                    wait_link(h, f, s, p)
                    to_partner(h, f, s, p)

    def onward_first():
        for f in (-1, 1):
            for h in (0, 1):
                send(h, f, 0, 0 if f == -1 else 1, True, -f, (2, 0))

    def across(f):
        for h in (0, 1):
            for step in (1, -1):
                send(h, f, 0, None, False, step, (f, -step))

    def onward_second(f):
        for s in (-1, 1):
            for h in (0, 1):
                send(h, f, s, 0 if s == -1 else 1, False, -s, (f, 2))

    def mm(g):
        items = groups[g]
        for f, s in items:
            for h in (0, 1):
                dx, dz = (f, s) if h == 0 else (s, f)
                if (dx, dz) in tok_wait:
                    tok_wait.pop((dx, dz)).wait()
                for p in pieces(f, s):
                    wait_partner(h, f, s, p)

        def step(i, carry):
            h = lax.rem(i, 2)
            j = i // 2
            f = sum(jnp.where(j == k, fs[0], 0) for k, fs in enumerate(items))
            s = sum(jnp.where(j == k, fs[1], 0) for k, fs in enumerate(items))
            b = block_of(h, f, s)
            row = pl.multiple_of(b * (2 * R), 2 * R)
            d = jnp.dot(tok[b], wbuf[h, pl.ds(row, 2 * R), :], preferred_element_type=jnp.float32)
            if g == 0:
                acc[h] = d
            else:
                acc[h] = acc[h] + d
            return carry

        lax.fori_loop(0, 2 * len(items), step, 0)

    pack()
    across(0)
    mm(0)
    off_start()
    take(1)
    onward_first()
    across(-1)
    for j in range(4):
        off_step(j)
    off_end()
    take(2)
    across(1)
    mm(1)
    take(3)
    mm(2)
    take(4)
    onward_second(0)
    across(2)
    mm(3)
    take(5)
    onward_second(-1)
    mm(4)
    off_collect()
    take(6)
    onward_second(1)
    mm(5)
    take(7)
    onward_second(2)
    mm(6)
    take(8)
    mm(7)
    take(9)
    mm(8)
    mm(9)

    far = [(i, k) for i in offs for k in (0, -1, 1, 2, -2) if (i, k) != (0, 0)]

    def spot(i, k):
        return offs.index(i) * 5 + (0, -1, 1, 2, -2).index(k)

    def mirror(i, k):
        return spot(i if i == 2 else -i, -k)

    zs = (0, -1, 1, 2)
    near = [(i, k, o) for i in offs for k in zs for o in (0, 1) if (i, k, o) != (0, 0, 0)]

    me = (x * 4 + zl) * 2 + c
    rows_in[me] = packed[me]
    counts_in[me] = counts[...]

    def post():
        tcopies = []
        for n, (i, k) in enumerate(far):
            cp = pltpu.make_async_remote_copy(
                src_ref=pos_ref, dst_ref=tbuf.at[mirror(i, k)], send_sem=tsend.at[0], recv_sem=trecv.at[0],
                device_id=chip(i, k), device_id_type=MESH)
            cp.start()
            tcopies.append(cp)
        ncopies = []
        for n, (i, k, o) in enumerate(near):
            to = chip(i, k)
            core = 1 - c if o else c
            to = to[:4] + (core,)
            owner_at = (to[2] * 4 + to[3]) * 2 + core
            for src, dst, ss, rr in ((packed.at[owner_at], rows_in.at[me], nsend, nrecv), (counts, counts_in.at[me], csend, crecv)):
                cp = pltpu.make_async_remote_copy(
                    src_ref=src, dst_ref=dst, send_sem=ss.at[0], recv_sem=rr.at[0], device_id=to, device_id_type=MESH)
                cp.start()
                ncopies.append(cp)

    T = M // 4
    H = part.shape[1] // 2
    left, right = pl.ds(0, H), pl.ds(H, H)

    def quarter(step):
        return pl.ds(pl.multiple_of(lax.rem(y + step + 4, 4) * T, T), T)

    def partial(step):
        rs = quarter(step)
        total = None
        for h in (0, 1):
            hid = jnp.maximum(acc[h, rs, :], 0.0).astype(jnp.bfloat16)
            d = jnp.dot(hid, wo_ref[pl.ds(h * C, C), :], preferred_element_type=jnp.float32)
            total = d if total is None else total + d
        part[rs, :] = total

    ycopies = []

    def ysend_to(slot, step):
        cp = pltpu.make_async_remote_copy(
            src_ref=ysend.at[slot], dst_ref=yrecv.at[slot], send_sem=ysem.at[0], recv_sem=yrsem.at[slot],
            device_id=column(step), device_id_type=MESH)
        cp.start()
        ycopies.append(cp)

    def ywait(slot):
        pltpu.make_async_remote_copy(
            src_ref=ysend.at[slot], dst_ref=yrecv.at[slot], send_sem=ysem.at[0], recv_sem=yrsem.at[slot],
            device_id=partner, device_id_type=MESH).wait_recv()

    if ny > 1:
        partial(2)
        ysend[0] = part[quarter(2), left].astype(bf)
        ysend_to(0, -1)
        ysend[1] = part[quarter(2), right].astype(bf)
        ysend_to(1, 1)
        partial(-1)
        ysend[2] = part[quarter(-1), right].astype(bf)
        ysend_to(2, -1)
        partial(1)
        ysend[3] = part[quarter(1), left].astype(bf)
        ysend_to(3, 1)
        post()
        ywait(0)
        ysend[4] = (yrecv[0].astype(f32) + part[quarter(-1), left]).astype(bf)
        ysend_to(4, -1)
        ywait(1)
        ysend[5] = (yrecv[1].astype(f32) + part[quarter(1), right]).astype(bf)
        ysend_to(5, 1)
        partial(0)
        ywait(2)
        ywait(3)
        ywait(4)
        ywait(5)
        own_q = quarter(0)
        qbuf[0, :, left] = ((part[own_q, left] + yrecv[3].astype(f32) + yrecv[4].astype(f32)) * SCALE).astype(bf)
        qbuf[0, :, right] = ((part[own_q, right] + yrecv[2].astype(f32) + yrecv[5].astype(f32)) * SCALE).astype(bf)
    else:
        post()
        partial(0)
        qbuf[0] = (part[pl.ds(0, T), :] * SCALE).astype(bf)

    P2 = T // 2
    P4 = T // 4

    def qview(h, f, s, piece):
        dx, dz = (f, s) if h == 0 else (s, f)
        rows = pl.ds(h * P2, P2) if piece is None else pl.ds(h * P2 + piece * P4, P4)
        return qbuf.at[offs.index(dx) * 4 + offs.index(dz), rows, :]

    qsends = []

    def qgo(h, f, s, piece, first, step, kind):
        cp = pltpu.make_async_remote_copy(
            src_ref=qview(h, f, s, piece), dst_ref=qview(h, kind[0], kind[1], piece), send_sem=qsend.at[0],
            recv_sem=qrecv.at[key(h, kind[0], kind[1], piece)],
            device_id=along(h, first, step), device_id_type=MESH)
        cp.start()
        qsends.append(cp)

    def qwait(h, f, s, piece):
        ref = qview(h, f, s, piece)
        pltpu.make_async_remote_copy(
            src_ref=ref, dst_ref=ref, send_sem=qsend.at[0],
            recv_sem=qrecv.at[key(h, f, s, piece)], device_id=partner, device_id_type=MESH).wait_recv()

    for first in (True, False):
        for h in (0, 1):
            for step in (1, -1):
                qgo(h, 0, 0, None, first, step, (-step, 0) if first else (0, -step))

    def qrelay(g):
        for f, s in groups[g]:
            for h in (0, 1):
                for p in pieces(f, s):
                    qwait(h, f, s, p)
                if s == 0 and f != 2:
                    qgo(h, f, 0, 0 if f == -1 else 1, True, -f, (2, 0))
                if s == 0:
                    for step in (1, -1):
                        qgo(h, f, 0, None, False, step, (f, -step))
                elif s != 2:
                    qgo(h, f, s, 0 if s == -1 else 1, False, -s, (f, 2))

    for cp in swaps:
        cp.wait_recv()
    tbuf[0] = pos_ref[...]
    arrived(tbuf.at[pl.ds(1, len(far))], trecv.at[0])

    base = (x * 4 + zl) * (2 * B)
    CH = min(1024, 2 * B)
    lane = lax.broadcasted_iota(jnp.int32, (1, T), 1)
    lower = lax.rem(lane, P2) < P4
    sub = lax.broadcasted_iota(jnp.int32, (8, T), 0)
    W = sbuf.shape[2]

    SUB = min(64, CH)
    G8 = SUB // 8
    levels = G8.bit_length() - 1

    def pick_of(values, i):
        return sum(jnp.where(i == k, v, 0) for k, v in enumerate(values))

    def place(items, i):
        if isinstance(i, int):
            return tuple(offs.index(v) for v in items[i])
        return tuple(pick_of([offs.index(item[d]) for item in items], i) for d in (0, 1))

    def turn(at, qt):
        qt[...] = jnp.transpose(qbuf[at[0] * 4 + at[1]])

    def multiply(rows, logits, qt):
        prod = jnp.dot(bankbuf[rows, :], qt[...], preferred_element_type=f32)
        off = offb[rows, :]
        if T > off.shape[1]:
            off = jnp.concatenate([off] * (T // off.shape[1]), axis=1)
        logits[rows, :] = prod - off

    def block(ahead, logits_ahead, qt, at, logits):
        if ahead is not None:
            turn(ahead, qt)
        if at is not None:
            ix, iz = at
            slot = ix * 4 + iz
            target = tbuf[ix * 5 + iz]
            behind = jnp.logical_and(lower, jnp.broadcast_to(iz, lower.shape) == 3)
            target = jnp.where(behind, tbuf[ix * 5 + 4], target)
            t = jnp.broadcast_to(target - base, (8, T))
            group = lax.shift_right_arithmetic(t, 3)
            which = lax.shift_right_arithmetic(group, levels)

        def chunk(k, carry):
            first = pl.multiple_of(k * CH, CH)
            if ahead is not None:
                multiply(pl.ds(first, CH), logits_ahead, qt)
            if at is None:
                return carry
            m, total, hit = carry
            bits = [jnp.bitwise_and(lax.shift_right_arithmetic(group, b), 1) == 1 for b in range(levels)]
            for u in range(CH // SUB):
                logit = logits[pl.ds(first + u * SUB, SUB), :].reshape(G8, 8, T)
                top = jnp.maximum(m, jnp.max(logit, axis=0))
                chosen = [logit[r] for r in range(G8)]
                for b in range(levels):
                    chosen = [jnp.where(bits[b], chosen[2 * r + 1], chosen[2 * r]) for r in range(len(chosen) // 2)]
                hit = jnp.where(which == k * (CH // SUB) + u, chosen[0], hit)
                total = total * jnp.exp2(m - top) + jnp.sum(jnp.exp2(logit - top[None]), axis=0)
                m = top
            return m, total, hit

        zero = jnp.zeros((8, T), f32)
        m, total, hit = lax.fori_loop(0, 2 * B // CH, chunk, (jnp.full((8, T), -jnp.inf, f32), zero, zero))
        if at is None:
            return
        top = jnp.max(m, axis=0, keepdims=True)
        total = jnp.sum(total * jnp.exp2(m - top), axis=0, keepdims=True)
        score = jnp.sum(jnp.where(jnp.bitwise_and(t, 7) == sub, hit, 0.0), axis=0, keepdims=True)
        for n, v in enumerate((top, total, score)):
            for k in range(2):
                sbuf[slot, pl.ds(n * 2 + k, 1), :] = v[:, k * W:(k + 1) * W]

    def give_back(items):
        for dx, dz in items:
            for k in ((dz,) if dz != 2 else (2, -2)):
                if (dx, k) == (0, 0):
                    continue
                cp = pltpu.make_async_remote_copy(
                    src_ref=sbuf.at[offs.index(dx) * 4 + offs.index(dz)], dst_ref=stats.at[mirror(dx, k)],
                    send_sem=ssend.at[0], recv_sem=srecv.at[0], device_id=chip(dx, k), device_id_type=MESH)
                cp.start()

    def blocks(items, last):
        todo = [last] + items[:-1]

        def pair(i, carry):
            block(place(items, 2 * i), logits1, qt1, place(todo, 2 * i), logits0)
            block(place(items, 2 * i + 1), logits0, qt0, place(todo, 2 * i + 1), logits1)
            return carry

        if len(items) == 2:
            pair(0, 0)
        else:
            lax.fori_loop(0, len(items) // 2, pair, 0)
        give_back(todo)

    block((0, 0), logits0, qt0, None, None)
    qrelay(1)
    qrelay(2)
    blocks([(-1, 0), (1, 0), (0, -1), (0, 1)], (0, 0))
    qrelay(3)
    qrelay(4)
    qrelay(5)
    blocks([(-1, -1), (-1, 1), (1, -1), (1, 1)], (0, 1))
    qrelay(6)
    qrelay(7)
    blocks([(2, 0), (0, 2)], (1, 1))
    qrelay(8)
    blocks([(2, -1), (2, 1), (-1, 2), (1, 2)], (0, 2))
    qrelay(9)
    block((3, 3), logits1, qt1, (2, 3), logits0)
    give_back([(1, 2)])
    block(None, None, None, (3, 3), logits1)
    give_back([(2, 2)])

    arrived(rows_in.at[pl.ds(0, len(near))], nrecv.at[0])
    arrived(counts_in.at[pl.ds(0, len(near))], crecv.at[0])
    J = peers_in_pool * cap
    width = counts.shape[1]
    every = counts_in[...].reshape(peers_in_pool, width)
    mine_only = jnp.where(lax.broadcasted_iota(i32, every.shape, 1) == me, every, 0.0)
    count = jnp.sum(mine_only, axis=1, keepdims=True)
    source = lax.broadcasted_iota(i32, (peers_in_pool, J), 0)
    column_of = lax.broadcasted_iota(i32, (peers_in_pool, J), 1) // cap
    valid = jnp.sum(jnp.where(source == column_of, count, 0.0), axis=0, keepdims=True)
    ahead = jnp.sum(jnp.where(source < column_of, count, 0.0), axis=0, keepdims=True)
    nth = lax.rem(lax.broadcasted_iota(i32, (1, J), 1), cap)
    slot_of = lax.rem(head_ref[0] + ahead.astype(i32) + nth, B)
    slot_of = jnp.where(nth < valid.astype(i32), slot_of, -1)
    tile = min(256, B)

    def write(r, carry):
        first = pl.multiple_of(r * tile, tile)
        spread = onehot(lax.broadcasted_iota(i32, (tile, J), 0) + first, slot_of)
        fresh = jnp.dot(spread, rows_in[...].reshape(J, rows_in.shape[2]), preferred_element_type=f32)
        hits = jnp.dot(spread, jnp.ones((J, rows_in.shape[2]), bf), preferred_element_type=f32)
        old = bankbuf[pl.ds(pl.multiple_of(c * B + first, tile), tile), :]
        newbank_ref[pl.ds(first, tile), :] = jnp.where(hits > 0.5, fresh, old.astype(f32)).astype(bf)
        return carry

    lax.fori_loop(0, B // tile, write, 0)

    stats[0] = sbuf[0]
    arrived(stats.at[pl.ds(1, len(far))], srecv.at[0])
    low = lax.broadcasted_iota(jnp.int32, (8, W), 1) < P4
    parts = []
    for i in offs:
        for k in (0, -1, 1):
            st = stats[spot(i, k)]
            parts.append((st[0:2], st[2:4], st[4:6]))
        st = jnp.where(low, stats[spot(i, 2)], stats[spot(i, -2)])
        parts.append((st[0:2], st[2:4], st[4:6]))
    top = functools.reduce(jnp.maximum, [p[0] for p in parts])
    total = sum(p[1] * jnp.exp2(p[0] - top) for p in parts)
    score = sum(p[2] for p in parts)
    loss = LN2 * (top - score) + jnp.log(total)
    for k in range(2):
        out_ref[:, k * W:(k + 1) * W] = loss[k:k + 1, :]

    sent(wbuf.at[0, pl.ds(0, 30 * R), :], send_sem.at[0])
    sent(wbuf.at[0], psend.at[0])
    sent(tbuf.at[pl.ds(1, len(far))], tsend.at[0])
    sent(rows_in.at[pl.ds(0, len(near))], nsend.at[0])
    sent(counts_in.at[pl.ds(0, len(near))], csend.at[0])
    sent(qbuf.at[pl.ds(0, 15)], qsend.at[0])
    sent(stats.at[pl.ds(1, len(far))], ssend.at[0])
    for cp in swaps:
        cp.wait_send()
    if ny > 1:
        sent(ysend, ysem.at[0])
        sent(offb.at[pl.ds(0, (ny - 1) * OR), :], osend.at[0])


def tower(tokens, w_hidden, w_out, bank, log_freq, item_ids, positives, new_items, new_owner, queue_head):
    M, K = tokens.shape[1:]
    R, N = w_hidden.shape
    E = w_out.shape[1]
    B = bank.shape[0]
    T = M // 4
    L = item_ids.shape[1]
    pool = K // R
    OR = B // lax.axis_size("tensor")
    cap = 2 * new_items.shape[0] // pool
    anywhere = pl.BlockSpec(memory_space=pl.ANY)
    vmem = pl.BlockSpec(memory_space=pltpu.VMEM)
    dma = pltpu.SemaphoreType.DMA
    return pl.pallas_call(
        tower_kernel,
        out_shape=(jax.ShapeDtypeStruct((1, T), jnp.float32), jax.ShapeDtypeStruct((B, E), jnp.bfloat16)),
        in_specs=[anywhere, anywhere, vmem, anywhere, anywhere, vmem, vmem, vmem, vmem,
                  pl.BlockSpec(memory_space=pltpu.SMEM)],
        out_specs=(vmem, vmem),
        scratch_shapes=[
            pltpu.VMEM((16, M, 2 * R), jnp.bfloat16),
            pltpu.VMEM((2, K, N // 2), jnp.bfloat16),
            pltpu.VMEM((2, M, N // 2), jnp.float32),
            pltpu.VMEM((M, E), jnp.float32),
            pltpu.VMEM((6, T, E // 2), jnp.bfloat16),
            pltpu.VMEM((6, T, E // 2), jnp.bfloat16),
            pltpu.VMEM((2 * B, E), jnp.bfloat16),
            pltpu.VMEM((2 * B, T // 2), jnp.float32),
            pltpu.VMEM((16, T, E), jnp.bfloat16),
            pltpu.VMEM((E, T), jnp.bfloat16),
            pltpu.VMEM((E, T), jnp.bfloat16),
            pltpu.VMEM((2 * B, T), jnp.float32),
            pltpu.VMEM((2 * B, T), jnp.float32),
            pltpu.VMEM((20, 1, T), jnp.int32),
            pltpu.VMEM((16, 8, T // 2), jnp.float32),
            pltpu.VMEM((20, 8, T // 2), jnp.float32),
            pltpu.VMEM(log_freq.shape, jnp.bfloat16),
            pltpu.VMEM((OR, log_freq.shape[0] // 8), jnp.bfloat16),
            pltpu.VMEM((OR, L), jnp.int32),
            pltpu.VMEM((OR, L), jnp.float32),
            pltpu.VMEM((pool, cap, E), jnp.bfloat16),
            pltpu.VMEM((1, 128), jnp.float32),
            pltpu.VMEM((pool, cap, E), jnp.bfloat16),
            pltpu.VMEM((pool, 1, 128), jnp.float32),
            dma((16,)), dma((4,)), dma((1,)), dma((64,)), dma((1,)), dma((64,)),
            dma((2,)), dma((2,)), dma((1,)), dma((6,)), dma((1,)), dma((64,)),
            dma((1,)), dma((1,)), dma((1,)), dma((1,)), dma((1,)), dma((1,)), dma((1,)), dma((1,)),
            dma((1,)), dma((1,)),
        ],
        compiler_params=pltpu.CompilerParams(collective_id=0, has_side_effects=True, vmem_limit_bytes=56 * 1024 * 1024),
        name="tower",
    )(tokens, w_hidden, w_out, bank, log_freq, item_ids, positives, new_items, new_owner, queue_head)


def body(
    tokens, w_hidden, w_out, bank, item_ids, log_freq, positives, new_items, new_owner, queue_head
):
    results = tower(
        tokens, w_hidden, w_out, bank, log_freq.reshape(-1, 128), item_ids.reshape(-1, 128),
        positives, new_items, new_owner.reshape(1, -1), queue_head,
    )
    return settle(results)


def settle_kernel(loss_in, bank_in, loss_out, bank_out):
    loss_out[...] = loss_in[...]
    bank_out[...] = bank_in[...]


def settle(results):
    vmem = pl.BlockSpec(memory_space=pltpu.VMEM)
    return pl.pallas_call(
        settle_kernel,
        out_shape=tuple(jax.ShapeDtypeStruct(r.shape, r.dtype) for r in results),
        in_specs=[vmem, vmem],
        out_specs=(vmem, vmem),
        name="settle",
    )(*results)


def solution(mesh):
    finer = Mesh(
        mesh.devices.reshape(mesh.shape["dp"], mesh.shape["tensor"], 4, 4, 2),
        ("dp", "tensor", "pool_0", "pool_1", "pool_2"),
    )
    in_specs = (
        P(DP_POOL, None, None),
        P(POOL, "tensor"),
        P("tensor", None),
        P(POOL, None),
        P(POOL),
        P(),
        P(DP_POOL, "tensor"),
        P(POOL, None),
        P(POOL, None),
        P(POOL),
    )
    out_specs = (P(DP_POOL, "tensor"), P(POOL, None))
    return jax.shard_map(body, mesh=finer, in_specs=in_specs, out_specs=out_specs, check_vma=False)
```

```python
import functools
import jax
import jax.numpy as jnp
from jax import lax
from jax.experimental import pallas as pl
from jax.experimental.pallas import tpu as pltpu

AXES = ("dp", "tensor", "pool_0", "pool_1", "pool_2")
from jax.sharding import Mesh
from jax.sharding import PartitionSpec as P

MESH = pl.DeviceIdType.MESH
POOL = ("pool_0", "pool_1", "pool_2")
DP_POOL = ("dp", "pool_0", "pool_1", "pool_2")


LOG2E = 1.4426950408889634
LN2 = 0.6931471805599453
SCALE = 5.0 * LOG2E


def tower_kernel(tok_hbm, w_hbm, wo_ref, bank_hbm, freq_hbm, ids_ref, pos_ref, items_ref,
                 owner_ref, head_ref, out_ref, newbank_ref, tok, wbuf, acc, part, ysend, yrecv,
                 bankbuf, offb, qbuf, qt0, qt1, logits0, logits1, tbuf, sbuf, stats, table, pick, where_at, found, packed, counts, rows_in, counts_in, tok_sem, own_sem, send_sem, recv_sem, psend, precv,
                 xsend, xrecv, ysem, yrsem, qsend, qrecv, tsend, trecv, ssend, srecv,
                 nsend, nrecv, csend, crecv, osend, orecv):
    dp, y, x, zl, c = (lax.axis_index(a) for a in AXES)
    ny = lax.axis_size("tensor")
    pz = dp * 4 + zl
    R = w_hbm.shape[0]
    C = w_hbm.shape[1] // 2
    Q = C // 2
    M = tok.shape[1]
    offs = (0, -1, 1, 2)

    def chip(dx, dz):
        xx = lax.rem(x + dx + 4, 4)
        zz = lax.rem(pz + dz + 8, 8)
        return (zz // 4, y, xx, lax.rem(zz, 4), c)

    def along(h, first, step):
        return chip(step, 0) if (h == 0) == first else chip(0, step)

    partner = (dp, y, x, zl, 1 - c)

    def arrived(ref, sem):
        pltpu.make_async_remote_copy(
            src_ref=ref, dst_ref=ref, send_sem=send_sem.at[0], recv_sem=sem,
            device_id=partner, device_id_type=MESH).wait_recv()

    def sent(ref, sem):
        pltpu.make_async_remote_copy(
            src_ref=ref, dst_ref=ref, send_sem=sem, recv_sem=recv_sem.at[0],
            device_id=partner, device_id_type=MESH).wait_send()

    def column(step):
        return (dp, lax.rem(y + step + ny, ny), x, zl, c)

    def block_of(h, f, s):
        dx = f * (1 - h) + s * h
        dz = s * (1 - h) + f * h
        return lax.rem(x + dx + 4, 4) * 4 + lax.rem(zl + dz + 4, 4)

    def view(h, f, s, piece, core):
        row = pl.multiple_of(block_of(h, f, s) * (2 * R) + core * R, R)
        cols = slice(None) if piece is None else pl.ds(piece * Q, Q)
        return wbuf.at[h, pl.ds(row, R), cols]

    def key(h, f, s, piece):
        return ((h * 4 + offs.index(f)) * 4 + offs.index(s)) * 2 + (piece or 0)

    sends = []

    def send(h, f, s, piece, first, step, kind):
        nf, ns = kind
        ref = view(h, f, s, piece, c)
        cp = pltpu.make_async_remote_copy(
            src_ref=ref, dst_ref=ref, send_sem=send_sem.at[0],
            recv_sem=recv_sem.at[key(h, nf, ns, piece)],
            device_id=along(h, first, step), device_id_type=MESH)
        cp.start()
        sends.append(cp)

    psends = []

    def to_partner(h, f, s, piece):
        ref = view(h, f, s, piece, c)
        cp = pltpu.make_async_remote_copy(
            src_ref=ref, dst_ref=ref, send_sem=psend.at[0],
            recv_sem=precv.at[key(h, f, s, piece)], device_id=partner, device_id_type=MESH)
        cp.start()
        psends.append(cp)

    def wait_link(h, f, s, piece):
        ref = view(h, f, s, piece, c)
        pltpu.make_async_remote_copy(
            src_ref=ref, dst_ref=ref, send_sem=send_sem.at[0],
            recv_sem=recv_sem.at[key(h, f, s, piece)], device_id=partner, device_id_type=MESH).wait_recv()

    def wait_partner(h, f, s, piece):
        ref = view(h, f, s, piece, 1 - c)
        pltpu.make_async_remote_copy(
            src_ref=ref, dst_ref=ref, send_sem=send_sem.at[0],
            recv_sem=precv.at[key(h, f, s, piece)], device_id=partner, device_id_type=MESH).wait_recv()

    def pieces(f, s):
        return (0, 1) if (f == 2 and s == 0) or s == 2 else (None,)

    B = bank_hbm.shape[0]
    mine = pl.ds(pl.multiple_of(c * B, B), B)
    own = [pltpu.make_async_copy(w_hbm.at[:, pl.ds(h * C, C)], view(h, 0, 0, None, c), own_sem.at[h]) for h in (0, 1)]
    own.append(pltpu.make_async_copy(bank_hbm, bankbuf.at[mine, :], own_sem.at[2]))
    freq_copy = pltpu.make_async_copy(freq_hbm, table, own_sem.at[3])
    for cp in own:
        cp.start()

    barrier = pltpu.get_barrier_semaphore()
    peers = [chip(1, 0), chip(-1, 0), chip(0, 1), chip(0, -1), partner]
    if ny > 1:
        peers += [column(step) for step in range(1, ny)]
    for p in peers:
        pl.semaphore_signal(barrier, inc=1, device_id=p, device_id_type=MESH)

    groups = [[(0, 0)], [(-1, 0), (1, 0)], [(0, -1), (0, 1)], [(2, 0)],
              [(-1, -1), (-1, 1)], [(1, -1), (1, 1)], [(0, 2)], [(2, -1), (2, 1)], [(-1, 2)], [(1, 2)], [(2, 2)]]

    tok_wait = {}
    n = 0
    for g in groups:
        for f, s in g:
            for h in (0, 1):
                dx, dz = (f, s) if h == 0 else (s, f)
                if (dx, dz) in tok_wait:
                    continue
                b = block_of(0, dx, dz)
                cp = pltpu.make_async_copy(
                    tok_hbm.at[0, :, pl.ds(pl.multiple_of(b * 2 * R, 2 * R), 2 * R)], tok.at[b], tok_sem.at[n])
                cp.start()
                tok_wait[(dx, dz)] = cp
                n += 1

    for cp in own:
        cp.wait()
    pl.semaphore_wait(barrier, len(peers))

    for h in (0, 1):
        to_partner(h, 0, 0, None)
    for h in (0, 1):
        for step in (1, -1):
            send(h, 0, 0, None, True, step, (-step, 0))

    swaps = []

    def swap(ref):
        cp = pltpu.make_async_remote_copy(
            src_ref=ref.at[mine, :], dst_ref=ref.at[mine, :], send_sem=xsend.at[len(swaps)],
            recv_sem=xrecv.at[len(swaps)], device_id=partner, device_id_type=MESH)
        cp.start()
        swaps.append(cp)

    swap(bankbuf)
    freq_copy.start()

    bf = jnp.bfloat16
    f32 = jnp.float32
    i32 = jnp.int32

    def onehot(a, b):
        return jnp.where(a == b, 1.0, 0.0).astype(bf)

    peers_in_pool = packed.shape[0]
    cap = packed.shape[1]

    def pack():
        n = items_ref.shape[0]
        width = counts.shape[1]
        owner = owner_ref[...]
        mark = jnp.where(lax.broadcasted_iota(i32, (width, n), 0) == owner, 1.0, 0.0)
        lowrow = lax.broadcasted_iota(i32, (n, n), 0)
        lowcol = lax.broadcasted_iota(i32, (n, n), 1)
        upper = jnp.where(lowrow < lowcol, 1.0, 0.0).astype(bf)
        ahead = jnp.dot(mark.astype(bf), upper, preferred_element_type=f32)
        before = jnp.sum(mark * ahead, axis=0, keepdims=True)
        place = owner * cap + before.astype(i32)
        spread = onehot(lax.broadcasted_iota(i32, (peers_in_pool * cap, n), 0), place)
        rows = jnp.dot(spread, items_ref[...], preferred_element_type=f32)
        packed[...] = rows.astype(bf).reshape(packed.shape)
        tally = lax.dot_general(jnp.ones((8, n), bf), mark.astype(bf), (((1,), (1,)), ((), ())), preferred_element_type=f32)
        counts[...] = tally[0:1, :]

    L = ids_ref.shape[1]
    A = table.shape[0] // 8

    G = ids_ref.shape[0] // ny
    OR = B // ny
    here_rows = pl.ds(pl.multiple_of(c * B + y * OR, OR), OR)

    def off_start():
        for g in range(G):
            row = ids_ref[pl.ds(y * G + g, 1), :].astype(f32)
            idx = jnp.transpose(jnp.broadcast_to(row, (L, L))).astype(i32)
            where_at[pl.ds(g * L, L), :] = idx
            line = lax.rem(idx // L, A)
            wide = jnp.concatenate([line] * (A // L), axis=1) if A > L else line[:, :A]
            pick[pl.ds(g * L, L), :] = onehot(wide, lax.broadcasted_iota(i32, (L, A), 1))

    def off_step(j):
        if j == 0:
            freq_copy.wait()
        tile = min(256, OR)

        def rows_step(r, carry):
            rs = pl.ds(pl.multiple_of(r * tile, tile), tile)
            pair = jnp.concatenate([table[pl.ds(2 * j * A, A), :], table[pl.ds((2 * j + 1) * A, A), :]], axis=1)
            d = jnp.dot(pick[rs, :], pair, preferred_element_type=f32)
            part_of = where_at[rs, :] // (L * A)
            got = jnp.where(part_of == 2 * j, d[:, :L], jnp.where(part_of == 2 * j + 1, d[:, L:], 0.0))
            if j == 0:
                found[rs, :] = got
            else:
                found[rs, :] = found[rs, :] + got
            return carry

        lax.fori_loop(0, OR // tile, rows_step, 0)

    def off_end():
        lane_at = lax.broadcasted_iota(i32, (OR, L), 1)
        val = jnp.sum(jnp.where(lax.rem(where_at[...], L) == lane_at, found[...], 0.0), axis=1, keepdims=True)
        offb[here_rows, :] = jnp.broadcast_to(val * LOG2E, (OR, offb.shape[1]))
        for step in range(1, ny):
            pltpu.make_async_remote_copy(
                src_ref=offb.at[here_rows, :], dst_ref=offb.at[here_rows, :], send_sem=osend.at[0],
                recv_sem=orecv.at[0], device_id=column(step), device_id_type=MESH).start()

    def off_collect():
        if ny > 1:
            arrived(offb.at[pl.ds(0, (ny - 1) * OR), :], orecv.at[0])
        swap(offb)

    def take(g):
        for f, s in groups[g]:
            for h in (0, 1):
                for p in pieces(f, s):
                    wait_link(h, f, s, p)
                    to_partner(h, f, s, p)

    def onward_first():
        for f in (-1, 1):
            for h in (0, 1):
                send(h, f, 0, 0 if f == -1 else 1, True, -f, (2, 0))

    def across(f):
        for h in (0, 1):
            for step in (1, -1):
                send(h, f, 0, None, False, step, (f, -step))

    def onward_second(f):
        for s in (-1, 1):
            for h in (0, 1):
                send(h, f, s, 0 if s == -1 else 1, False, -s, (f, 2))

    def ready(g):
        for f, s in groups[g]:
            for h in (0, 1):
                dx, dz = (f, s) if h == 0 else (s, f)
                if (dx, dz) in tok_wait:
                    tok_wait.pop((dx, dz)).wait()
                for p in pieces(f, s):
                    wait_partner(h, f, s, p)

    def mm(g):
        items = groups[g]
        ready(g)

        def step(i, carry):
            h = lax.rem(i, 2)
            j = i // 2
            f = sum(jnp.where(j == k, fs[0], 0) for k, fs in enumerate(items))
            s = sum(jnp.where(j == k, fs[1], 0) for k, fs in enumerate(items))
            b = block_of(h, f, s)
            row = pl.multiple_of(b * (2 * R), 2 * R)
            d = jnp.dot(tok[b], wbuf[h, pl.ds(row, 2 * R), :], preferred_element_type=jnp.float32)
            if g == 0:
                acc[h] = d
            else:
                acc[h] = acc[h] + d
            return carry

        lax.fori_loop(0, 2 * len(items), step, 0)

    pack()
    across(0)
    mm(0)
    off_start()
    take(1)
    onward_first()
    across(-1)
    for j in range(4):
        off_step(j)
    off_end()
    take(2)
    across(1)
    mm(1)
    take(3)
    mm(2)
    take(4)
    onward_second(0)
    across(2)
    mm(3)
    take(5)
    onward_second(-1)
    mm(4)
    off_collect()
    take(6)
    onward_second(1)
    mm(5)
    take(7)
    onward_second(2)
    mm(6)
    take(8)
    mm(7)
    take(9)
    mm(8)
    take(10)
    mm(9)
    ready(10)

    far = [(i, k) for i in offs for k in (0, -1, 1, 2, -2) if (i, k) != (0, 0)]

    def spot(i, k):
        return offs.index(i) * 5 + (0, -1, 1, 2, -2).index(k)

    def mirror(i, k):
        return spot(i if i == 2 else -i, -k)

    zs = (0, -1, 1, 2)
    near = [(i, k, o) for i in offs for k in zs for o in (0, 1) if (i, k, o) != (0, 0, 0)]

    me = (x * 4 + zl) * 2 + c
    rows_in[me] = packed[me]
    counts_in[me] = counts[...]

    def post():
        tcopies = []
        for n, (i, k) in enumerate(far):
            cp = pltpu.make_async_remote_copy(
                src_ref=pos_ref, dst_ref=tbuf.at[mirror(i, k)], send_sem=tsend.at[0], recv_sem=trecv.at[0],
                device_id=chip(i, k), device_id_type=MESH)
            cp.start()
            tcopies.append(cp)
        ncopies = []
        for n, (i, k, o) in enumerate(near):
            to = chip(i, k)
            core = 1 - c if o else c
            to = to[:4] + (core,)
            owner_at = (to[2] * 4 + to[3]) * 2 + core
            for src, dst, ss, rr in ((packed.at[owner_at], rows_in.at[me], nsend, nrecv), (counts, counts_in.at[me], csend, crecv)):
                cp = pltpu.make_async_remote_copy(
                    src_ref=src, dst_ref=dst, send_sem=ss.at[0], recv_sem=rr.at[0], device_id=to, device_id_type=MESH)
                cp.start()
                ncopies.append(cp)

    T = M // 4
    H = part.shape[1] // 2
    left, right = pl.ds(0, H), pl.ds(H, H)

    def quarter(step):
        return pl.ds(pl.multiple_of(lax.rem(y + step + 4, 4) * T, T), T)

    far_block = block_of(0, 2, 2)
    far_rows = pl.ds(pl.multiple_of(far_block * (2 * R), 2 * R), 2 * R)

    def partial(step):
        rs = quarter(step)
        total = None
        for h in (0, 1):
            end = jnp.dot(tok[far_block, rs, :], wbuf[h, far_rows, :], preferred_element_type=jnp.float32)
            hid = jnp.maximum(acc[h, rs, :] + end, 0.0).astype(jnp.bfloat16)
            d = jnp.dot(hid, wo_ref[pl.ds(h * C, C), :], preferred_element_type=jnp.float32)
            total = d if total is None else total + d
        part[rs, :] = total

    ycopies = []

    def ysend_to(slot, step):
        cp = pltpu.make_async_remote_copy(
            src_ref=ysend.at[slot], dst_ref=yrecv.at[slot], send_sem=ysem.at[0], recv_sem=yrsem.at[slot],
            device_id=column(step), device_id_type=MESH)
        cp.start()
        ycopies.append(cp)

    def ywait(slot):
        pltpu.make_async_remote_copy(
            src_ref=ysend.at[slot], dst_ref=yrecv.at[slot], send_sem=ysem.at[0], recv_sem=yrsem.at[slot],
            device_id=partner, device_id_type=MESH).wait_recv()

    if ny > 1:
        partial(2)
        ysend[0] = part[quarter(2), left].astype(bf)
        ysend_to(0, -1)
        ysend[1] = part[quarter(2), right].astype(bf)
        ysend_to(1, 1)
        partial(-1)
        ysend[2] = part[quarter(-1), right].astype(bf)
        ysend_to(2, -1)
        partial(1)
        ysend[3] = part[quarter(1), left].astype(bf)
        ysend_to(3, 1)
        post()
        ywait(0)
        ysend[4] = (yrecv[0].astype(f32) + part[quarter(-1), left]).astype(bf)
        ysend_to(4, -1)
        ywait(1)
        ysend[5] = (yrecv[1].astype(f32) + part[quarter(1), right]).astype(bf)
        ysend_to(5, 1)
        partial(0)
        ywait(2)
        ywait(3)
        ywait(4)
        ywait(5)
        own_q = quarter(0)
        qbuf[0, :, left] = ((part[own_q, left] + yrecv[3].astype(f32) + yrecv[4].astype(f32)) * SCALE).astype(bf)
        qbuf[0, :, right] = ((part[own_q, right] + yrecv[2].astype(f32) + yrecv[5].astype(f32)) * SCALE).astype(bf)
    else:
        post()
        partial(0)
        qbuf[0] = (part[pl.ds(0, T), :] * SCALE).astype(bf)

    P2 = T // 2
    P4 = T // 4

    def qview(h, f, s, piece):
        dx, dz = (f, s) if h == 0 else (s, f)
        rows = pl.ds(h * P2, P2) if piece is None else pl.ds(h * P2 + piece * P4, P4)
        return qbuf.at[offs.index(dx) * 4 + offs.index(dz), rows, :]

    qsends = []

    def qgo(h, f, s, piece, first, step, kind):
        cp = pltpu.make_async_remote_copy(
            src_ref=qview(h, f, s, piece), dst_ref=qview(h, kind[0], kind[1], piece), send_sem=qsend.at[0],
            recv_sem=qrecv.at[key(h, kind[0], kind[1], piece)],
            device_id=along(h, first, step), device_id_type=MESH)
        cp.start()
        qsends.append(cp)

    def qwait(h, f, s, piece):
        ref = qview(h, f, s, piece)
        pltpu.make_async_remote_copy(
            src_ref=ref, dst_ref=ref, send_sem=qsend.at[0],
            recv_sem=qrecv.at[key(h, f, s, piece)], device_id=partner, device_id_type=MESH).wait_recv()

    for first in (True, False):
        for h in (0, 1):
            for step in (1, -1):
                qgo(h, 0, 0, None, first, step, (-step, 0) if first else (0, -step))

    def qrelay(g):
        for f, s in groups[g]:
            for h in (0, 1):
                for p in pieces(f, s):
                    qwait(h, f, s, p)
                if s == 0 and f != 2:
                    qgo(h, f, 0, 0 if f == -1 else 1, True, -f, (2, 0))
                if s == 0:
                    for step in (1, -1):
                        qgo(h, f, 0, None, False, step, (f, -step))
                elif s != 2:
                    qgo(h, f, s, 0 if s == -1 else 1, False, -s, (f, 2))

    for cp in swaps:
        cp.wait_recv()
    tbuf[0] = pos_ref[...]
    arrived(tbuf.at[pl.ds(1, len(far))], trecv.at[0])

    base = (x * 4 + zl) * (2 * B)
    CH = min(1024, 2 * B)
    lane = lax.broadcasted_iota(jnp.int32, (1, T), 1)
    lower = lax.rem(lane, P2) < P4
    sub = lax.broadcasted_iota(jnp.int32, (8, T), 0)
    W = sbuf.shape[2]

    SUB = min(64, CH)
    G8 = SUB // 8
    levels = G8.bit_length() - 1

    def pick_of(values, i):
        return sum(jnp.where(i == k, v, 0) for k, v in enumerate(values))

    def place(items, i):
        if isinstance(i, int):
            return tuple(offs.index(v) for v in items[i])
        return tuple(pick_of([offs.index(item[d]) for item in items], i) for d in (0, 1))

    def turn(at, qt):
        qt[...] = jnp.transpose(qbuf[at[0] * 4 + at[1]])

    def multiply(rows, logits, qt):
        prod = jnp.dot(bankbuf[rows, :], qt[...], preferred_element_type=f32)
        off = offb[rows, :]
        if T > off.shape[1]:
            off = jnp.concatenate([off] * (T // off.shape[1]), axis=1)
        logits[rows, :] = prod - off

    def block(ahead, logits_ahead, qt, at, logits):
        if ahead is not None:
            turn(ahead, qt)
        if at is not None:
            ix, iz = at
            slot = ix * 4 + iz
            target = tbuf[ix * 5 + iz]
            behind = jnp.logical_and(lower, jnp.broadcast_to(iz, lower.shape) == 3)
            target = jnp.where(behind, tbuf[ix * 5 + 4], target)
            t = jnp.broadcast_to(target - base, (8, T))
            group = lax.shift_right_arithmetic(t, 3)
            which = lax.shift_right_arithmetic(group, levels)

        def chunk(k, carry):
            first = pl.multiple_of(k * CH, CH)
            if ahead is not None:
                multiply(pl.ds(first, CH), logits_ahead, qt)
            if at is None:
                return carry
            m, total, hit = carry
            bits = [jnp.bitwise_and(lax.shift_right_arithmetic(group, b), 1) == 1 for b in range(levels)]
            for u in range(CH // SUB):
                logit = logits[pl.ds(first + u * SUB, SUB), :].reshape(G8, 8, T)
                top = jnp.maximum(m, jnp.max(logit, axis=0))
                chosen = [logit[r] for r in range(G8)]
                for b in range(levels):
                    chosen = [jnp.where(bits[b], chosen[2 * r + 1], chosen[2 * r]) for r in range(len(chosen) // 2)]
                hit = jnp.where(which == k * (CH // SUB) + u, chosen[0], hit)
                total = total * jnp.exp2(m - top) + jnp.sum(jnp.exp2(logit - top[None]), axis=0)
                m = top
            return m, total, hit

        zero = jnp.zeros((8, T), f32)
        m, total, hit = lax.fori_loop(0, 2 * B // CH, chunk, (jnp.full((8, T), -jnp.inf, f32), zero, zero))
        if at is None:
            return
        top = jnp.max(m, axis=0, keepdims=True)
        total = jnp.sum(total * jnp.exp2(m - top), axis=0, keepdims=True)
        score = jnp.sum(jnp.where(jnp.bitwise_and(t, 7) == sub, hit, 0.0), axis=0, keepdims=True)
        for n, v in enumerate((top, total, score)):
            for k in range(2):
                sbuf[slot, pl.ds(n * 2 + k, 1), :] = v[:, k * W:(k + 1) * W]

    def give_back(items):
        for dx, dz in items:
            for k in ((dz,) if dz != 2 else (2, -2)):
                if (dx, k) == (0, 0):
                    continue
                cp = pltpu.make_async_remote_copy(
                    src_ref=sbuf.at[offs.index(dx) * 4 + offs.index(dz)], dst_ref=stats.at[mirror(dx, k)],
                    send_sem=ssend.at[0], recv_sem=srecv.at[0], device_id=chip(dx, k), device_id_type=MESH)
                cp.start()

    def blocks(items, last):
        todo = [last] + items[:-1]

        def pair(i, carry):
            block(place(items, 2 * i), logits1, qt1, place(todo, 2 * i), logits0)
            block(place(items, 2 * i + 1), logits0, qt0, place(todo, 2 * i + 1), logits1)
            return carry

        if len(items) == 2:
            pair(0, 0)
        else:
            lax.fori_loop(0, len(items) // 2, pair, 0)
        give_back(todo)

    block((0, 0), logits0, qt0, None, None)
    qrelay(1)
    qrelay(2)
    blocks([(-1, 0), (1, 0), (0, -1), (0, 1)], (0, 0))
    qrelay(3)
    qrelay(4)
    qrelay(5)
    blocks([(-1, -1), (-1, 1), (1, -1), (1, 1)], (0, 1))
    qrelay(6)
    qrelay(7)
    blocks([(2, 0), (0, 2)], (1, 1))
    qrelay(8)
    qrelay(9)
    blocks([(2, -1), (2, 1), (-1, 2), (1, 2)], (0, 2))
    qrelay(10)
    block((3, 3), logits1, qt1, (2, 3), logits0)
    give_back([(1, 2)])
    block(None, None, None, (3, 3), logits1)
    give_back([(2, 2)])

    arrived(rows_in.at[pl.ds(0, len(near))], nrecv.at[0])
    arrived(counts_in.at[pl.ds(0, len(near))], crecv.at[0])
    J = peers_in_pool * cap
    width = counts.shape[1]
    every = counts_in[...].reshape(peers_in_pool, width)
    mine_only = jnp.where(lax.broadcasted_iota(i32, every.shape, 1) == me, every, 0.0)
    count = jnp.sum(mine_only, axis=1, keepdims=True)
    source = lax.broadcasted_iota(i32, (peers_in_pool, J), 0)
    column_of = lax.broadcasted_iota(i32, (peers_in_pool, J), 1) // cap
    valid = jnp.sum(jnp.where(source == column_of, count, 0.0), axis=0, keepdims=True)
    ahead = jnp.sum(jnp.where(source < column_of, count, 0.0), axis=0, keepdims=True)
    nth = lax.rem(lax.broadcasted_iota(i32, (1, J), 1), cap)
    slot_of = lax.rem(head_ref[0] + ahead.astype(i32) + nth, B)
    slot_of = jnp.where(nth < valid.astype(i32), slot_of, -1)
    tile = min(256, B)

    def write(r, carry):
        first = pl.multiple_of(r * tile, tile)
        spread = onehot(lax.broadcasted_iota(i32, (tile, J), 0) + first, slot_of)
        fresh = jnp.dot(spread, rows_in[...].reshape(J, rows_in.shape[2]), preferred_element_type=f32)
        hits = jnp.dot(spread, jnp.ones((J, rows_in.shape[2]), bf), preferred_element_type=f32)
        old = bankbuf[pl.ds(pl.multiple_of(c * B + first, tile), tile), :]
        newbank_ref[pl.ds(first, tile), :] = jnp.where(hits > 0.5, fresh, old.astype(f32)).astype(bf)
        return carry

    lax.fori_loop(0, B // tile, write, 0)

    stats[0] = sbuf[0]
    arrived(stats.at[pl.ds(1, len(far))], srecv.at[0])
    low = lax.broadcasted_iota(jnp.int32, (8, W), 1) < P4
    parts = []
    for i in offs:
        for k in (0, -1, 1):
            st = stats[spot(i, k)]
            parts.append((st[0:2], st[2:4], st[4:6]))
        st = jnp.where(low, stats[spot(i, 2)], stats[spot(i, -2)])
        parts.append((st[0:2], st[2:4], st[4:6]))
    top = functools.reduce(jnp.maximum, [p[0] for p in parts])
    total = sum(p[1] * jnp.exp2(p[0] - top) for p in parts)
    score = sum(p[2] for p in parts)
    loss = LN2 * (top - score) + jnp.log(total)
    for k in range(2):
        out_ref[:, k * W:(k + 1) * W] = loss[k:k + 1, :]

    sent(wbuf.at[0, pl.ds(0, 30 * R), :], send_sem.at[0])
    sent(wbuf.at[0], psend.at[0])
    sent(tbuf.at[pl.ds(1, len(far))], tsend.at[0])
    sent(rows_in.at[pl.ds(0, len(near))], nsend.at[0])
    sent(counts_in.at[pl.ds(0, len(near))], csend.at[0])
    sent(qbuf.at[pl.ds(0, 15)], qsend.at[0])
    sent(stats.at[pl.ds(1, len(far))], ssend.at[0])
    for cp in swaps:
        cp.wait_send()
    if ny > 1:
        sent(ysend, ysem.at[0])
        sent(offb.at[pl.ds(0, (ny - 1) * OR), :], osend.at[0])


def tower(tokens, w_hidden, w_out, bank, log_freq, item_ids, positives, new_items, new_owner, queue_head):
    M, K = tokens.shape[1:]
    R, N = w_hidden.shape
    E = w_out.shape[1]
    B = bank.shape[0]
    T = M // 4
    L = item_ids.shape[1]
    pool = K // R
    OR = B // lax.axis_size("tensor")
    cap = 2 * new_items.shape[0] // pool
    anywhere = pl.BlockSpec(memory_space=pl.ANY)
    vmem = pl.BlockSpec(memory_space=pltpu.VMEM)
    dma = pltpu.SemaphoreType.DMA
    return pl.pallas_call(
        tower_kernel,
        out_shape=(jax.ShapeDtypeStruct((1, T), jnp.float32), jax.ShapeDtypeStruct((B, E), jnp.bfloat16)),
        in_specs=[anywhere, anywhere, vmem, anywhere, anywhere, vmem, vmem, vmem, vmem,
                  pl.BlockSpec(memory_space=pltpu.SMEM)],
        out_specs=(vmem, vmem),
        scratch_shapes=[
            pltpu.VMEM((16, M, 2 * R), jnp.bfloat16),
            pltpu.VMEM((2, K, N // 2), jnp.bfloat16),
            pltpu.VMEM((2, M, N // 2), jnp.float32),
            pltpu.VMEM((M, E), jnp.float32),
            pltpu.VMEM((6, T, E // 2), jnp.bfloat16),
            pltpu.VMEM((6, T, E // 2), jnp.bfloat16),
            pltpu.VMEM((2 * B, E), jnp.bfloat16),
            pltpu.VMEM((2 * B, T // 2), jnp.float32),
            pltpu.VMEM((16, T, E), jnp.bfloat16),
            pltpu.VMEM((E, T), jnp.bfloat16),
            pltpu.VMEM((E, T), jnp.bfloat16),
            pltpu.VMEM((2 * B, T), jnp.float32),
            pltpu.VMEM((2 * B, T), jnp.float32),
            pltpu.VMEM((20, 1, T), jnp.int32),
            pltpu.VMEM((16, 8, T // 2), jnp.float32),
            pltpu.VMEM((20, 8, T // 2), jnp.float32),
            pltpu.VMEM(log_freq.shape, jnp.bfloat16),
            pltpu.VMEM((OR, log_freq.shape[0] // 8), jnp.bfloat16),
            pltpu.VMEM((OR, L), jnp.int32),
            pltpu.VMEM((OR, L), jnp.float32),
            pltpu.VMEM((pool, cap, E), jnp.bfloat16),
            pltpu.VMEM((1, 128), jnp.float32),
            pltpu.VMEM((pool, cap, E), jnp.bfloat16),
            pltpu.VMEM((pool, 1, 128), jnp.float32),
            dma((16,)), dma((4,)), dma((1,)), dma((64,)), dma((1,)), dma((64,)),
            dma((2,)), dma((2,)), dma((1,)), dma((6,)), dma((1,)), dma((64,)),
            dma((1,)), dma((1,)), dma((1,)), dma((1,)), dma((1,)), dma((1,)), dma((1,)), dma((1,)),
            dma((1,)), dma((1,)),
        ],
        compiler_params=pltpu.CompilerParams(collective_id=0, has_side_effects=True, vmem_limit_bytes=56 * 1024 * 1024),
        name="tower",
    )(tokens, w_hidden, w_out, bank, log_freq, item_ids, positives, new_items, new_owner, queue_head)


def body(
    tokens, w_hidden, w_out, bank, item_ids, log_freq, positives, new_items, new_owner, queue_head
):
    results = tower(
        tokens, w_hidden, w_out, bank, log_freq.reshape(-1, 128), item_ids.reshape(-1, 128),
        positives, new_items, new_owner.reshape(1, -1), queue_head,
    )
    return settle(results)


def settle_kernel(loss_in, bank_in, loss_out, bank_out):
    loss_out[...] = loss_in[...]
    bank_out[...] = bank_in[...]


def settle(results):
    vmem = pl.BlockSpec(memory_space=pltpu.VMEM)
    return pl.pallas_call(
        settle_kernel,
        out_shape=tuple(jax.ShapeDtypeStruct(r.shape, r.dtype) for r in results),
        in_specs=[vmem, vmem],
        out_specs=(vmem, vmem),
        name="settle",
    )(*results)


def solution(mesh):
    finer = Mesh(
        mesh.devices.reshape(mesh.shape["dp"], mesh.shape["tensor"], 4, 4, 2),
        ("dp", "tensor", "pool_0", "pool_1", "pool_2"),
    )
    in_specs = (
        P(DP_POOL, None, None),
        P(POOL, "tensor"),
        P("tensor", None),
        P(POOL, None),
        P(POOL),
        P(),
        P(DP_POOL, "tensor"),
        P(POOL, None),
        P(POOL, None),
        P(POOL),
    )
    out_specs = (P(DP_POOL, "tensor"), P(POOL, None))
    return jax.shard_map(body, mesh=finer, in_specs=in_specs, out_specs=out_specs, check_vma=False)
```
